512 devices in a mesh: blk: 128 (over z, y, core), rhs: 4 (over x).
Axes of the slice: x: 4, y: 8, z: 8, core: 2. Of those that a mesh axis runs over, the one named last changes fastest.
Arguments:
- thermal_solution: float32 [16, 1024, 1024], P('rhs', 'blk'), may hold values from -6 to 6
- heat_forcing: float32 [16, 1024, 1024], P('rhs', 'blk'), may hold values from -6 to 6
- extinction_factor: float32 [1024, 1024], P('blk'), may hold values from 0.01 to 1
- cluster_label: int32 [1024, 1024], P('blk'), may hold values from 0 to 511, as said below
Outputs:
- corrected: float32 [16, 1024, 1024], P('rhs', 'blk')
- residual_ratio: float32 [16], replicated
The draws below stay inside these ranges and needn't reach their ends.
Inputs may be any that keep to these rules, and one draw needn't show every extreme that they name: `cluster_label`: each aggregate number of a slab is held by 4 or more of that slab's cells, and the cells of one aggregate lie within 8 rows and 8 columns of one another.
All inputs are finite; a program needn't handle non-finite values.
Results may differ from the reference program's by a relative error of at most 0.0003.
Values sent between devices are 32-bit elements; how exact they have to be, the bound alone decides.
No kernel may reach another device: no remote copies, remote signals or barrier semaphores. Data moves between devices by JAX's collectives and lax.ppermute only.
A program may use at most 64 MiB of HBM per device.

```python
import math
import jax
import jax.numpy as jnp
from jax import lax

FORCING_SETS = 16
SX = 8
MESH_WIDTH = 1024
AGG = 512
MESH_HEIGHT = 1024
N_BLK = 128


def draw_cluster_label(key, part):
    local_rows = jnp.arange(MESH_HEIGHT) % SX
    mesh_width = jnp.arange(MESH_WIDTH)
    patch_row = local_rows // 4
    patch_col = mesh_width // 4
    first_key, second_key = jax.random.split(jax.random.fold_in(key, 11))
    move_up = (jax.random.randint(first_key, (MESH_HEIGHT, MESH_WIDTH), 0, 4) == 0) & ((local_rows % 4 == 0) & (patch_row > 0))[:, None]
    move_left = (jax.random.randint(second_key, (MESH_HEIGHT, MESH_WIDTH), 0, 4) == 0) & ((mesh_width % 4 == 0) & (patch_col > 0))[None, :]
    rows_final = patch_row[:, None] - move_up.astype(jnp.int32)
    cols_final = patch_col[None, :] - move_left.astype(jnp.int32)
    return (rows_final * (MESH_WIDTH // 4) + cols_final).astype(jnp.int32)


def block_levels(key, dims, cuts, low, largest):
    loudness, own = 1.0, jax.random.fold_in(key, 6)
    for axis_at, parts in cuts:
        draws = jnp.exp(jax.random.uniform(jax.random.fold_in(own, axis_at), (parts,), jnp.float32, low / len(cuts), largest / len(cuts)))
        loudness = loudness * jnp.repeat(draws, dims[axis_at] // parts).reshape([-1 if axis == axis_at else 1 for axis in range(len(dims))])
    return loudness


def bell_draw(key, dims, scale, reach, cuts=(), kind=jnp.bfloat16):
    gain = block_levels(key, dims, cuts, -0.22, 0.18) if cuts else 1.0
    drawn = jax.random.normal(key, dims, jnp.float32) * scale * gain
    return jnp.minimum(jnp.maximum(drawn, -reach), reach).astype(kind)


def setup_inputs(seed: int = 0) -> dict:
    key_list = jax.random.split(jax.random.key(seed), 5)
    thermal_solution = bell_draw(key_list[0], (FORCING_SETS, MESH_HEIGHT, MESH_WIDTH), 1.0, 6.0, ((0, 4), (1, 128)), jnp.float32)
    heat_forcing = bell_draw(key_list[1], (FORCING_SETS, MESH_HEIGHT, MESH_WIDTH), 1.0, 6.0, ((0, 4), (1, 128)), jnp.float32)
    extinction_factor = jnp.clip(jnp.exp(math.log(1.0) - 4.6051702 * jax.random.uniform(key_list[2], (MESH_HEIGHT, MESH_WIDTH), jnp.float32) ** block_levels(key_list[2], (MESH_HEIGHT, MESH_WIDTH), ((0, 128),), -0.2, 0.2)), 0.01, 1.0)
    cluster_label = draw_cluster_label(jax.random.fold_in(key_list[4], 71), 0)
    return dict(thermal_solution=thermal_solution, heat_forcing=heat_forcing, extinction_factor=extinction_factor, cluster_label=cluster_label)


damping_fine = 0.8
damping_coarse = 0.5

def stencil(field, extinction_factor):
    padded = jnp.pad(field, ((0, 0), (1, 1), (1, 1)))
    neighbours = padded[:, :-2, 1:-1] + padded[:, 2:, 1:-1] + padded[:, 1:-1, :-2] + padded[:, 1:-1, 2:]
    return (4.0 + extinction_factor) * field - neighbours

def reference(thermal_solution, heat_forcing, extinction_factor, cluster_label):
    slab_of = (jnp.arange(MESH_HEIGHT) // SX).astype(jnp.int32)
    keygrid = (cluster_label + (slab_of * AGG)[:, None]).astype(jnp.int32)
    flat_keys = keygrid.reshape(-1)
    segments = N_BLK * AGG
    diagonal0 = 4.0 + extinction_factor

    def top_level_smoother(iterate):
        return iterate + damping_fine * (heat_forcing - stencil(iterate, extinction_factor)) / diagonal0

    def restrict(field):
        return jax.vmap(lambda plane: jax.ops.segment_sum(plane.reshape(-1), flat_keys, num_segments=segments))(field)

    def prolong(coarse):
        return jnp.take(coarse, flat_keys, axis=1).reshape(FORCING_SETS, MESH_HEIGHT, MESH_WIDTH)

    def apply_coarse(coarse):
        return restrict(stencil(prolong(coarse), extinction_factor))
    keypad = jnp.pad(keygrid, 1, constant_values=-1)
    same = (keypad[:-2, 1:-1] == keygrid).astype(jnp.float32) + (keypad[2:, 1:-1] == keygrid).astype(jnp.float32) + (keypad[1:-1, :-2] == keygrid).astype(jnp.float32) + (keypad[1:-1, 2:] == keygrid).astype(jnp.float32)
    diagonal1 = jax.ops.segment_sum((4.0 + extinction_factor - same).reshape(-1), flat_keys, num_segments=segments)
    smoothed_iterate = top_level_smoother(top_level_smoother(thermal_solution))
    coarse_rhs = restrict(heat_forcing - stencil(smoothed_iterate, extinction_factor))
    level_one = damping_coarse * coarse_rhs / diagonal1
    level_one = level_one + damping_coarse * (coarse_rhs - apply_coarse(level_one)) / diagonal1
    coarse_res = coarse_rhs - apply_coarse(level_one)
    slab_count = float(N_BLK)
    slab_rhs = coarse_res.reshape(FORCING_SETS, N_BLK, AGG).sum(-1) / (AGG * slab_count)
    slab_diag = 2.0 + lax.optimization_barrier(jnp.mean(extinction_factor.reshape(N_BLK, SX * MESH_WIDTH), axis=-1)) / (slab_count * slab_count)
    offdiag = jnp.full((N_BLK,), -1.0, slab_diag.dtype)
    lower_band = offdiag.at[0].set(0.0)
    upper_band = offdiag.at[N_BLK - 1].set(0.0)
    slab_corr = lax.linalg.tridiagonal_solve(lower_band, slab_diag, upper_band, slab_rhs.T)
    level_one = level_one + jnp.repeat(slab_corr.T, AGG, axis=1)
    for sweep_number in range(2):
        level_one = level_one + damping_coarse * (coarse_rhs - apply_coarse(level_one)) / diagonal1
    corrected = top_level_smoother(top_level_smoother(smoothed_iterate + prolong(level_one)))
    final_res = heat_forcing - stencil(corrected, extinction_factor)
    ratios = jnp.sqrt(lax.optimization_barrier(jnp.sum(final_res * final_res, axis=(1, 2))) / lax.optimization_barrier(jnp.sum(heat_forcing * heat_forcing, axis=(1, 2))))
    return (corrected, ratios)
```

```python
import functools

import jax
import jax.numpy as jnp
from jax import lax
from jax.experimental import pallas as pl
from jax.experimental.pallas import tpu as pltpu
from jax.sharding import PartitionSpec as P

damping_fine = 0.8
damping_coarse = 0.5
REACH = 7
F32 = jnp.float32


def vmem_call(body, outs, scratch=(), smem_args=(), n_in=0):
    in_specs = [
        pl.BlockSpec(memory_space=pltpu.SMEM if k in smem_args else pltpu.VMEM)
        for k in range(n_in)
    ]
    return pl.pallas_call(
        body,
        out_shape=[jax.ShapeDtypeStruct(s, F32) for s in outs],
        in_specs=in_specs,
        out_specs=[pl.BlockSpec(memory_space=pltpu.VMEM)] * len(outs),
        scratch_shapes=list(scratch),
        compiler_params=pltpu.CompilerParams(vmem_limit_bytes=48 << 20),
    )


def iotas(shape):
    return (
        lax.broadcasted_iota(jnp.int32, shape, 0),
        lax.broadcasted_iota(jnp.int32, shape, 1),
    )


def sideways(x):
    rows, width = x.shape
    col = lax.broadcasted_iota(jnp.int32, x.shape, 1)
    left = jnp.where(col == 0, 0.0, pltpu.roll(x, 1, 1))
    right = jnp.where(col == width - 1, 0.0, pltpu.roll(x, width - 1, 1))
    return left + right


def neighbours(x, above, below):
    rows = x.shape[0]
    row = lax.broadcasted_iota(jnp.int32, x.shape, 0)
    up = jnp.where(row == 0, above, pltpu.roll(x, 1, 0))
    down = jnp.where(row == rows - 1, below, pltpu.roll(x, rows - 1, 0))
    return up + down + sideways(x)


def seg_sum(lab, fields, lab_ref, lab_shift, field_shift, out_ref):
    rows, width = lab.shape
    n = len(fields)
    shifts = list(range(-REACH, REACH + 1))
    for d, dx in enumerate(shifts):
        amount = (-dx) % width
        lab_shift[d] = pltpu.roll(lab, amount, 1) if amount else lab
        for f in range(n):
            field_shift[d, f] = pltpu.roll(fields[f], amount, 1) if amount else fields[f]
    chunk = 256

    def step(j, carry):
        at = pl.ds(pl.multiple_of(j * chunk, chunk), chunk)
        own = lab_ref[:, at]
        sums = [jnp.zeros((rows, chunk), F32) for _ in range(n)]
        for d in range(len(shifts)):
            for r in range(rows):
                there = jnp.broadcast_to(lab_shift[d, pl.ds(r, 1), at], (rows, chunk))
                same = there == own
                for f in range(n):
                    w = jnp.broadcast_to(field_shift[d, f, pl.ds(r, 1), at], (rows, chunk))
                    sums[f] = sums[f] + jnp.where(same, w, 0.0)
        for f in range(n):
            out_ref[f, :, at] = sums[f]
        return carry

    lax.fori_loop(0, width // chunk, step, 0)


def seg_scratch(n, rows, width):
    d = 2 * REACH + 1
    return [
        pltpu.VMEM((d, rows, width), jnp.int32),
        pltpu.VMEM((d, n, rows, width), F32),
        pltpu.VMEM((n, rows, width), F32),
    ]


def pack_kernel(u, f, ext, first, last):
    cases, rows, width = u.shape
    ones = jnp.ones((cases, width), F32)
    for out, order in ((first, (0, 1, 2)), (last, (rows - 1, rows - 2, rows - 3))):
        for k in range(3):
            out[k] = u[:, order[k], :]
        for k in range(2):
            out[3 + k] = f[:, order[k], :]
            out[5 + k] = jnp.broadcast_to(ext[pl.ds(order[k], 1), :], (cases, width))
        out[7] = ones


def both(before, after, k):
    return jnp.concatenate([before[k], after[k]], axis=0)


def two_sweeps(u, u_halo, f, f_halo, diag, diag_halo, valid):
    cases = len(u)
    rows = u[0].shape[0]
    gain = damping_fine / diag
    gain_halo = [damping_fine / d for d in diag_halo]
    keep = 1.0 - damping_fine

    def edge(x):
        return jnp.concatenate(
            [v[0:1] for v in x] + [v[rows - 1 : rows] for v in x], axis=0
        )

    def sweep(x, halo, depth):
        new = [
            keep * x[c]
            + gain * (f[c] + neighbours(x[c], halo[0][c : c + 1], halo[0][cases + c : cases + c + 1]))
            for c in range(cases)
        ]
        inner = [edge(x)] + halo
        new_halo = []
        for k in range(depth):
            v = keep * halo[k] + gain_halo[k] * (
                f_halo[k] + inner[k] + inner[k + 2] + sideways(halo[k])
            )
            new_halo.append(v * valid)
        return new, new_halo

    x, h = sweep(u, u_halo, 2)
    x, h = sweep(x, h, 1)
    res = [
        f[c] - diag * x[c] + neighbours(x[c], h[0][c : c + 1], h[0][cases + c : cases + c + 1])
        for c in range(cases)
    ]
    return x, res


def total(x):
    rows, width = x.shape
    part = x[:, 0:128]
    for k in range(1, width // 128):
        part = part + x[:, k * 128 : (k + 1) * 128]
    return jnp.sum(jnp.sum(part, axis=1, keepdims=True), axis=0, keepdims=True)


def lane_row(values):
    lane = lax.broadcasted_iota(jnp.int32, (1, 128), 1)
    row = jnp.zeros((1, 128), F32)
    for k, v in values:
        row = jnp.where(lane == k, v, row)
    return row


def pre_kernel(u, f, ext, lab, before, after, smooth, b, h, x0, first, last, rsum, ls, fs, ss):
    cases, rows, width = u.shape
    diag = 4.0 + ext[...]
    us = [u[c] for c in range(cases)]
    fl = [f[c] for c in range(cases)]
    u_halo = [both(before, after, k) for k in range(3)]
    f_halo = [both(before, after, 3 + k) for k in range(2)]
    d_halo = [4.0 + both(before, after, 5 + k) for k in range(2)]
    valid = both(before, after, 7)
    x, res = two_sweeps(us, u_halo, fl, f_halo, diag, d_halo, valid)
    for c in range(cases):
        smooth[c] = x[c]
    key = lab[...]
    row, col = iotas(key.shape)
    one = jnp.ones(key.shape, F32)
    zero = jnp.zeros(key.shape, F32)
    m = jnp.where((pltpu.roll(key, 1, 0) == key) & (row > 0), one, zero)
    m = m + jnp.where((pltpu.roll(key, rows - 1, 0) == key) & (row < rows - 1), one, zero)
    m = m + jnp.where((pltpu.roll(key, 1, 1) == key) & (col > 0), one, zero)
    m = m + jnp.where((pltpu.roll(key, width - 1, 1) == key) & (col < width - 1), one, zero)
    seg_sum(key, res + [diag - m], lab, ls, fs, ss)
    half = damping_coarse / ss[cases]
    h[...] = half
    for c in range(cases):
        b[c] = ss[c]
        v = half * ss[c]
        x0[c] = v
        first[pl.ds(c, 1), :] = v[0:1]
        last[pl.ds(c, 1), :] = v[rows - 1 : rows]
    rsum[...] = lane_row([(c, total(res[c])) for c in range(cases)])


def coarse_step(x, above, below, ext, lab, b, h, ls, fs, ss):
    cases = len(x)
    diag = 4.0 + ext[...]
    w = [
        diag * x[c] - neighbours(x[c], above[c], below[c])
        for c in range(cases)
    ]
    seg_sum(lab[...], w, lab, ls, fs, ss)
    return [x[c] + h[...] * (b[c] - ss[c]) for c in range(cases)]


def store_edges(x, first, last):
    rows = x[0].shape[0]
    for c in range(len(x)):
        first[pl.ds(c, 1), :] = x[c][0:1]
        last[pl.ds(c, 1), :] = x[c][rows - 1 : rows]


def coarse_kernel_a(x0, ext, lab, b, h, rsum, before, after, x1, first, last, gather, ls, fs, ss):
    cases, rows, width = x0.shape
    x = coarse_step(
        [x0[c] for c in range(cases)],
        [before[pl.ds(c, 1), :] for c in range(cases)],
        [after[pl.ds(c, 1), :] for c in range(cases)],
        ext, lab, b, h, ls, fs, ss,
    )
    store_edges(x, first, last)
    row, col = iotas((rows, width))
    one = jnp.ones((rows, width), F32)
    zero = jnp.zeros((rows, width), F32)
    weight = ext[...]
    for at_edge in (row == 0, row == rows - 1, col == 0, col == width - 1):
        weight = weight + jnp.where(at_edge, one, zero)
    values = []
    for c in range(cases):
        x1[c] = x[c]
        own = rsum[:, c : c + 1] - total(weight * x[c])
        values.append((c, own))
        values.append((cases + c, total(x[c][0:1])))
        values.append((2 * cases + c, total(x[c][rows - 1 : rows])))
    values.append((3 * cases, total(ext[...])))
    gather[...] = jnp.broadcast_to(lane_row(values), gather.shape)


def solve_slabs(g, cases, groups, cells):
    n = g.shape[0]
    row, lane = iotas(g.shape)
    top = pltpu.roll(pltpu.roll(g, 128 - cases, 1), n - 1, 0)
    bottom = pltpu.roll(pltpu.roll(g, 128 - 2 * cases, 1), 1, 0)
    b = g + jnp.where(row == n - 1, 0.0, top) + jnp.where(row == 0, 0.0, bottom)
    b = jnp.where(lane < cases, b / (groups * float(n)), 0.0)
    mean = jnp.broadcast_to(g[:, 3 * cases : 3 * cases + 1], g.shape) / float(cells)
    d = 2.0 + mean / (float(n) * float(n))
    lower = jnp.where(row == 0, 0.0, 1.0)
    upper = jnp.where(row == n - 1, 0.0, 1.0)
    excess = (d - lower) - upper
    s = 1
    while s < n:
        inv = 1.0 / (lower + upper + excess)
        alpha = lower * pltpu.roll(inv, s, 0)
        gamma = upper * pltpu.roll(inv, n - s, 0)
        b = b + alpha * pltpu.roll(b, s, 0) + gamma * pltpu.roll(b, n - s, 0)
        excess = excess + alpha * pltpu.roll(excess, s, 0) + gamma * pltpu.roll(excess, n - s, 0)
        lower = alpha * pltpu.roll(lower, s, 0)
        upper = gamma * pltpu.roll(upper, n - s, 0)
        s *= 2
    return b / (lower + upper + excess)


def coarse_kernel_b(groups, at, x1, ext, lab, b, h, before, after, gathered, x3, first, last, ls, fs, ss, e_ref):
    cases, rows, width = x1.shape
    n = gathered.shape[0]
    i = at[0]
    e_ref[pl.ds(8, n), :] = solve_slabs(gathered[...], cases, groups, rows * width)
    e_ref[pl.ds(0, 8), :] = jnp.zeros((8, 128), F32)
    e_ref[pl.ds(8 + n, 8), :] = jnp.zeros((8, 128), F32)
    e_above = e_ref[pl.ds(i + 7, 1), :]
    e_own = e_ref[pl.ds(i + 8, 1), :]
    e_below = e_ref[pl.ds(i + 9, 1), :]
    x = coarse_step(
        [x1[c] + e_own[:, c : c + 1] for c in range(cases)],
        [before[pl.ds(c, 1), :] + e_above[:, c : c + 1] for c in range(cases)],
        [after[pl.ds(c, 1), :] + e_below[:, c : c + 1] for c in range(cases)],
        ext, lab, b, h, ls, fs, ss,
    )
    store_edges(x, first, last)
    for c in range(cases):
        x3[c] = x[c]


def coarse_kernel_c(x3, ext, lab, b, h, smooth, before, after, v, first, last, ls, fs, ss):
    cases, rows, width = x3.shape
    x = coarse_step(
        [x3[c] for c in range(cases)],
        [before[pl.ds(c, 1), :] for c in range(cases)],
        [after[pl.ds(c, 1), :] for c in range(cases)],
        ext, lab, b, h, ls, fs, ss,
    )
    for c in range(cases):
        y = smooth[c] + x[c]
        v[c] = y
        for k in range(3):
            first[k, pl.ds(c, 1), :] = y[k : k + 1]
            last[k, pl.ds(c, 1), :] = y[rows - 1 - k : rows - k]


def post_kernel(v, f, ext, before, after, before_v, after_v, out, gather):
    cases, rows, width = v.shape
    diag = 4.0 + ext[...]
    fl = [f[c] for c in range(cases)]
    v_halo = [both(before_v, after_v, k) for k in range(3)]
    f_halo = [both(before, after, 3 + k) for k in range(2)]
    d_halo = [4.0 + both(before, after, 5 + k) for k in range(2)]
    valid = both(before, after, 7)
    x, res = two_sweeps([v[c] for c in range(cases)], v_halo, fl, f_halo, diag, d_halo, valid)
    values = []
    for c in range(cases):
        out[c] = x[c]
        values.append((c, total(res[c] * res[c])))
        values.append((cases + c, total(fl[c] * fl[c])))
    gather[...] = jnp.broadcast_to(lane_row(values), gather.shape)


def ratio_kernel(cases, g, out):
    s = jnp.sum(g[...], axis=0, keepdims=True)
    ratio = jnp.sqrt(s / pltpu.roll(s, 128 - cases, 1))
    lane = lax.broadcasted_iota(jnp.int32, s.shape, 1)
    out[...] = jnp.broadcast_to(jnp.where(lane < cases, ratio, 0.0), out.shape)


def local(thermal_solution, heat_forcing, extinction_factor, cluster_label):
    cases, rows, width = thermal_solution.shape
    n = lax.axis_size("blk")
    n_rhs = lax.axis_size("rhs")
    groups = rows * width // 16
    field = (cases, rows, width)
    up = [(i, i + 1) for i in range(n - 1)]
    down = [(j, i) for i, j in up]

    def exchange(first, last):
        return lax.ppermute(last, "blk", up), lax.ppermute(first, "blk", down)

    def to_all(x, axis):
        return lax.all_to_all(x, axis, 0, 0, tiled=True)

    seg4 = seg_scratch(cases, rows, width)
    edge = (cases, width)
    u, f, ext, lab = thermal_solution, heat_forcing, extinction_factor, cluster_label
    first, last = vmem_call(pack_kernel, [(8, cases, width)] * 2, n_in=3)(u, f, ext)
    before, after = exchange(first, last)
    smooth, b, h, x0, first, last, rsum = vmem_call(
        pre_kernel,
        [field, field, (rows, width), field, edge, edge, (1, 128)],
        seg_scratch(cases + 1, rows, width),
        n_in=6,
    )(u, f, ext, lab, before, after)
    ab, be = exchange(first, last)
    x1, first, last, mine = vmem_call(
        coarse_kernel_a, [field, edge, edge, (n, 128)], seg4, n_in=8
    )(x0, ext, lab, b, h, rsum, ab, be)
    ab, be = exchange(first, last)
    gathered = to_all(mine, "blk")
    at = lax.axis_index("blk").astype(jnp.int32).reshape(1)
    x3, first, last = vmem_call(
        functools.partial(coarse_kernel_b, groups),
        [field, edge, edge],
        seg4 + [pltpu.VMEM((n + 16, 128), F32)],
        smem_args=(0,),
        n_in=9,
    )(at, x1, ext, lab, b, h, ab, be, gathered)
    ab, be = exchange(first, last)
    v, first, last = vmem_call(
        coarse_kernel_c, [field, (3, cases, width), (3, cases, width)], seg4, n_in=8
    )(x3, ext, lab, b, h, smooth, ab, be)
    ab, be = exchange(first, last)
    corrected, mine = vmem_call(post_kernel, [field, (n, 128)], n_in=7)(
        v, f, ext, before, after, ab, be
    )
    gathered = to_all(mine, "blk")
    (ratio,) = vmem_call(
        functools.partial(ratio_kernel, cases), [(n_rhs, 128)], n_in=1
    )(gathered)
    every = to_all(ratio, "rhs")
    return corrected, every[:, :cases].reshape(n_rhs * cases)


def solution(mesh):
    in_specs = (P("rhs", "blk", None), P("rhs", "blk", None), P("blk", None), P("blk", None))
    out_specs = (P("rhs", "blk", None), P())
    return jax.shard_map(local, mesh=mesh, in_specs=in_specs, out_specs=out_specs, check_vma=False)
```

```python
import functools

import jax
import jax.numpy as jnp
from jax import lax
from jax.experimental import pallas as pl
from jax.experimental.pallas import tpu as pltpu
from jax.sharding import PartitionSpec as P

damping_fine = 0.8
damping_coarse = 0.5
REACH = 7
F32 = jnp.float32


def vmem_call(body, outs, scratch=(), smem_args=(), n_in=0):
    in_specs = [
        pl.BlockSpec(memory_space=pltpu.SMEM if k in smem_args else pltpu.VMEM)
        for k in range(n_in)
    ]
    return pl.pallas_call(
        body,
        out_shape=[
            jax.ShapeDtypeStruct(*(s if isinstance(s[0], tuple) else (s, F32))) for s in outs
        ],
        in_specs=in_specs,
        out_specs=[pl.BlockSpec(memory_space=pltpu.VMEM)] * len(outs),
        scratch_shapes=list(scratch),
        compiler_params=pltpu.CompilerParams(vmem_limit_bytes=48 << 20),
    )


def iotas(shape):
    return (
        lax.broadcasted_iota(jnp.int32, shape, 0),
        lax.broadcasted_iota(jnp.int32, shape, 1),
    )


def sideways(x):
    rows, width = x.shape
    col = lax.broadcasted_iota(jnp.int32, x.shape, 1)
    left = jnp.where(col == 0, 0.0, pltpu.roll(x, 1, 1))
    right = jnp.where(col == width - 1, 0.0, pltpu.roll(x, width - 1, 1))
    return left + right


def neighbours(x, above, below):
    rows = x.shape[0]
    row = lax.broadcasted_iota(jnp.int32, x.shape, 0)
    up = jnp.where(row == 0, above, pltpu.roll(x, 1, 0))
    down = jnp.where(row == rows - 1, below, pltpu.roll(x, rows - 1, 0))
    return up + down + sideways(x)


def offsets():
    return [d for d in range(-REACH, REACH + 1) if d]


def seg_sum(fields, tables):
    row_at, row_ok, same_col = tables
    rows, width = fields[0].shape
    col = list(fields)
    for k in range(1, rows):
        m = same_col[k - 1]
        col = [s + m * pltpu.roll(w, k, 0) for s, w in zip(col, fields)]
    out = list(col)
    for d, dx in enumerate(offsets()):
        at, ok = row_at[d], row_ok[d]
        out = [
            t
            + ok
            * jnp.take_along_axis(
                pltpu.roll(s, (-dx) % width, 1), at, axis=0, mode="promise_in_bounds"
            )
            for t, s in zip(out, col)
        ]
    return out


def table_kernel(ext, lab, row_at, row_ok, same_col, h):
    key = lab[...]
    rows, width = key.shape
    for k in range(1, rows):
        same_col[k - 1] = jnp.where(pltpu.roll(key, k, 0) == key, 1.0, 0.0)
    for d, dx in enumerate(offsets()):
        there = pltpu.roll(key, (-dx) % width, 1)
        at = jnp.full(key.shape, -1, jnp.int32)
        for r in range(rows):
            at = jnp.where(jnp.broadcast_to(there[r : r + 1], key.shape) == key, r, at)
        row_ok[d] = jnp.where(at >= 0, 1.0, 0.0)
        row_at[d] = jnp.maximum(at, 0)
    row, col = iotas(key.shape)
    one = jnp.ones(key.shape, F32)
    zero = jnp.zeros(key.shape, F32)
    m = jnp.where((pltpu.roll(key, 1, 0) == key) & (row > 0), one, zero)
    m = m + jnp.where((pltpu.roll(key, rows - 1, 0) == key) & (row < rows - 1), one, zero)
    m = m + jnp.where((pltpu.roll(key, 1, 1) == key) & (col > 0), one, zero)
    m = m + jnp.where((pltpu.roll(key, width - 1, 1) == key) & (col < width - 1), one, zero)
    (diag1,) = seg_sum([4.0 + ext[...] - m], (row_at, row_ok, same_col))
    h[...] = damping_coarse / diag1


def pack_kernel(u, f, ext, first, last):
    cases, rows, width = u.shape
    ones = jnp.ones((cases, width), F32)
    for out, order in ((first, (0, 1, 2)), (last, (rows - 1, rows - 2, rows - 3))):
        for k in range(3):
            out[k] = u[:, order[k], :]
        for k in range(2):
            out[3 + k] = f[:, order[k], :]
            out[5 + k] = jnp.broadcast_to(ext[pl.ds(order[k], 1), :], (cases, width))
        out[7] = ones


def both(before, after, k):
    return jnp.concatenate([before[k], after[k]], axis=0)


def two_sweeps(u, u_halo, f, f_halo, diag, diag_halo, valid):
    cases = len(u)
    rows = u[0].shape[0]
    gain = damping_fine / diag
    gain_halo = [damping_fine / d for d in diag_halo]
    keep = 1.0 - damping_fine

    def edge(x):
        return jnp.concatenate(
            [v[0:1] for v in x] + [v[rows - 1 : rows] for v in x], axis=0
        )

    def sweep(x, halo, depth):
        new = [
            keep * x[c]
            + gain * (f[c] + neighbours(x[c], halo[0][c : c + 1], halo[0][cases + c : cases + c + 1]))
            for c in range(cases)
        ]
        inner = [edge(x)] + halo
        new_halo = []
        for k in range(depth):
            v = keep * halo[k] + gain_halo[k] * (
                f_halo[k] + inner[k] + inner[k + 2] + sideways(halo[k])
            )
            new_halo.append(v * valid)
        return new, new_halo

    x, h = sweep(u, u_halo, 2)
    x, h = sweep(x, h, 1)
    res = [
        f[c] - diag * x[c] + neighbours(x[c], h[0][c : c + 1], h[0][cases + c : cases + c + 1])
        for c in range(cases)
    ]
    return x, res


def total(x):
    rows, width = x.shape
    part = x[:, 0:128]
    for k in range(1, width // 128):
        part = part + x[:, k * 128 : (k + 1) * 128]
    return jnp.sum(jnp.sum(part, axis=1, keepdims=True), axis=0, keepdims=True)


def lane_row(values):
    lane = lax.broadcasted_iota(jnp.int32, (1, 128), 1)
    row = jnp.zeros((1, 128), F32)
    for k, v in values:
        row = jnp.where(lane == k, v, row)
    return row


def pre_kernel(u, f, ext, before, after, row_at, row_ok, same_col, h, smooth, b, x0, first, last, rsum):
    cases, rows, width = u.shape
    diag = 4.0 + ext[...]
    us = [u[c] for c in range(cases)]
    fl = [f[c] for c in range(cases)]
    u_halo = [both(before, after, k) for k in range(3)]
    f_halo = [both(before, after, 3 + k) for k in range(2)]
    d_halo = [4.0 + both(before, after, 5 + k) for k in range(2)]
    valid = both(before, after, 7)
    x, res = two_sweeps(us, u_halo, fl, f_halo, diag, d_halo, valid)
    for c in range(cases):
        smooth[c] = x[c]
    sums = seg_sum(res, (row_at, row_ok, same_col))
    for c in range(cases):
        b[c] = sums[c]
        v = h[...] * sums[c]
        x0[c] = v
        first[pl.ds(c, 1), :] = v[0:1]
        last[pl.ds(c, 1), :] = v[rows - 1 : rows]
    rsum[...] = lane_row([(c, total(res[c])) for c in range(cases)])


def coarse_step(x, above, below, ext, b, h, tables):
    cases = len(x)
    diag = 4.0 + ext[...]
    w = [diag * x[c] - neighbours(x[c], above[c], below[c]) for c in range(cases)]
    sums = seg_sum(w, tables)
    return [x[c] + h[...] * (b[c] - sums[c]) for c in range(cases)]


def store_edges(x, first, last):
    rows = x[0].shape[0]
    for c in range(len(x)):
        first[pl.ds(c, 1), :] = x[c][0:1]
        last[pl.ds(c, 1), :] = x[c][rows - 1 : rows]


def coarse_kernel_a(x0, ext, b, row_at, row_ok, same_col, h, rsum, before, after, x1, first, last, gather):
    cases, rows, width = x0.shape
    x = coarse_step(
        [x0[c] for c in range(cases)],
        [before[pl.ds(c, 1), :] for c in range(cases)],
        [after[pl.ds(c, 1), :] for c in range(cases)],
        ext, b, h, (row_at, row_ok, same_col),
    )
    store_edges(x, first, last)
    row, col = iotas((rows, width))
    one = jnp.ones((rows, width), F32)
    zero = jnp.zeros((rows, width), F32)
    weight = ext[...]
    for at_edge in (row == 0, row == rows - 1, col == 0, col == width - 1):
        weight = weight + jnp.where(at_edge, one, zero)
    values = []
    for c in range(cases):
        x1[c] = x[c]
        own = rsum[:, c : c + 1] - total(weight * x[c])
        values.append((c, own))
        values.append((cases + c, total(x[c][0:1])))
        values.append((2 * cases + c, total(x[c][rows - 1 : rows])))
    values.append((3 * cases, total(ext[...])))
    gather[...] = jnp.broadcast_to(lane_row(values), gather.shape)


def solve_slabs(g, cases, groups, cells):
    n = g.shape[0]
    row, lane = iotas(g.shape)
    top = pltpu.roll(pltpu.roll(g, 128 - cases, 1), n - 1, 0)
    bottom = pltpu.roll(pltpu.roll(g, 128 - 2 * cases, 1), 1, 0)
    b = g + jnp.where(row == n - 1, 0.0, top) + jnp.where(row == 0, 0.0, bottom)
    b = jnp.where(lane < cases, b / (groups * float(n)), 0.0)
    mean = jnp.broadcast_to(g[:, 3 * cases : 3 * cases + 1], g.shape) / float(cells)
    d = 2.0 + mean / (float(n) * float(n))
    lower = jnp.where(row == 0, 0.0, 1.0)
    upper = jnp.where(row == n - 1, 0.0, 1.0)
    excess = (d - lower) - upper
    s = 1
    while s < n:
        inv = 1.0 / (lower + upper + excess)
        alpha = lower * pltpu.roll(inv, s, 0)
        gamma = upper * pltpu.roll(inv, n - s, 0)
        b = b + alpha * pltpu.roll(b, s, 0) + gamma * pltpu.roll(b, n - s, 0)
        excess = excess + alpha * pltpu.roll(excess, s, 0) + gamma * pltpu.roll(excess, n - s, 0)
        lower = alpha * pltpu.roll(lower, s, 0)
        upper = gamma * pltpu.roll(upper, n - s, 0)
        s *= 2
    return b / (lower + upper + excess)


def coarse_kernel_b(groups, at, x1, ext, b, row_at, row_ok, same_col, h, before, after, gathered, x3, first, last, e_ref):
    cases, rows, width = x1.shape
    n = gathered.shape[0]
    i = at[0]
    e_ref[pl.ds(8, n), :] = solve_slabs(gathered[...], cases, groups, rows * width)
    e_ref[pl.ds(0, 8), :] = jnp.zeros((8, 128), F32)
    e_ref[pl.ds(8 + n, 8), :] = jnp.zeros((8, 128), F32)
    e_above = e_ref[pl.ds(i + 7, 1), :]
    e_own = e_ref[pl.ds(i + 8, 1), :]
    e_below = e_ref[pl.ds(i + 9, 1), :]
    x = coarse_step(
        [x1[c] + e_own[:, c : c + 1] for c in range(cases)],
        [before[pl.ds(c, 1), :] + e_above[:, c : c + 1] for c in range(cases)],
        [after[pl.ds(c, 1), :] + e_below[:, c : c + 1] for c in range(cases)],
        ext, b, h, (row_at, row_ok, same_col),
    )
    store_edges(x, first, last)
    for c in range(cases):
        x3[c] = x[c]


def coarse_kernel_c(x3, ext, b, row_at, row_ok, same_col, h, smooth, before, after, v, first, last):
    cases, rows, width = x3.shape
    x = coarse_step(
        [x3[c] for c in range(cases)],
        [before[pl.ds(c, 1), :] for c in range(cases)],
        [after[pl.ds(c, 1), :] for c in range(cases)],
        ext, b, h, (row_at, row_ok, same_col),
    )
    for c in range(cases):
        y = smooth[c] + x[c]
        v[c] = y
        for k in range(3):
            first[k, pl.ds(c, 1), :] = y[k : k + 1]
            last[k, pl.ds(c, 1), :] = y[rows - 1 - k : rows - k]


def post_kernel(v, f, ext, before, after, before_v, after_v, out, gather):
    cases, rows, width = v.shape
    diag = 4.0 + ext[...]
    fl = [f[c] for c in range(cases)]
    v_halo = [both(before_v, after_v, k) for k in range(3)]
    f_halo = [both(before, after, 3 + k) for k in range(2)]
    d_halo = [4.0 + both(before, after, 5 + k) for k in range(2)]
    valid = both(before, after, 7)
    x, res = two_sweeps([v[c] for c in range(cases)], v_halo, fl, f_halo, diag, d_halo, valid)
    values = []
    for c in range(cases):
        out[c] = x[c]
        values.append((c, total(res[c] * res[c])))
        values.append((cases + c, total(fl[c] * fl[c])))
    gather[...] = jnp.broadcast_to(lane_row(values), gather.shape)


def ratio_kernel(cases, g, out):
    s = jnp.sum(g[...], axis=0, keepdims=True)
    ratio = jnp.sqrt(s / pltpu.roll(s, 128 - cases, 1))
    lane = lax.broadcasted_iota(jnp.int32, s.shape, 1)
    out[...] = jnp.broadcast_to(jnp.where(lane < cases, ratio, 0.0), out.shape)


def local(thermal_solution, heat_forcing, extinction_factor, cluster_label):
    cases, rows, width = thermal_solution.shape
    n = lax.axis_size("blk")
    n_rhs = lax.axis_size("rhs")
    groups = rows * width // 16
    field = (cases, rows, width)
    up = [(i, i + 1) for i in range(n - 1)]
    down = [(j, i) for i, j in up]

    def exchange(first, last):
        return lax.ppermute(last, "blk", up), lax.ppermute(first, "blk", down)

    def to_all(x, axis):
        return lax.all_to_all(x, axis, 0, 0, tiled=True)

    edge = (cases, width)
    u, f, ext, lab = thermal_solution, heat_forcing, extinction_factor, cluster_label
    first, last = vmem_call(pack_kernel, [(8, cases, width)] * 2, n_in=3)(u, f, ext)
    before, after = exchange(first, last)
    shifts = len(offsets())
    cells = (rows, width)
    tables = vmem_call(
        table_kernel,
        [((shifts, rows, width), jnp.int32), (shifts, rows, width), (rows - 1, rows, width), cells],
        n_in=2,
    )(ext, lab)
    smooth, b, x0, first, last, rsum = vmem_call(
        pre_kernel, [field, field, field, edge, edge, (1, 128)], n_in=9
    )(u, f, ext, before, after, *tables)
    ab, be = exchange(first, last)
    x1, first, last, mine = vmem_call(
        coarse_kernel_a, [field, edge, edge, (n, 128)], n_in=10
    )(x0, ext, b, *tables, rsum, ab, be)
    ab, be = exchange(first, last)
    gathered = to_all(mine, "blk")
    at = lax.axis_index("blk").astype(jnp.int32).reshape(1)
    x3, first, last = vmem_call(
        functools.partial(coarse_kernel_b, groups),
        [field, edge, edge],
        [pltpu.VMEM((n + 16, 128), F32)],
        smem_args=(0,),
        n_in=11,
    )(at, x1, ext, b, *tables, ab, be, gathered)
    ab, be = exchange(first, last)
    v, first, last = vmem_call(
        coarse_kernel_c, [field, (3, cases, width), (3, cases, width)], n_in=10
    )(x3, ext, b, *tables, smooth, ab, be)
    ab, be = exchange(first, last)
    corrected, mine = vmem_call(post_kernel, [field, (n, 128)], n_in=7)(
        v, f, ext, before, after, ab, be
    )
    gathered = to_all(mine, "blk")
    (ratio,) = vmem_call(
        functools.partial(ratio_kernel, cases), [(n_rhs, 128)], n_in=1
    )(gathered)
    every = to_all(ratio, "rhs")
    return corrected, every[:, :cases].reshape(n_rhs * cases)


def solution(mesh):
    in_specs = (P("rhs", "blk", None), P("rhs", "blk", None), P("blk", None), P("blk", None))
    out_specs = (P("rhs", "blk", None), P())
    return jax.shard_map(local, mesh=mesh, in_specs=in_specs, out_specs=out_specs, check_vma=False)
```

```python
import functools

import jax
import jax.numpy as jnp
from jax import lax
from jax.experimental import pallas as pl
from jax.experimental.pallas import tpu as pltpu
from jax.sharding import PartitionSpec as P

damping_fine = 0.8
damping_coarse = 0.5
REACH = 7
F32 = jnp.float32


def vmem_call(body, outs, scratch=(), smem_args=(), n_in=0):
    in_specs = [
        pl.BlockSpec(memory_space=pltpu.SMEM if k in smem_args else pltpu.VMEM)
        for k in range(n_in)
    ]
    return pl.pallas_call(
        body,
        out_shape=[
            jax.ShapeDtypeStruct(*(s if isinstance(s[0], tuple) else (s, F32))) for s in outs
        ],
        in_specs=in_specs,
        out_specs=[pl.BlockSpec(memory_space=pltpu.VMEM)] * len(outs),
        scratch_shapes=list(scratch),
        compiler_params=pltpu.CompilerParams(vmem_limit_bytes=48 << 20),
    )


def iotas(shape):
    return (
        lax.broadcasted_iota(jnp.int32, shape, 0),
        lax.broadcasted_iota(jnp.int32, shape, 1),
    )


def sideways(x):
    rows, width = x.shape
    col = lax.broadcasted_iota(jnp.int32, x.shape, 1)
    left = jnp.where(col == 0, 0.0, pltpu.roll(x, 1, 1))
    right = jnp.where(col == width - 1, 0.0, pltpu.roll(x, width - 1, 1))
    return left + right


def neighbours(x, above, below):
    rows = x.shape[0]
    row = lax.broadcasted_iota(jnp.int32, x.shape, 0)
    up = jnp.where(row == 0, above, pltpu.roll(x, 1, 0))
    down = jnp.where(row == rows - 1, below, pltpu.roll(x, rows - 1, 0))
    return up + down + sideways(x)


def offsets():
    return [d for d in range(-REACH, REACH + 1) if d]


def seg_sum(fields, tables):
    row_at, row_ok, same_col = tables
    rows, width = fields[0].shape
    col = list(fields)
    for k in range(1, rows):
        m = same_col[k - 1]
        col = [s + m * pltpu.roll(w, k, 0) for s, w in zip(col, fields)]
    out = list(col)
    for d, dx in enumerate(offsets()):
        at, ok = row_at[d], row_ok[d]
        out = [
            t
            + ok
            * jnp.take_along_axis(
                pltpu.roll(s, (-dx) % width, 1), at, axis=0, mode="promise_in_bounds"
            )
            for t, s in zip(out, col)
        ]
    return out


def table_kernel(n, me, ext, lab, row_at, row_ok, same_col, h, y3):
    key = lab[...]
    rows, width = key.shape
    for k in range(1, rows):
        same_col[k - 1] = jnp.where(pltpu.roll(key, k, 0) == key, 1.0, 0.0)
    for d, dx in enumerate(offsets()):
        there = pltpu.roll(key, (-dx) % width, 1)
        at = jnp.full(key.shape, -1, jnp.int32)
        for r in range(rows):
            at = jnp.where(jnp.broadcast_to(there[r : r + 1], key.shape) == key, r, at)
        row_ok[d] = jnp.where(at >= 0, 1.0, 0.0)
        row_at[d] = jnp.maximum(at, 0)
    row, col = iotas(key.shape)
    one = jnp.ones(key.shape, F32)
    zero = jnp.zeros(key.shape, F32)
    m = jnp.where((pltpu.roll(key, 1, 0) == key) & (row > 0), one, zero)
    m = m + jnp.where((pltpu.roll(key, rows - 1, 0) == key) & (row < rows - 1), one, zero)
    m = m + jnp.where((pltpu.roll(key, 1, 1) == key) & (col > 0), one, zero)
    m = m + jnp.where((pltpu.roll(key, width - 1, 1) == key) & (col < width - 1), one, zero)
    above = jnp.where(me[0] > 0, 1.0, 0.0)
    below = jnp.where(me[0] < n - 1, 1.0, 0.0)
    top = jnp.where(row == 0, one, zero)
    bottom = jnp.where(row == rows - 1, one, zero)
    open_sides = open_weight(ext[...])
    diag1, s_top, s_own, s_bottom = seg_sum(
        [4.0 + ext[...] - m, top, open_sides, bottom], (row_at, row_ok, same_col)
    )
    half = damping_coarse / diag1
    h[...] = half
    y3[0] = above * (half * s_top)
    y3[1] = 1.0 - half * s_own
    y3[2] = below * (half * s_bottom)


def open_weight(ext):
    rows, width = ext.shape
    row, col = iotas(ext.shape)
    one = jnp.ones(ext.shape, F32)
    zero = jnp.zeros(ext.shape, F32)
    weight = ext
    for at_edge in (row == 0, row == rows - 1, col == 0, col == width - 1):
        weight = weight + jnp.where(at_edge, one, zero)
    return weight


def pack_kernel(u, f, ext, first, last):
    cases, rows, width = u.shape
    ones = jnp.ones((cases, width), F32)
    for out, order in ((first, (0, 1, 2)), (last, (rows - 1, rows - 2, rows - 3))):
        for k in range(3):
            out[k] = u[:, order[k], :]
        for k in range(2):
            out[3 + k] = f[:, order[k], :]
            out[5 + k] = jnp.broadcast_to(ext[pl.ds(order[k], 1), :], (cases, width))
        out[7] = ones


def both(before, after, k):
    return jnp.concatenate([before[k], after[k]], axis=0)


def two_sweeps(u, u_halo, f, f_halo, diag, diag_halo, valid):
    cases = len(u)
    rows = u[0].shape[0]
    gain = damping_fine / diag
    gain_halo = [damping_fine / d for d in diag_halo]
    keep = 1.0 - damping_fine

    def edge(x):
        return jnp.concatenate([v[0:1] for v in x] + [v[rows - 1 : rows] for v in x], axis=0)

    def around(x, halo, c):
        return neighbours(x[c], halo[0][c : c + 1], halo[0][cases + c : cases + c + 1])

    def sweep(x, halo, depth):
        new = []
        for c in range(cases):
            push = around(x, halo, c)
            new.append(keep * x[c] + gain * (push if f is None else f[c] + push))
        inner = [edge(x)] + halo
        new_halo = []
        for k in range(depth):
            push = inner[k] + inner[k + 2] + sideways(halo[k])
            push = push if f is None else f_halo[k] + push
            new_halo.append((keep * halo[k] + gain_halo[k] * push) * valid)
        return new, new_halo

    x, h = sweep(u, u_halo, 2)
    x, h = sweep(x, h, 1)
    res = []
    for c in range(cases):
        r = around(x, h, c) - diag * x[c]
        res.append(r if f is None else f[c] + r)
    return x, res


def total(x):
    rows, width = x.shape
    part = x[:, 0:128]
    for k in range(1, width // 128):
        part = part + x[:, k * 128 : (k + 1) * 128]
    return jnp.sum(jnp.sum(part, axis=1, keepdims=True), axis=0, keepdims=True)


def lane_row(values):
    lane = lax.broadcasted_iota(jnp.int32, (1, 128), 1)
    row = jnp.zeros((1, 128), F32)
    for k, v in values:
        row = jnp.where(lane == k, v, row)
    return row


def pre_kernel(u, f, ext, before, after, row_at, row_ok, same_col, h, y3, smooth, b, x0, first, last, rsum):
    cases, rows, width = u.shape
    diag = 4.0 + ext[...]
    us = [u[c] for c in range(cases)]
    fl = [f[c] for c in range(cases)]
    u_halo = [both(before, after, k) for k in range(3)]
    f_halo = [both(before, after, 3 + k) for k in range(2)]
    d_halo = [4.0 + both(before, after, 5 + k) for k in range(2)]
    valid = both(before, after, 7)
    x, res = two_sweeps(us, u_halo, fl, f_halo, diag, d_halo, valid)
    for c in range(cases):
        smooth[c] = x[c]
    sums = seg_sum(res, (row_at, row_ok, same_col))
    for c in range(cases):
        b[c] = sums[c]
        v = h[...] * sums[c]
        x0[c] = v
        first[pl.ds(c, 1), :] = v[0:1]
        last[pl.ds(c, 1), :] = v[rows - 1 : rows]
    for j in range(3):
        y = y3[j]
        first[pl.ds(cases + j, 1), :] = y[0:1]
        last[pl.ds(cases + j, 1), :] = y[rows - 1 : rows]
    for out in (first, last):
        out[pl.ds(cases + 3, 1), :] = jnp.zeros((1, width), F32)
    rsum[...] = lane_row([(c, total(res[c])) for c in range(cases)])


def coarse_step(x, above, below, ext, b, h, tables):
    cases = len(x)
    diag = 4.0 + ext[...]
    w = [diag * x[c] - neighbours(x[c], above[c], below[c]) for c in range(cases)]
    sums = seg_sum(w, tables)
    return [x[c] + h[...] * (b[c] - sums[c]) for c in range(cases)]


def store_edges(x, first, last):
    rows = x[0].shape[0]
    for c in range(len(x)):
        first[pl.ds(c, 1), :] = x[c][0:1]
        last[pl.ds(c, 1), :] = x[c][rows - 1 : rows]


def coarse_kernel_a(x0, ext, b, row_at, row_ok, same_col, h, y3, rsum, before, after, x1, y4, first, last, part):
    cases, rows, width = x0.shape
    tables = (row_at, row_ok, same_col)
    none = jnp.zeros((rows, width), F32)
    no_row = jnp.zeros((1, width), F32)
    old = [x0[c] for c in range(cases)] + [none] + [y3[j] for j in range(3)] + [none]
    above = [before[pl.ds(c, 1), :] for c in range(cases + 3)] + [no_row, no_row]
    below = [after[pl.ds(c, 1), :] for c in range(cases)] + [no_row, no_row]
    below = below + [after[pl.ds(cases + j, 1), :] for j in range(3)]
    rhs = [b[c] for c in range(cases)] + [none] * 5
    x = coarse_step(old, above, below, ext, rhs, h, tables)
    no_rows = jnp.zeros((8, width), F32)
    for out in (first, last):
        for k in range(4):
            out[k] = no_rows
    for c in range(cases):
        first[0, pl.ds(c, 1), :] = x[c][0:1]
        last[0, pl.ds(c, 1), :] = x[c][rows - 1 : rows]
    for j in range(5):
        y = x[cases + j]
        y4[j] = y
        for k in range(3):
            first[1 + k, pl.ds(j, 1), :] = y[k : k + 1]
            last[1 + k, pl.ds(j, 1), :] = y[rows - 1 - k : rows - k]
    weight = open_weight(ext[...])
    values = []
    for c in range(cases):
        x1[c] = x[c]
        own = rsum[:, c : c + 1] - total(weight * x[c])
        values.append((c, own))
        values.append((cases + c, total(x[c][0:1])))
        values.append((2 * cases + c, total(x[c][rows - 1 : rows])))
    values.append((3 * cases, total(ext[...])))
    part[...] = lane_row(values)


REACH_E = 3
ORDER = [0, -1, 1, -2, 2, -3, 3]
LANE_PERP, LANE_LOAD, LANE_D, LANE_C, LANE_L = 16, 20, 24, 32, 64


def dot(x, y):
    return total(x * y)


def response_kernel(ext, before, after, y4, ab, be, phi, q, part):
    rows, width = ext.shape
    m = 2 * REACH_E + 1
    diag = 4.0 + ext[...]
    none = jnp.zeros((rows, width), F32)
    fields = [none] + [y4[j] for j in range(5)] + [none]
    two_rows = jnp.zeros((2, width), F32)
    halo = []
    for k in range(3):
        up, down = ab[1 + k], be[1 + k]
        halo.append(jnp.concatenate([up[0:5], two_rows, two_rows, down[0:5]], axis=0))

    def spread(k):
        up = jnp.broadcast_to(before[k][0:1], (m, width))
        down = jnp.broadcast_to(after[k][0:1], (m, width))
        return jnp.concatenate([up, down], axis=0)

    d_halo = [4.0 + spread(5 + k) for k in range(2)]
    x, res = two_sweeps(fields, halo, None, None, diag, d_halo, spread(7))
    for j in range(m):
        phi[j] = x[j]
    every = res[0]
    for j in range(1, m):
        every = every + res[j]
    basis = [every] + [res[REACH_E + j] for j in ORDER[1:]]
    values = []
    for j in range(m):
        v = basis[j]
        q[j] = v
        d = dot(v, v)
        inv = jnp.where(d > 0.0, 1.0 / jnp.where(d > 0.0, d, 1.0), 0.0)
        values.append((LANE_D + j, d))
        for k in range(j + 1, m):
            factor = dot(v, basis[k]) * inv
            values.append((LANE_L + m * j + k, factor))
            basis[k] = basis[k] - factor * v
    part[...] = lane_row(values)


def solve_slabs(g, cases, groups, cells):
    n = g.shape[0]
    row, lane = iotas(g.shape)
    top = pltpu.roll(pltpu.roll(g, 128 - cases, 1), n - 1, 0)
    bottom = pltpu.roll(pltpu.roll(g, 128 - 2 * cases, 1), 1, 0)
    b = g + jnp.where(row == n - 1, 0.0, top) + jnp.where(row == 0, 0.0, bottom)
    b = jnp.where(lane < cases, b / (groups * float(n)), 0.0)
    mean = jnp.broadcast_to(g[:, 3 * cases : 3 * cases + 1], g.shape) / float(cells)
    d = 2.0 + mean / (float(n) * float(n))
    lower = jnp.where(row == 0, 0.0, 1.0)
    upper = jnp.where(row == n - 1, 0.0, 1.0)
    excess = (d - lower) - upper
    s = 1
    while s < n:
        inv = 1.0 / (lower + upper + excess)
        alpha = lower * pltpu.roll(inv, s, 0)
        gamma = upper * pltpu.roll(inv, n - s, 0)
        b = b + alpha * pltpu.roll(b, s, 0) + gamma * pltpu.roll(b, n - s, 0)
        excess = excess + alpha * pltpu.roll(excess, s, 0) + gamma * pltpu.roll(excess, n - s, 0)
        lower = alpha * pltpu.roll(lower, s, 0)
        upper = gamma * pltpu.roll(upper, n - s, 0)
        s *= 2
    return b / (lower + upper + excess)


def coarse_kernel_b(x1, ext, b, row_at, row_ok, same_col, h, ab, be, x3, first, last):
    cases = x1.shape[0]
    x = coarse_step(
        [x1[c] for c in range(cases)],
        [ab[0, pl.ds(c, 1), :] for c in range(cases)],
        [be[0, pl.ds(c, 1), :] for c in range(cases)],
        ext, b, h, (row_at, row_ok, same_col),
    )
    store_edges(x, first, last)
    for c in range(cases):
        x3[c] = x[c]


def coarse_kernel_c(x3, ext, b, row_at, row_ok, same_col, h, smooth, before, after, v, first, last):
    cases, rows, width = x3.shape
    x = coarse_step(
        [x3[c] for c in range(cases)],
        [before[pl.ds(c, 1), :] for c in range(cases)],
        [after[pl.ds(c, 1), :] for c in range(cases)],
        ext, b, h, (row_at, row_ok, same_col),
    )
    for c in range(cases):
        y = smooth[c] + x[c]
        v[c] = y
        for k in range(3):
            first[k, pl.ds(c, 1), :] = y[k : k + 1]
            last[k, pl.ds(c, 1), :] = y[rows - 1 - k : rows - k]


def post_kernel(v, f, ext, before, after, before_v, after_v, q, part_a, part_e, out, gather):
    cases, rows, width = v.shape
    m = q.shape[0]
    diag = 4.0 + ext[...]
    fl = [f[c] for c in range(cases)]
    v_halo = [both(before_v, after_v, k) for k in range(3)]
    f_halo = [both(before, after, 3 + k) for k in range(2)]
    d_halo = [4.0 + both(before, after, 5 + k) for k in range(2)]
    valid = both(before, after, 7)
    x, res = two_sweeps([v[c] for c in range(cases)], v_halo, fl, f_halo, diag, d_halo, valid)
    for c in range(cases):
        out[c] = x[c]
    inv = []
    for j in range(m):
        d = part_e[:, LANE_D + j : LANE_D + j + 1]
        inv.append(jnp.where(d > 0.0, 1.0 / jnp.where(d > 0.0, d, 1.0), 0.0))
    values = []
    for c in range(cases):
        r = res[c]
        share = None
        for _ in range(2):
            step = [dot(r, q[j]) * inv[j] for j in range(m)]
            for j in range(m):
                r = r - step[j] * q[j]
            share = step if share is None else [p + t for p, t in zip(share, step)]
        values.append((LANE_PERP + c, dot(r, r)))
        values.append((LANE_LOAD + c, dot(fl[c], fl[c])))
        for j in range(m):
            values.append((LANE_C + cases * j + c, share[j]))
    row = part_a[...] + part_e[...] + lane_row(values)
    gather[...] = jnp.broadcast_to(row, gather.shape)


def final_kernel(groups, at, base, phi, gathered, out, ratio, e_ref):
    cases, rows, width = base.shape
    n = gathered.shape[0]
    m = phi.shape[0]
    i = at[0]
    g = gathered[...]
    row, lane = iotas(g.shape)
    e = solve_slabs(g, cases, groups, rows * width)
    margin = 8
    e_ref[pl.ds(0, margin), :] = jnp.zeros((margin, 128), F32)
    e_ref[pl.ds(margin, n), :] = e
    e_ref[pl.ds(margin + n, margin), :] = jnp.zeros((margin, 128), F32)
    near = [e_ref[pl.ds(i + margin + j, 1), :] for j in range(-REACH_E, REACH_E + 1)]
    for c in range(cases):
        x = base[c]
        for j in range(m):
            x = x + near[j][:, c : c + 1] * phi[j]
        out[c] = x

    def lanes(k):
        return pltpu.roll(g, 128 - k, 1)

    def column(k):
        return jnp.broadcast_to(g[:, k : k + 1], g.shape)

    t = [e] + [e_ref[pl.ds(margin + j, n), :] - e for j in ORDER[1:]]
    norm = lanes(LANE_PERP)
    for j in range(m):
        z = lanes(LANE_C + cases * j) + t[j]
        for k in range(j + 1, m):
            z = z + column(LANE_L + m * j + k) * t[k]
        norm = norm + column(LANE_D + j) * (z * z)
    norm = jnp.sum(norm, axis=0, keepdims=True)
    load = jnp.sum(lanes(LANE_LOAD), axis=0, keepdims=True)
    first = lax.broadcasted_iota(jnp.int32, norm.shape, 1) < cases
    r = jnp.sqrt(jnp.where(first, norm, 0.0) / jnp.where(first, load, 1.0))
    ratio[...] = jnp.broadcast_to(r, ratio.shape)


def local(thermal_solution, heat_forcing, extinction_factor, cluster_label):
    cases, rows, width = thermal_solution.shape
    n = lax.axis_size("blk")
    n_rhs = lax.axis_size("rhs")
    groups = rows * width // 16
    field = (cases, rows, width)
    up = [(i, i + 1) for i in range(n - 1)]
    down = [(j, i) for i, j in up]

    def exchange(first, last):
        return lax.ppermute(last, "blk", up), lax.ppermute(first, "blk", down)

    def to_all(x, axis):
        return lax.all_to_all(x, axis, 0, 0, tiled=True)

    edge = (cases, width)
    edges = (8, width)
    deep = (4, 8, width)
    u, f, ext, lab = thermal_solution, heat_forcing, extinction_factor, cluster_label
    at = lax.axis_index("blk").astype(jnp.int32).reshape(1)
    first, last = vmem_call(pack_kernel, [(8, cases, width)] * 2, n_in=3)(u, f, ext)
    before, after = exchange(first, last)
    shifts = len(offsets())
    cells = (rows, width)
    *tables, y3 = vmem_call(
        functools.partial(table_kernel, n),
        [
            ((shifts, rows, width), jnp.int32),
            (shifts, rows, width),
            (rows - 1, rows, width),
            cells,
            (3, rows, width),
        ],
        smem_args=(0,),
        n_in=3,
    )(at, ext, lab)
    smooth, b, x0, first, last, rsum = vmem_call(
        pre_kernel, [field, field, field, edges, edges, (1, 128)], n_in=10
    )(u, f, ext, before, after, *tables, y3)
    ab, be = exchange(first, last)
    x1, y4, first, last, part_a = vmem_call(
        coarse_kernel_a, [field, (5, rows, width), deep, deep, (1, 128)], n_in=11
    )(x0, ext, b, *tables, y3, rsum, ab, be)
    ab, be = exchange(first, last)
    m = 2 * REACH_E + 1
    phi, q, part_e = vmem_call(
        response_kernel, [(m, rows, width), (m, rows, width), (1, 128)], n_in=6
    )(ext, before, after, y4, ab, be)
    x3, first, last = vmem_call(coarse_kernel_b, [field, edge, edge], n_in=9)(
        x1, ext, b, *tables, ab, be
    )
    ab, be = exchange(first, last)
    v, first, last = vmem_call(
        coarse_kernel_c, [field, (3, cases, width), (3, cases, width)], n_in=10
    )(x3, ext, b, *tables, smooth, ab, be)
    ab, be = exchange(first, last)
    base, mine = vmem_call(post_kernel, [field, (n, 128)], n_in=10)(
        v, f, ext, before, after, ab, be, q, part_a, part_e
    )
    gathered = to_all(mine, "blk")
    corrected, ratio = vmem_call(
        functools.partial(final_kernel, groups),
        [field, (n_rhs, 128)],
        [pltpu.VMEM((n + 16, 128), F32)],
        smem_args=(0,),
        n_in=4,
    )(at, base, phi, gathered)
    every = to_all(ratio, "rhs")
    return corrected, every[:, :cases].reshape(n_rhs * cases)


def solution(mesh):
    in_specs = (P("rhs", "blk", None), P("rhs", "blk", None), P("blk", None), P("blk", None))
    out_specs = (P("rhs", "blk", None), P())
    return jax.shard_map(local, mesh=mesh, in_specs=in_specs, out_specs=out_specs, check_vma=False)
```

```python
import functools

import jax
import jax.numpy as jnp
from jax import lax
from jax.experimental import pallas as pl
from jax.experimental.pallas import tpu as pltpu
from jax.sharding import PartitionSpec as P

damping_fine = 0.8
damping_coarse = 0.5
REACH = 7
F32 = jnp.float32


def vmem_call(body, outs, scratch=(), smem_args=(), n_in=0):
    in_specs = [
        pl.BlockSpec(memory_space=pltpu.SMEM if k in smem_args else pltpu.VMEM)
        for k in range(n_in)
    ]
    return pl.pallas_call(
        body,
        out_shape=[
            jax.ShapeDtypeStruct(*(s if isinstance(s[0], tuple) else (s, F32))) for s in outs
        ],
        in_specs=in_specs,
        out_specs=[pl.BlockSpec(memory_space=pltpu.VMEM)] * len(outs),
        scratch_shapes=list(scratch),
        compiler_params=pltpu.CompilerParams(vmem_limit_bytes=48 << 20),
    )


class View:
    def __init__(self, own_chip, cross, chip):
        self.own_chip = own_chip
        self.chip, self.cross = chip, cross

    def __getitem__(self, k):
        return jnp.where(self.own_chip, self.chip[k], self.cross[k])


def sides(me, cross, chip):
    odd = (me[0] & 1) == 1
    return View(odd, cross, chip), View(jnp.logical_not(odd), cross, chip)


def row_of(c):
    return (pl.ds(c, 1), slice(None))


def sender(me, cross, chip):
    odd = (me[0] & 1) == 1

    def put(k, first, last):
        chip[k] = jnp.where(odd, first, last)
        cross[k] = jnp.where(odd, last, first)

    return put


def iotas(shape):
    return (
        lax.broadcasted_iota(jnp.int32, shape, 0),
        lax.broadcasted_iota(jnp.int32, shape, 1),
    )


def sideways(x):
    rows, width = x.shape
    col = lax.broadcasted_iota(jnp.int32, x.shape, 1)
    left = jnp.where(col == 0, 0.0, pltpu.roll(x, 1, 1))
    right = jnp.where(col == width - 1, 0.0, pltpu.roll(x, width - 1, 1))
    return left + right


def neighbours(x, above, below):
    rows = x.shape[0]
    row = lax.broadcasted_iota(jnp.int32, x.shape, 0)
    up = jnp.where(row == 0, above, pltpu.roll(x, 1, 0))
    down = jnp.where(row == rows - 1, below, pltpu.roll(x, rows - 1, 0))
    return up + down + sideways(x)


def offsets():
    return [d for d in range(-REACH, REACH + 1) if d]


def seg_sum(fields, tables):
    row_at, row_ok, same_col = tables
    rows, width = fields[0].shape
    col = list(fields)
    for k in range(1, rows):
        m = same_col[k - 1]
        col = [s + m * pltpu.roll(w, k, 0) for s, w in zip(col, fields)]
    out = list(col)
    for d, dx in enumerate(offsets()):
        at, ok = row_at[d], row_ok[d]
        out = [
            t
            + ok
            * jnp.take_along_axis(
                pltpu.roll(s, (-dx) % width, 1), at, axis=0, mode="promise_in_bounds"
            )
            for t, s in zip(out, col)
        ]
    return out


def table_kernel(n, me, ext, lab, row_at, row_ok, same_col, h, y3):
    key = lab[...]
    rows, width = key.shape
    for k in range(1, rows):
        same_col[k - 1] = jnp.where(pltpu.roll(key, k, 0) == key, 1.0, 0.0)
    for d, dx in enumerate(offsets()):
        there = pltpu.roll(key, (-dx) % width, 1)
        at = jnp.full(key.shape, -1, jnp.int32)
        for r in range(rows):
            at = jnp.where(jnp.broadcast_to(there[r : r + 1], key.shape) == key, r, at)
        row_ok[d] = jnp.where(at >= 0, 1.0, 0.0)
        row_at[d] = jnp.maximum(at, 0)
    row, col = iotas(key.shape)
    one = jnp.ones(key.shape, F32)
    zero = jnp.zeros(key.shape, F32)
    m = jnp.where((pltpu.roll(key, 1, 0) == key) & (row > 0), one, zero)
    m = m + jnp.where((pltpu.roll(key, rows - 1, 0) == key) & (row < rows - 1), one, zero)
    m = m + jnp.where((pltpu.roll(key, 1, 1) == key) & (col > 0), one, zero)
    m = m + jnp.where((pltpu.roll(key, width - 1, 1) == key) & (col < width - 1), one, zero)
    above = jnp.where(me[0] > 0, 1.0, 0.0)
    below = jnp.where(me[0] < n - 1, 1.0, 0.0)
    top = jnp.where(row == 0, one, zero)
    bottom = jnp.where(row == rows - 1, one, zero)
    open_sides = open_weight(ext[...])
    diag1, s_top, s_own, s_bottom = seg_sum(
        [4.0 + ext[...] - m, top, open_sides, bottom], (row_at, row_ok, same_col)
    )
    half = damping_coarse / diag1
    h[...] = half
    y3[0] = above * (half * s_top)
    y3[1] = 1.0 - half * s_own
    y3[2] = below * (half * s_bottom)


def open_weight(ext):
    rows, width = ext.shape
    row, col = iotas(ext.shape)
    one = jnp.ones(ext.shape, F32)
    zero = jnp.zeros(ext.shape, F32)
    weight = ext
    for at_edge in (row == 0, row == rows - 1, col == 0, col == width - 1):
        weight = weight + jnp.where(at_edge, one, zero)
    return weight


def pack_kernel(me, u_hbm, f_hbm, ext_hbm, cross, chip, u, f, ext, sem):
    copies = [
        pltpu.make_async_copy(src, dst, sem.at[k])
        for k, (src, dst) in enumerate(((u_hbm, u), (f_hbm, f), (ext_hbm, ext)))
    ]
    for copy in copies:
        copy.start()
    for copy in copies:
        copy.wait()
    cases, rows, width = u.shape
    put = sender(me, cross, chip)
    ones = jnp.ones((cases, width), F32)
    end = rows - 1
    for k in range(3):
        put(k, u[:, k, :], u[:, end - k, :])
    for k in range(2):
        put(3 + k, f[:, k, :], f[:, end - k, :])
        put(
            5 + k,
            jnp.broadcast_to(ext[pl.ds(k, 1), :], (cases, width)),
            jnp.broadcast_to(ext[pl.ds(end - k, 1), :], (cases, width)),
        )
    put(7, ones, ones)


def both(before, after, k):
    return jnp.concatenate([before[k], after[k]], axis=0)


def two_sweeps(u, u_halo, f, f_halo, diag, diag_halo, valid):
    cases = len(u)
    rows = u[0].shape[0]
    gain = damping_fine / diag
    gain_halo = [damping_fine / d for d in diag_halo]
    keep = 1.0 - damping_fine

    def edge(x):
        return jnp.concatenate([v[0:1] for v in x] + [v[rows - 1 : rows] for v in x], axis=0)

    def around(x, halo, c):
        return neighbours(x[c], halo[0][c : c + 1], halo[0][cases + c : cases + c + 1])

    def sweep(x, halo, depth):
        new = []
        for c in range(cases):
            push = around(x, halo, c)
            new.append(keep * x[c] + gain * (push if f is None else f[c] + push))
        inner = [edge(x)] + halo
        new_halo = []
        for k in range(depth):
            push = inner[k] + inner[k + 2] + sideways(halo[k])
            push = push if f is None else f_halo[k] + push
            new_halo.append((keep * halo[k] + gain_halo[k] * push) * valid)
        return new, new_halo

    x, h = sweep(u, u_halo, 2)
    x, h = sweep(x, h, 1)
    res = []
    for c in range(cases):
        r = around(x, h, c) - diag * x[c]
        res.append(r if f is None else f[c] + r)
    return x, res


def total(x):
    rows, width = x.shape
    part = x[:, 0:128]
    for k in range(1, width // 128):
        part = part + x[:, k * 128 : (k + 1) * 128]
    return jnp.sum(jnp.sum(part, axis=1, keepdims=True), axis=0, keepdims=True)


def lane_row(values):
    lane = lax.broadcasted_iota(jnp.int32, (1, 128), 1)
    row = jnp.zeros((1, 128), F32)
    for k, v in values:
        row = jnp.where(lane == k, v, row)
    return row


def pre_kernel(me, u, f, ext, cross, chip, row_at, row_ok, same_col, h, y3, smooth, b, x0, to_cross, to_chip, rsum):
    before, after = sides(me, cross, chip)
    put = sender(me, to_cross, to_chip)
    cases, rows, width = u.shape
    diag = 4.0 + ext[...]
    us = [u[c] for c in range(cases)]
    fl = [f[c] for c in range(cases)]
    u_halo = [both(before, after, k) for k in range(3)]
    f_halo = [both(before, after, 3 + k) for k in range(2)]
    d_halo = [4.0 + both(before, after, 5 + k) for k in range(2)]
    valid = both(before, after, 7)
    x, res = two_sweeps(us, u_halo, fl, f_halo, diag, d_halo, valid)
    for c in range(cases):
        smooth[c] = x[c]
    sums = seg_sum(res, (row_at, row_ok, same_col))
    for c in range(cases):
        b[c] = sums[c]
        v = h[...] * sums[c]
        x0[c] = v
        put(row_of(c), v[0:1], v[rows - 1 : rows])
    for j in range(3):
        y = y3[j]
        put(row_of(cases + j), y[0:1], y[rows - 1 : rows])
    put(row_of(cases + 3), jnp.zeros((1, width), F32), jnp.zeros((1, width), F32))
    rsum[...] = lane_row([(c, total(res[c])) for c in range(cases)])


def coarse_step(x, above, below, ext, b, h, tables):
    cases = len(x)
    diag = 4.0 + ext[...]
    w = [diag * x[c] - neighbours(x[c], above[c], below[c]) for c in range(cases)]
    sums = seg_sum(w, tables)
    return [x[c] + h[...] * (b[c] - sums[c]) for c in range(cases)]


def coarse_kernel_a(me, x0, ext, b, row_at, row_ok, same_col, h, y3, rsum, cross, chip, x1, y4, to_cross, to_chip, part):
    before, after = sides(me, cross, chip)
    put = sender(me, to_cross, to_chip)
    cases, rows, width = x0.shape
    tables = (row_at, row_ok, same_col)
    none = jnp.zeros((rows, width), F32)
    no_row = jnp.zeros((1, width), F32)
    old = [x0[c] for c in range(cases)] + [none] + [y3[j] for j in range(3)] + [none]
    above = [before[pl.ds(c, 1), :] for c in range(cases + 3)] + [no_row, no_row]
    below = [after[pl.ds(c, 1), :] for c in range(cases)] + [no_row, no_row]
    below = below + [after[pl.ds(cases + j, 1), :] for j in range(3)]
    rhs = [b[c] for c in range(cases)] + [none] * 5
    x = coarse_step(old, above, below, ext, rhs, h, tables)
    no_rows = jnp.zeros((8, width), F32)
    for k in range(4):
        put(k, no_rows, no_rows)
    for c in range(cases):
        put((0,) + row_of(c), x[c][0:1], x[c][rows - 1 : rows])
    for j in range(5):
        y = x[cases + j]
        y4[j] = y
        for k in range(3):
            put((1 + k,) + row_of(j), y[k : k + 1], y[rows - 1 - k : rows - k])
    weight = open_weight(ext[...])
    values = []
    for c in range(cases):
        x1[c] = x[c]
        own = rsum[:, c : c + 1] - total(weight * x[c])
        values.append((c, own))
        values.append((cases + c, total(x[c][0:1])))
        values.append((2 * cases + c, total(x[c][rows - 1 : rows])))
    values.append((3 * cases, total(ext[...])))
    part[...] = lane_row(values)


REACH_E = 3
ORDER = [0, -1, 1, -2, 2, -3, 3]
LANE_PERP, LANE_LOAD, LANE_D, LANE_C, LANE_L = 16, 20, 24, 32, 64


def dot(x, y):
    return total(x * y)


def response_kernel(me, ext, cross, chip, y4, cross_y, chip_y, phi, q, part):
    before, after = sides(me, cross, chip)
    ab, be = sides(me, cross_y, chip_y)
    rows, width = ext.shape
    m = 2 * REACH_E + 1
    diag = 4.0 + ext[...]
    none = jnp.zeros((rows, width), F32)
    fields = [none] + [y4[j] for j in range(5)] + [none]
    two_rows = jnp.zeros((2, width), F32)
    halo = []
    for k in range(3):
        up, down = ab[1 + k], be[1 + k]
        halo.append(jnp.concatenate([up[0:5], two_rows, two_rows, down[0:5]], axis=0))

    def spread(k):
        up = jnp.broadcast_to(before[k][0:1], (m, width))
        down = jnp.broadcast_to(after[k][0:1], (m, width))
        return jnp.concatenate([up, down], axis=0)

    d_halo = [4.0 + spread(5 + k) for k in range(2)]
    x, res = two_sweeps(fields, halo, None, None, diag, d_halo, spread(7))
    for j in range(m):
        phi[j] = x[j]
    every = res[0]
    for j in range(1, m):
        every = every + res[j]
    basis = [every] + [res[REACH_E + j] for j in ORDER[1:]]
    values = []
    for j in range(m):
        v = basis[j]
        q[j] = v
        d = dot(v, v)
        inv = jnp.where(d > 0.0, 1.0 / jnp.where(d > 0.0, d, 1.0), 0.0)
        values.append((LANE_D + j, d))
        for k in range(j + 1, m):
            factor = dot(v, basis[k]) * inv
            values.append((LANE_L + m * j + k, factor))
            basis[k] = basis[k] - factor * v
    part[...] = lane_row(values)


def solve_slabs(g, cases, groups, cells):
    n = g.shape[0]
    row, lane = iotas(g.shape)
    top = pltpu.roll(pltpu.roll(g, 128 - cases, 1), n - 1, 0)
    bottom = pltpu.roll(pltpu.roll(g, 128 - 2 * cases, 1), 1, 0)
    b = g + jnp.where(row == n - 1, 0.0, top) + jnp.where(row == 0, 0.0, bottom)
    b = jnp.where(lane < cases, b / (groups * float(n)), 0.0)
    mean = jnp.broadcast_to(g[:, 3 * cases : 3 * cases + 1], g.shape) / float(cells)
    d = 2.0 + mean / (float(n) * float(n))
    lower = jnp.where(row == 0, 0.0, 1.0)
    upper = jnp.where(row == n - 1, 0.0, 1.0)
    excess = (d - lower) - upper
    s = 1
    while s < n:
        inv = 1.0 / (lower + upper + excess)
        alpha = lower * pltpu.roll(inv, s, 0)
        gamma = upper * pltpu.roll(inv, n - s, 0)
        b = b + alpha * pltpu.roll(b, s, 0) + gamma * pltpu.roll(b, n - s, 0)
        excess = excess + alpha * pltpu.roll(excess, s, 0) + gamma * pltpu.roll(excess, n - s, 0)
        lower = alpha * pltpu.roll(lower, s, 0)
        upper = gamma * pltpu.roll(upper, n - s, 0)
        s *= 2
    return b / (lower + upper + excess)


def coarse_kernel_b(me, x1, ext, b, row_at, row_ok, same_col, h, cross, chip, x3, to_cross, to_chip):
    ab, be = sides(me, cross, chip)
    put = sender(me, to_cross, to_chip)
    cases, rows, _ = x1.shape
    x = coarse_step(
        [x1[c] for c in range(cases)],
        [ab[(0,) + row_of(c)] for c in range(cases)],
        [be[(0,) + row_of(c)] for c in range(cases)],
        ext, b, h, (row_at, row_ok, same_col),
    )
    for c in range(cases):
        x3[c] = x[c]
        put(row_of(c), x[c][0:1], x[c][rows - 1 : rows])


def coarse_kernel_c(me, x3, ext, b, row_at, row_ok, same_col, h, smooth, cross, chip, v, to_cross, to_chip):
    before, after = sides(me, cross, chip)
    put = sender(me, to_cross, to_chip)
    cases, rows, width = x3.shape
    x = coarse_step(
        [x3[c] for c in range(cases)],
        [before[pl.ds(c, 1), :] for c in range(cases)],
        [after[pl.ds(c, 1), :] for c in range(cases)],
        ext, b, h, (row_at, row_ok, same_col),
    )
    for c in range(cases):
        y = smooth[c] + x[c]
        v[c] = y
        for k in range(3):
            put((k,) + row_of(c), y[k : k + 1], y[rows - 1 - k : rows - k])


def post_kernel(me, v, f, ext, cross, chip, cross_v, chip_v, q, part_a, part_e, out, gather):
    before, after = sides(me, cross, chip)
    before_v, after_v = sides(me, cross_v, chip_v)
    cases, rows, width = v.shape
    m = q.shape[0]
    diag = 4.0 + ext[...]
    fl = [f[c] for c in range(cases)]
    v_halo = [both(before_v, after_v, k) for k in range(3)]
    f_halo = [both(before, after, 3 + k) for k in range(2)]
    d_halo = [4.0 + both(before, after, 5 + k) for k in range(2)]
    valid = both(before, after, 7)
    x, res = two_sweeps([v[c] for c in range(cases)], v_halo, fl, f_halo, diag, d_halo, valid)
    for c in range(cases):
        out[c] = x[c]
    inv = []
    for j in range(m):
        d = part_e[:, LANE_D + j : LANE_D + j + 1]
        inv.append(jnp.where(d > 0.0, 1.0 / jnp.where(d > 0.0, d, 1.0), 0.0))
    values = []
    for c in range(cases):
        r = res[c]
        share = None
        for _ in range(2):
            step = [dot(r, q[j]) * inv[j] for j in range(m)]
            for j in range(m):
                r = r - step[j] * q[j]
            share = step if share is None else [p + t for p, t in zip(share, step)]
        values.append((LANE_PERP + c, dot(r, r)))
        values.append((LANE_LOAD + c, dot(fl[c], fl[c])))
        for j in range(m):
            values.append((LANE_C + cases * j + c, share[j]))
    row = part_a[...] + part_e[...] + lane_row(values)
    gather[...] = jnp.broadcast_to(row, gather.shape)


def final_kernel(groups, me, base, phi, gathered, out, ratio, e_ref):
    cases, rows, width = base.shape
    n = gathered.shape[0]
    m = phi.shape[0]
    i = me[0]
    g = gathered[...]
    row, lane = iotas(g.shape)
    e = solve_slabs(g, cases, groups, rows * width)
    margin = 8
    e_ref[pl.ds(0, margin), :] = jnp.zeros((margin, 128), F32)
    e_ref[pl.ds(margin, n), :] = e
    e_ref[pl.ds(margin + n, margin), :] = jnp.zeros((margin, 128), F32)
    near = [e_ref[pl.ds(i + margin + j, 1), :] for j in range(-REACH_E, REACH_E + 1)]
    for c in range(cases):
        x = base[c]
        for j in range(m):
            x = x + near[j][:, c : c + 1] * phi[j]
        out[c] = x

    def lanes(k):
        return pltpu.roll(g, 128 - k, 1)

    def column(k):
        return jnp.broadcast_to(g[:, k : k + 1], g.shape)

    t = [e] + [e_ref[pl.ds(margin + j, n), :] - e for j in ORDER[1:]]
    norm = lanes(LANE_PERP)
    for j in range(m):
        z = lanes(LANE_C + cases * j) + t[j]
        for k in range(j + 1, m):
            z = z + column(LANE_L + m * j + k) * t[k]
        norm = norm + column(LANE_D + j) * (z * z)
    norm = jnp.sum(norm, axis=0, keepdims=True)
    load = jnp.sum(lanes(LANE_LOAD), axis=0, keepdims=True)
    first = lax.broadcasted_iota(jnp.int32, norm.shape, 1) < cases
    r = jnp.sqrt(jnp.where(first, norm, 0.0) / jnp.where(first, load, 1.0))
    mine = pltpu.roll(jnp.where(first, r, 0.0), me[1] * cases, 1)
    ratio[...] = mine[:, : ratio.shape[1]]


def local(thermal_solution, heat_forcing, extinction_factor, cluster_label):
    cases, rows, width = thermal_solution.shape
    n = lax.axis_size("blk")
    n_rhs = lax.axis_size("rhs")
    groups = rows * width // 16
    field = (cases, rows, width)
    pairs = [(i, i + 1) for i in range(1, n - 1, 2)]
    cross_chip = pairs + [(j, i) for i, j in pairs]
    on_chip = [(i, i ^ 1) for i in range(n)]

    def exchange(cross, chip):
        cross = lax.ppermute(cross, "blk", cross_chip)
        return cross, lax.ppermute(chip, "blk", on_chip)

    edge = (cases, width)
    edges = (8, width)
    deep = (4, 8, width)
    u, f, ext, lab = thermal_solution, heat_forcing, extinction_factor, cluster_label
    me = jnp.stack([lax.axis_index("blk"), lax.axis_index("rhs")]).astype(jnp.int32)
    cells = (rows, width)
    hbm = pl.BlockSpec(memory_space=pl.ANY)
    sent = pl.pallas_call(
        pack_kernel,
        out_shape=[jax.ShapeDtypeStruct((8, cases, width), F32)] * 2,
        in_specs=[pl.BlockSpec(memory_space=pltpu.SMEM), hbm, hbm, hbm],
        out_specs=[pl.BlockSpec(memory_space=pltpu.VMEM)] * 2,
        scratch_shapes=[
            pltpu.VMEM(field, F32),
            pltpu.VMEM(field, F32),
            pltpu.VMEM(cells, F32),
            pltpu.SemaphoreType.DMA((3,)),
        ],
    )(me, u, f, ext)
    halo = exchange(*sent)
    shifts = len(offsets())
    *tables, y3 = vmem_call(
        functools.partial(table_kernel, n),
        [
            ((shifts, rows, width), jnp.int32),
            (shifts, rows, width),
            (rows - 1, rows, width),
            cells,
            (3, rows, width),
        ],
        smem_args=(0,),
        n_in=3,
    )(me, ext, lab)
    call = functools.partial(vmem_call, smem_args=(0,))
    smooth, b, x0, *sent, rsum = call(
        pre_kernel, [field, field, field, edges, edges, (1, 128)], n_in=11
    )(me, u, f, ext, *halo, *tables, y3)
    rows_x = exchange(*sent)
    x1, y4, *sent, part_a = call(
        coarse_kernel_a, [field, (5, rows, width), deep, deep, (1, 128)], n_in=12
    )(me, x0, ext, b, *tables, y3, rsum, *rows_x)
    rows_x = exchange(*sent)
    m = 2 * REACH_E + 1
    phi, q, part_e = call(
        response_kernel, [(m, rows, width), (m, rows, width), (1, 128)], n_in=7
    )(me, ext, *halo, y4, *rows_x)
    x3, *sent = call(coarse_kernel_b, [field, edge, edge], n_in=10)(
        me, x1, ext, b, *tables, *rows_x
    )
    rows_x = exchange(*sent)
    v, *sent = call(
        coarse_kernel_c, [field, (3, cases, width), (3, cases, width)], n_in=11
    )(me, x3, ext, b, *tables, smooth, *rows_x)
    rows_x = exchange(*sent)
    base, mine = call(post_kernel, [field, (n, 128)], n_in=11)(
        me, v, f, ext, *halo, *rows_x, q, part_a, part_e
    )
    gathered = lax.all_to_all(mine, "blk", 0, 0, tiled=True)
    corrected, ratio = call(
        functools.partial(final_kernel, groups),
        [field, (1, n_rhs * cases)],
        [pltpu.VMEM((n + 16, 128), F32)],
        n_in=4,
    )(me, base, phi, gathered)
    return corrected, lax.psum(ratio.reshape(n_rhs * cases), "rhs")


def solution(mesh):
    in_specs = (P("rhs", "blk", None), P("rhs", "blk", None), P("blk", None), P("blk", None))
    out_specs = (P("rhs", "blk", None), P())
    return jax.shard_map(local, mesh=mesh, in_specs=in_specs, out_specs=out_specs, check_vma=False)
```

```python
import functools

import jax
import jax.numpy as jnp
from jax import lax
from jax.experimental import pallas as pl
from jax.experimental.pallas import tpu as pltpu
from jax.sharding import PartitionSpec as P

damping_fine = 0.8
damping_coarse = 0.5
REACH = 7
F32 = jnp.float32


VMEM = pl.BlockSpec(memory_space=pltpu.VMEM)


def with_place(body):
    def kernel(*refs):
        body((lax.axis_index("blk"), lax.axis_index("rhs")), *refs)

    return kernel


def vmem_call(body, outs, scratch=(), n_in=0, in_space=pltpu.VMEM):
    limit = 48 << 20 if in_space == pltpu.VMEM else None
    return pl.pallas_call(
        with_place(body),
        out_shape=[
            jax.ShapeDtypeStruct(*(s if isinstance(s[0], tuple) else (s, F32))) for s in outs
        ],
        in_specs=[pl.BlockSpec(memory_space=in_space)] * n_in,
        out_specs=[VMEM] * len(outs),
        scratch_shapes=list(scratch),
        compiler_params=pltpu.CompilerParams(vmem_limit_bytes=limit),
    )


class View:
    def __init__(self, own_chip, cross, chip):
        self.own_chip = own_chip
        self.chip, self.cross = chip, cross

    def __getitem__(self, k):
        return jnp.where(self.own_chip, self.chip[k], self.cross[k])


def sides(me, cross, chip):
    odd = (me[0] & 1) == 1
    return View(odd, cross, chip), View(jnp.logical_not(odd), cross, chip)


def row_of(c):
    return (pl.ds(c, 1), slice(None))


def sender(me, cross, chip):
    odd = (me[0] & 1) == 1

    def put(k, first, last):
        chip[k] = jnp.where(odd, first, last)
        cross[k] = jnp.where(odd, last, first)

    return put


def iotas(shape):
    return (
        lax.broadcasted_iota(jnp.int32, shape, 0),
        lax.broadcasted_iota(jnp.int32, shape, 1),
    )


def sideways(x):
    rows, width = x.shape
    col = lax.broadcasted_iota(jnp.int32, x.shape, 1)
    left = jnp.where(col == 0, 0.0, pltpu.roll(x, 1, 1))
    right = jnp.where(col == width - 1, 0.0, pltpu.roll(x, width - 1, 1))
    return left + right


def neighbours(x, above, below):
    rows = x.shape[0]
    row = lax.broadcasted_iota(jnp.int32, x.shape, 0)
    up = jnp.where(row == 0, above, pltpu.roll(x, 1, 0))
    down = jnp.where(row == rows - 1, below, pltpu.roll(x, rows - 1, 0))
    return up + down + sideways(x)


def offsets():
    return [d for d in range(-REACH, REACH + 1) if d]


def seg_sum(fields, tables):
    row_at, row_ok, same_col = tables
    rows, width = fields[0].shape
    col = list(fields)
    for k in range(1, rows):
        m = same_col[k - 1]
        col = [s + m * pltpu.roll(w, k, 0) for s, w in zip(col, fields)]
    out = list(col)
    for d, dx in enumerate(offsets()):
        at, ok = row_at[d], row_ok[d]
        out = [
            t
            + ok
            * jnp.take_along_axis(
                pltpu.roll(s, (-dx) % width, 1), at, axis=0, mode="promise_in_bounds"
            )
            for t, s in zip(out, col)
        ]
    return out


def table_kernel(n, me, ext, lab, row_at, row_ok, same_col, h, y3):
    key = lab[...]
    rows, width = key.shape
    for k in range(1, rows):
        same_col[k - 1] = jnp.where(pltpu.roll(key, k, 0) == key, 1.0, 0.0)
    for d, dx in enumerate(offsets()):
        there = pltpu.roll(key, (-dx) % width, 1)
        at = jnp.full(key.shape, -1, jnp.int32)
        for r in range(rows):
            at = jnp.where(jnp.broadcast_to(there[r : r + 1], key.shape) == key, r, at)
        row_ok[d] = jnp.where(at >= 0, 1.0, 0.0)
        row_at[d] = jnp.maximum(at, 0)
    row, col = iotas(key.shape)
    one = jnp.ones(key.shape, F32)
    zero = jnp.zeros(key.shape, F32)
    m = jnp.where((pltpu.roll(key, 1, 0) == key) & (row > 0), one, zero)
    m = m + jnp.where((pltpu.roll(key, rows - 1, 0) == key) & (row < rows - 1), one, zero)
    m = m + jnp.where((pltpu.roll(key, 1, 1) == key) & (col > 0), one, zero)
    m = m + jnp.where((pltpu.roll(key, width - 1, 1) == key) & (col < width - 1), one, zero)
    above = jnp.where(me[0] > 0, 1.0, 0.0)
    below = jnp.where(me[0] < n - 1, 1.0, 0.0)
    top = jnp.where(row == 0, one, zero)
    bottom = jnp.where(row == rows - 1, one, zero)
    open_sides = open_weight(ext[...])
    diag1, s_top, s_own, s_bottom = seg_sum(
        [4.0 + ext[...] - m, top, open_sides, bottom], (row_at, row_ok, same_col)
    )
    half = damping_coarse / diag1
    h[...] = half
    y3[0] = above * (half * s_top)
    y3[1] = 1.0 - half * s_own
    y3[2] = below * (half * s_bottom)


def open_weight(ext):
    rows, width = ext.shape
    row, col = iotas(ext.shape)
    one = jnp.ones(ext.shape, F32)
    zero = jnp.zeros(ext.shape, F32)
    weight = ext
    for at_edge in (row == 0, row == rows - 1, col == 0, col == width - 1):
        weight = weight + jnp.where(at_edge, one, zero)
    return weight


GROUP_EXT = 5


def pack_kernel(me, u_hbm, f_hbm, ext_hbm, cross, chip, u, f, ext, sem):
    pairs = ((u_hbm, u), (f_hbm, f), (ext_hbm, ext))
    copies = [pltpu.make_async_copy(src, dst, sem.at[k]) for k, (src, dst) in enumerate(pairs)]
    for copy in copies:
        copy.start()
    for copy in copies:
        copy.wait()
    cases, rows, width = u.shape
    put = sender(me, cross, chip)
    ones = jnp.ones((1, width), F32)
    end = rows - 1
    for k in range(3):
        put(k, u[:, k, :], u[:, end - k, :])
    for k in range(2):
        put(3 + k, f[:, k, :], f[:, end - k, :])
        at = (GROUP_EXT,) + row_of(k)
        put(at, ext[pl.ds(k, 1), :], ext[pl.ds(end - k, 1), :])
    for k in range(2, cases):
        put((GROUP_EXT,) + row_of(k), ones, ones)


def both(before, after, k):
    return jnp.concatenate([before[k], after[k]], axis=0)


def spread(before, after, k, times):
    at = (GROUP_EXT,) + row_of(k)
    up, down = before[at], after[at]
    shape = (times, up.shape[1])
    return jnp.concatenate([jnp.broadcast_to(up, shape), jnp.broadcast_to(down, shape)], axis=0)


def two_sweeps(u, u_halo, f, f_halo, diag, diag_halo, valid):
    cases = len(u)
    rows = u[0].shape[0]
    gain = damping_fine / diag
    gain_halo = [damping_fine / d for d in diag_halo]
    keep = 1.0 - damping_fine

    def edge(x):
        return jnp.concatenate([v[0:1] for v in x] + [v[rows - 1 : rows] for v in x], axis=0)

    def around(x, halo, c):
        return neighbours(x[c], halo[0][c : c + 1], halo[0][cases + c : cases + c + 1])

    def sweep(x, halo, depth):
        new = []
        for c in range(cases):
            push = around(x, halo, c)
            new.append(keep * x[c] + gain * (push if f is None else f[c] + push))
        inner = [edge(x)] + halo
        new_halo = []
        for k in range(depth):
            push = inner[k] + inner[k + 2] + sideways(halo[k])
            push = push if f is None else f_halo[k] + push
            new_halo.append((keep * halo[k] + gain_halo[k] * push) * valid)
        return new, new_halo

    x, h = sweep(u, u_halo, 2)
    x, h = sweep(x, h, 1)
    res = []
    for c in range(cases):
        r = around(x, h, c) - diag * x[c]
        res.append(r if f is None else f[c] + r)
    return x, res


def total(x):
    rows, width = x.shape
    part = x[:, 0:128]
    for k in range(1, width // 128):
        part = part + x[:, k * 128 : (k + 1) * 128]
    return jnp.sum(jnp.sum(part, axis=1, keepdims=True), axis=0, keepdims=True)


def lane_row(values):
    lane = lax.broadcasted_iota(jnp.int32, (1, 128), 1)
    row = jnp.zeros((1, 128), F32)
    for k, v in values:
        row = jnp.where(lane == k, v, row)
    return row


def pre_kernel(me, u, f, ext, cross, chip, row_at, row_ok, same_col, h, y3, smooth, b, x0, to_cross, to_chip, rsum):
    before, after = sides(me, cross, chip)
    put = sender(me, to_cross, to_chip)
    cases, rows, width = u.shape
    diag = 4.0 + ext[...]
    us = [u[c] for c in range(cases)]
    fl = [f[c] for c in range(cases)]
    u_halo = [both(before, after, k) for k in range(3)]
    f_halo = [both(before, after, 3 + k) for k in range(2)]
    d_halo = [4.0 + spread(before, after, k, cases) for k in range(2)]
    valid = spread(before, after, 2, cases)
    x, res = two_sweeps(us, u_halo, fl, f_halo, diag, d_halo, valid)
    for c in range(cases):
        smooth[c] = x[c]
    sums = seg_sum(res, (row_at, row_ok, same_col))
    for c in range(cases):
        b[c] = sums[c]
        v = h[...] * sums[c]
        x0[c] = v
        put(row_of(c), v[0:1], v[rows - 1 : rows])
    for j in range(3):
        y = y3[j]
        put(row_of(cases + j), y[0:1], y[rows - 1 : rows])
    put(row_of(cases + 3), jnp.zeros((1, width), F32), jnp.zeros((1, width), F32))
    rsum[...] = lane_row([(c, total(res[c])) for c in range(cases)])


def coarse_step(x, above, below, ext, b, h, tables):
    cases = len(x)
    diag = 4.0 + ext[...]
    w = [diag * x[c] - neighbours(x[c], above[c], below[c]) for c in range(cases)]
    sums = seg_sum(w, tables)
    return [x[c] + h[...] * (b[c] - sums[c]) for c in range(cases)]


def x1_row(c):
    return (c // 3,) + row_of(5 + c % 3)


def coarse_kernel_a(me, x0, ext, b, row_at, row_ok, same_col, h, y3, rsum, cross, chip, x1, y4, to_cross, to_chip, part):
    before, after = sides(me, cross, chip)
    put = sender(me, to_cross, to_chip)
    cases, rows, width = x0.shape
    tables = (row_at, row_ok, same_col)
    none = jnp.zeros((rows, width), F32)
    no_row = jnp.zeros((1, width), F32)
    old = [x0[c] for c in range(cases)] + [none] + [y3[j] for j in range(3)] + [none]
    above = [before[pl.ds(c, 1), :] for c in range(cases + 3)] + [no_row, no_row]
    below = [after[pl.ds(c, 1), :] for c in range(cases)] + [no_row, no_row]
    below = below + [after[pl.ds(cases + j, 1), :] for j in range(3)]
    rhs = [b[c] for c in range(cases)] + [none] * 5
    x = coarse_step(old, above, below, ext, rhs, h, tables)
    for c in range(cases):
        put(x1_row(c), x[c][0:1], x[c][rows - 1 : rows])
    no_row = jnp.zeros((1, width), F32)
    for c in range(cases, 9):
        put(x1_row(c), no_row, no_row)
    for j in range(5):
        y = x[cases + j]
        y4[j] = y
        for k in range(3):
            put((k,) + row_of(j), y[k : k + 1], y[rows - 1 - k : rows - k])
    weight = open_weight(ext[...])
    values = []
    for c in range(cases):
        x1[c] = x[c]
        own = rsum[:, c : c + 1] - total(weight * x[c])
        values.append((c, own))
        values.append((cases + c, total(x[c][0:1])))
        values.append((2 * cases + c, total(x[c][rows - 1 : rows])))
    values.append((3 * cases, total(ext[...])))
    part[...] = lane_row(values)


REACH_E = 3
ORDER = [0, -1, 1, -2, 2, -3, 3]
LANE_PERP, LANE_LOAD, LANE_D, LANE_C, LANE_L = 16, 20, 24, 32, 64


def dot(x, y):
    return total(x * y)


def response_kernel(me, ext, cross, chip, y4, cross_y, chip_y, phi, q, part):
    before, after = sides(me, cross, chip)
    ab, be = sides(me, cross_y, chip_y)
    rows, width = ext.shape
    m = 2 * REACH_E + 1
    diag = 4.0 + ext[...]
    none = jnp.zeros((rows, width), F32)
    fields = [none] + [y4[j] for j in range(5)] + [none]
    two_rows = jnp.zeros((2, width), F32)
    halo = []
    for k in range(3):
        up, down = ab[k], be[k]
        halo.append(jnp.concatenate([up[0:5], two_rows, two_rows, down[0:5]], axis=0))

    d_halo = [4.0 + spread(before, after, k, m) for k in range(2)]
    x, res = two_sweeps(fields, halo, None, None, diag, d_halo, spread(before, after, 2, m))
    for j in range(m):
        phi[j] = x[j]
    every = res[0]
    for j in range(1, m):
        every = every + res[j]
    basis = [every] + [res[REACH_E + j] for j in ORDER[1:]]
    values = []
    for j in range(m):
        v = basis[j]
        q[j] = v
        d = dot(v, v)
        inv = jnp.where(d > 0.0, 1.0 / jnp.where(d > 0.0, d, 1.0), 0.0)
        values.append((LANE_D + j, d))
        for k in range(j + 1, m):
            factor = dot(v, basis[k]) * inv
            values.append((LANE_L + m * j + k, factor))
            basis[k] = basis[k] - factor * v
    part[...] = lane_row(values)


def solve_slabs(g, cases, groups, cells):
    n = g.shape[0]
    row, lane = iotas(g.shape)
    top = pltpu.roll(pltpu.roll(g, 128 - cases, 1), n - 1, 0)
    bottom = pltpu.roll(pltpu.roll(g, 128 - 2 * cases, 1), 1, 0)
    b = g + jnp.where(row == n - 1, 0.0, top) + jnp.where(row == 0, 0.0, bottom)
    b = jnp.where(lane < cases, b / (groups * float(n)), 0.0)
    mean = jnp.broadcast_to(g[:, 3 * cases : 3 * cases + 1], g.shape) / float(cells)
    d = 2.0 + mean / (float(n) * float(n))
    lower = jnp.where(row == 0, 0.0, 1.0)
    upper = jnp.where(row == n - 1, 0.0, 1.0)
    excess = (d - lower) - upper
    s = 1
    while s < n:
        inv = 1.0 / (lower + upper + excess)
        alpha = lower * pltpu.roll(inv, s, 0)
        gamma = upper * pltpu.roll(inv, n - s, 0)
        b = b + alpha * pltpu.roll(b, s, 0) + gamma * pltpu.roll(b, n - s, 0)
        excess = excess + alpha * pltpu.roll(excess, s, 0) + gamma * pltpu.roll(excess, n - s, 0)
        lower = alpha * pltpu.roll(lower, s, 0)
        upper = gamma * pltpu.roll(upper, n - s, 0)
        s *= 2
    return b / (lower + upper + excess)


def coarse_kernel_b(me, x1, ext, b, row_at, row_ok, same_col, h, cross, chip, x3, to_cross, to_chip):
    ab, be = sides(me, cross, chip)
    put = sender(me, to_cross, to_chip)
    cases, rows, _ = x1.shape
    x = coarse_step(
        [x1[c] for c in range(cases)],
        [ab[x1_row(c)] for c in range(cases)],
        [be[x1_row(c)] for c in range(cases)],
        ext, b, h, (row_at, row_ok, same_col),
    )
    for c in range(cases):
        x3[c] = x[c]
        put(row_of(c), x[c][0:1], x[c][rows - 1 : rows])


def coarse_kernel_c(me, x3, ext, b, row_at, row_ok, same_col, h, smooth, cross, chip, v, to_cross, to_chip):
    before, after = sides(me, cross, chip)
    put = sender(me, to_cross, to_chip)
    cases, rows, width = x3.shape
    x = coarse_step(
        [x3[c] for c in range(cases)],
        [before[pl.ds(c, 1), :] for c in range(cases)],
        [after[pl.ds(c, 1), :] for c in range(cases)],
        ext, b, h, (row_at, row_ok, same_col),
    )
    for c in range(cases):
        y = smooth[c] + x[c]
        v[c] = y
        for k in range(3):
            put((k,) + row_of(c), y[k : k + 1], y[rows - 1 - k : rows - k])


def post_kernel(me, v, f, ext, cross, chip, cross_v, chip_v, q, part_a, part_e, out, gather):
    before, after = sides(me, cross, chip)
    before_v, after_v = sides(me, cross_v, chip_v)
    cases, rows, width = v.shape
    m = q.shape[0]
    diag = 4.0 + ext[...]
    fl = [f[c] for c in range(cases)]
    v_halo = [both(before_v, after_v, k) for k in range(3)]
    f_halo = [both(before, after, 3 + k) for k in range(2)]
    d_halo = [4.0 + spread(before, after, k, cases) for k in range(2)]
    valid = spread(before, after, 2, cases)
    x, res = two_sweeps([v[c] for c in range(cases)], v_halo, fl, f_halo, diag, d_halo, valid)
    for c in range(cases):
        out[c] = x[c]
    inv = []
    for j in range(m):
        d = part_e[:, LANE_D + j : LANE_D + j + 1]
        inv.append(jnp.where(d > 0.0, 1.0 / jnp.where(d > 0.0, d, 1.0), 0.0))
    values = []
    for c in range(cases):
        r = res[c]
        share = None
        for _ in range(2):
            step = [dot(r, q[j]) * inv[j] for j in range(m)]
            for j in range(m):
                r = r - step[j] * q[j]
            share = step if share is None else [p + t for p, t in zip(share, step)]
        values.append((LANE_PERP + c, dot(r, r)))
        values.append((LANE_LOAD + c, dot(fl[c], fl[c])))
        for j in range(m):
            values.append((LANE_C + cases * j + c, share[j]))
    row = part_a[...] + part_e[...] + lane_row(values)
    gather[...] = jnp.broadcast_to(row, gather.shape)


def final_kernel(groups, me, base, phi, gathered, out, ratio, e_ref):
    cases, rows, width = base.shape
    n = gathered.shape[0]
    m = phi.shape[0]
    i = me[0]
    g = gathered[...]
    row, lane = iotas(g.shape)
    e = solve_slabs(g, cases, groups, rows * width)
    margin = 8
    e_ref[pl.ds(0, margin), :] = jnp.zeros((margin, 128), F32)
    e_ref[pl.ds(margin, n), :] = e
    e_ref[pl.ds(margin + n, margin), :] = jnp.zeros((margin, 128), F32)
    near = [e_ref[pl.ds(i + margin + j, 1), :] for j in range(-REACH_E, REACH_E + 1)]
    for c in range(cases):
        x = base[c]
        for j in range(m):
            x = x + near[j][:, c : c + 1] * phi[j]
        out[c] = x

    def lanes(k):
        return pltpu.roll(g, 128 - k, 1)

    def column(k):
        return jnp.broadcast_to(g[:, k : k + 1], g.shape)

    t = [e] + [e_ref[pl.ds(margin + j, n), :] - e for j in ORDER[1:]]
    norm = lanes(LANE_PERP)
    for j in range(m):
        z = lanes(LANE_C + cases * j) + t[j]
        for k in range(j + 1, m):
            z = z + column(LANE_L + m * j + k) * t[k]
        norm = norm + column(LANE_D + j) * (z * z)
    norm = jnp.sum(norm, axis=0, keepdims=True)
    load = jnp.sum(lanes(LANE_LOAD), axis=0, keepdims=True)
    first = lax.broadcasted_iota(jnp.int32, norm.shape, 1) < cases
    r = jnp.sqrt(jnp.where(first, norm, 0.0) / jnp.where(first, load, 1.0))
    mine = pltpu.roll(jnp.where(first, r, 0.0), me[1] * cases, 1)
    ratio[...] = mine[:, : ratio.shape[1]]


def doubling(n):
    step, steps = 1, []
    while step < n:
        steps.append([(i, i ^ (2 * step - 1)) for i in range(n)])
        step *= 2
    return steps


def local(thermal_solution, heat_forcing, extinction_factor, cluster_label):
    cases, rows, width = thermal_solution.shape
    n = lax.axis_size("blk")
    n_rhs = lax.axis_size("rhs")
    groups = rows * width // 16
    field = (cases, rows, width)
    pairs = [(i, i + 1) for i in range(1, n - 1, 2)]
    cross_chip = pairs + [(j, i) for i, j in pairs]
    on_chip = [(i, i ^ 1) for i in range(n)]

    def exchange(cross, chip):
        cross = lax.ppermute(cross, "blk", cross_chip)
        return cross, lax.ppermute(chip, "blk", on_chip)

    edge = (cases, width)
    edges = (8, width)
    deep = (3, 8, width)
    cells = (rows, width)
    u, f, ext, lab = thermal_solution, heat_forcing, extinction_factor, cluster_label
    sent = vmem_call(
        pack_kernel,
        [(6, cases, width)] * 2,
        [
            pltpu.VMEM(field, F32),
            pltpu.VMEM(field, F32),
            pltpu.VMEM(cells, F32),
            pltpu.SemaphoreType.DMA((3,)),
        ],
        n_in=3,
        in_space=pl.ANY,
    )(u, f, ext)
    halo = exchange(*sent)
    shifts = len(offsets())
    *tables, y3 = vmem_call(
        functools.partial(table_kernel, n),
        [
            ((shifts, rows, width), jnp.int32),
            (shifts, rows, width),
            (rows - 1, rows, width),
            cells,
            (3, rows, width),
        ],
        n_in=2,
    )(ext, lab)
    call = vmem_call
    smooth, b, x0, *sent, rsum = call(
        pre_kernel, [field, field, field, edges, edges, (1, 128)], n_in=10
    )(u, f, ext, *halo, *tables, y3)
    rows_x = exchange(*sent)
    x1, y4, *sent, part_a = call(
        coarse_kernel_a, [field, (5, rows, width), deep, deep, (1, 128)], n_in=11
    )(x0, ext, b, *tables, y3, rsum, *rows_x)
    rows_x = exchange(*sent)
    m = 2 * REACH_E + 1
    phi, q, part_e = call(
        response_kernel, [(m, rows, width), (m, rows, width), (1, 128)], n_in=6
    )(ext, *halo, y4, *rows_x)
    x3, *sent = call(coarse_kernel_b, [field, edge, edge], n_in=9)(
        x1, ext, b, *tables, *rows_x
    )
    rows_x = exchange(*sent)
    v, *sent = call(
        coarse_kernel_c, [field, (3, cases, width), (3, cases, width)], n_in=10
    )(x3, ext, b, *tables, smooth, *rows_x)
    rows_x = exchange(*sent)
    base, mine = call(post_kernel, [field, (n, 128)], n_in=10)(
        v, f, ext, *halo, *rows_x, q, part_a, part_e
    )
    gathered = lax.all_to_all(mine, "blk", 0, 0, tiled=True)
    corrected, ratio = call(
        functools.partial(final_kernel, groups),
        [field, (1, n_rhs * cases)],
        [pltpu.VMEM((n + 16, 128), F32)],
        n_in=3,
    )(base, phi, gathered)
    ratio = ratio.reshape(n_rhs * cases)
    for step in doubling(n_rhs):
        ratio = ratio + lax.ppermute(ratio, "rhs", step)
    return corrected, ratio


def solution(mesh):
    in_specs = (P("rhs", "blk", None), P("rhs", "blk", None), P("blk", None), P("blk", None))
    out_specs = (P("rhs", "blk", None), P())
    return jax.shard_map(local, mesh=mesh, in_specs=in_specs, out_specs=out_specs, check_vma=False)
```

```python
import functools

import jax
import jax.numpy as jnp
from jax import lax
from jax.experimental import pallas as pl
from jax.experimental.pallas import tpu as pltpu
from jax.sharding import PartitionSpec as P

damping_fine = 0.8
damping_coarse = 0.5
REACH = 7
F32 = jnp.float32


VMEM = pl.BlockSpec(memory_space=pltpu.VMEM)


def with_place(body):
    def kernel(*refs):
        body((lax.axis_index("blk"), lax.axis_index("rhs")), *refs)

    return kernel


def vmem_call(body, outs, scratch=(), n_in=0, in_space=pltpu.VMEM):
    limit = 48 << 20 if in_space == pltpu.VMEM else None
    return pl.pallas_call(
        with_place(body),
        out_shape=[
            jax.ShapeDtypeStruct(*(s if isinstance(s[0], tuple) else (s, F32))) for s in outs
        ],
        in_specs=[pl.BlockSpec(memory_space=in_space)] * n_in,
        out_specs=[VMEM] * len(outs),
        scratch_shapes=list(scratch),
        compiler_params=pltpu.CompilerParams(vmem_limit_bytes=limit),
    )


class View:
    def __init__(self, own_chip, cross, chip):
        self.own_chip = own_chip
        self.chip, self.cross = chip, cross

    def __getitem__(self, k):
        return jnp.where(self.own_chip, self.chip[k], self.cross[k])


def sides(me, cross, chip):
    odd = (me[0] & 1) == 1
    return View(odd, cross, chip), View(jnp.logical_not(odd), cross, chip)


def row_of(c):
    return (pl.ds(c, 1), slice(None))


def sender(me, cross, chip):
    odd = (me[0] & 1) == 1

    def put(k, first, last):
        chip[k] = jnp.where(odd, first, last)
        cross[k] = jnp.where(odd, last, first)

    return put


def iotas(shape):
    return (
        lax.broadcasted_iota(jnp.int32, shape, 0),
        lax.broadcasted_iota(jnp.int32, shape, 1),
    )


def sideways(x):
    rows, width = x.shape
    col = lax.broadcasted_iota(jnp.int32, x.shape, 1)
    left = jnp.where(col == 0, 0.0, pltpu.roll(x, 1, 1))
    right = jnp.where(col == width - 1, 0.0, pltpu.roll(x, width - 1, 1))
    return left + right


def neighbours(x, above, below):
    rows = x.shape[0]
    row = lax.broadcasted_iota(jnp.int32, x.shape, 0)
    up = jnp.where(row == 0, above, pltpu.roll(x, 1, 0))
    down = jnp.where(row == rows - 1, below, pltpu.roll(x, rows - 1, 0))
    return up + down + sideways(x)


def offsets():
    return [d for d in range(-REACH, REACH + 1) if d]


def seg_sum(fields, tables):
    row_at, row_ok, same_col = tables
    rows, width = fields[0].shape
    col = list(fields)
    for k in range(1, rows):
        m = same_col[k - 1]
        col = [s + m * pltpu.roll(w, k, 0) for s, w in zip(col, fields)]
    out = list(col)
    for d, dx in enumerate(offsets()):
        at, ok = row_at[d], row_ok[d]
        out = [
            t
            + ok
            * jnp.take_along_axis(
                pltpu.roll(s, (-dx) % width, 1), at, axis=0, mode="promise_in_bounds"
            )
            for t, s in zip(out, col)
        ]
    return out


def table_kernel(n, me, ext, lab, row_at, row_ok, same_col, h, y3):
    key = lab[...]
    rows, width = key.shape
    for k in range(1, rows):
        same_col[k - 1] = jnp.where(pltpu.roll(key, k, 0) == key, 1.0, 0.0)
    for d, dx in enumerate(offsets()):
        there = pltpu.roll(key, (-dx) % width, 1)
        at = jnp.full(key.shape, -1, jnp.int32)
        for r in range(rows):
            at = jnp.where(jnp.broadcast_to(there[r : r + 1], key.shape) == key, r, at)
        row_ok[d] = jnp.where(at >= 0, 1.0, 0.0)
        row_at[d] = jnp.maximum(at, 0)
    row, col = iotas(key.shape)
    one = jnp.ones(key.shape, F32)
    zero = jnp.zeros(key.shape, F32)
    m = jnp.where((pltpu.roll(key, 1, 0) == key) & (row > 0), one, zero)
    m = m + jnp.where((pltpu.roll(key, rows - 1, 0) == key) & (row < rows - 1), one, zero)
    m = m + jnp.where((pltpu.roll(key, 1, 1) == key) & (col > 0), one, zero)
    m = m + jnp.where((pltpu.roll(key, width - 1, 1) == key) & (col < width - 1), one, zero)
    above = jnp.where(me[0] > 0, 1.0, 0.0)
    below = jnp.where(me[0] < n - 1, 1.0, 0.0)
    top = jnp.where(row == 0, one, zero)
    bottom = jnp.where(row == rows - 1, one, zero)
    open_sides = open_weight(ext[...])
    diag1, s_top, s_own, s_bottom = seg_sum(
        [4.0 + ext[...] - m, top, open_sides, bottom], (row_at, row_ok, same_col)
    )
    half = damping_coarse / diag1
    h[...] = half
    y3[0] = above * (half * s_top)
    y3[1] = 1.0 - half * s_own
    y3[2] = below * (half * s_bottom)


def open_weight(ext):
    rows, width = ext.shape
    row, col = iotas(ext.shape)
    one = jnp.ones(ext.shape, F32)
    zero = jnp.zeros(ext.shape, F32)
    weight = ext
    for at_edge in (row == 0, row == rows - 1, col == 0, col == width - 1):
        weight = weight + jnp.where(at_edge, one, zero)
    return weight


GROUP_EXT = 5


def pack_kernel(me, u_hbm, f_hbm, ext_hbm, cross, chip, u, f, ext, sem):
    pairs = ((u_hbm, u), (f_hbm, f), (ext_hbm, ext))
    copies = [pltpu.make_async_copy(src, dst, sem.at[k]) for k, (src, dst) in enumerate(pairs)]
    for copy in copies:
        copy.start()
    for copy in copies:
        copy.wait()
    cases, rows, width = u.shape
    put = sender(me, cross, chip)
    ones = jnp.ones((1, width), F32)
    end = rows - 1
    for k in range(3):
        put(k, u[:, k, :], u[:, end - k, :])
    for k in range(2):
        put(3 + k, f[:, k, :], f[:, end - k, :])
        at = (GROUP_EXT,) + row_of(k)
        put(at, ext[pl.ds(k, 1), :], ext[pl.ds(end - k, 1), :])
    for k in range(2, cases):
        put((GROUP_EXT,) + row_of(k), ones, ones)


def both(before, after, k):
    return jnp.concatenate([before[k], after[k]], axis=0)


def spread(before, after, k, times):
    at = (GROUP_EXT,) + row_of(k)
    up, down = before[at], after[at]
    shape = (times, up.shape[1])
    return jnp.concatenate([jnp.broadcast_to(up, shape), jnp.broadcast_to(down, shape)], axis=0)


def two_sweeps(u, u_halo, f, f_halo, diag, diag_halo, valid):
    cases = len(u)
    rows = u[0].shape[0]
    gain = damping_fine / diag
    gain_halo = [damping_fine / d for d in diag_halo]
    keep = 1.0 - damping_fine

    def edge(x):
        return jnp.concatenate([v[0:1] for v in x] + [v[rows - 1 : rows] for v in x], axis=0)

    def around(x, halo, c):
        return neighbours(x[c], halo[0][c : c + 1], halo[0][cases + c : cases + c + 1])

    def sweep(x, halo, depth):
        new = []
        for c in range(cases):
            push = around(x, halo, c)
            new.append(keep * x[c] + gain * (push if f is None else f[c] + push))
        inner = [edge(x)] + halo
        new_halo = []
        for k in range(depth):
            push = inner[k] + inner[k + 2] + sideways(halo[k])
            push = push if f is None else f_halo[k] + push
            new_halo.append((keep * halo[k] + gain_halo[k] * push) * valid)
        return new, new_halo

    x, h = sweep(u, u_halo, 2)
    x, h = sweep(x, h, 1)
    res = []
    for c in range(cases):
        r = around(x, h, c) - diag * x[c]
        res.append(r if f is None else f[c] + r)
    return x, res


def total(x):
    rows, width = x.shape
    part = x[:, 0:128]
    for k in range(1, width // 128):
        part = part + x[:, k * 128 : (k + 1) * 128]
    return jnp.sum(jnp.sum(part, axis=1, keepdims=True), axis=0, keepdims=True)


def lane_row(values):
    lane = lax.broadcasted_iota(jnp.int32, (1, 128), 1)
    row = jnp.zeros((1, 128), F32)
    for k, v in values:
        row = jnp.where(lane == k, v, row)
    return row


def pre_kernel(me, u, f, ext, cross, chip, row_at, row_ok, same_col, h, y3, smooth, b, x0, to_cross, to_chip, rsum):
    before, after = sides(me, cross, chip)
    put = sender(me, to_cross, to_chip)
    cases, rows, width = u.shape
    diag = 4.0 + ext[...]
    us = [u[c] for c in range(cases)]
    fl = [f[c] for c in range(cases)]
    u_halo = [both(before, after, k) for k in range(3)]
    f_halo = [both(before, after, 3 + k) for k in range(2)]
    d_halo = [4.0 + spread(before, after, k, cases) for k in range(2)]
    valid = spread(before, after, 2, cases)
    x, res = two_sweeps(us, u_halo, fl, f_halo, diag, d_halo, valid)
    for c in range(cases):
        smooth[c] = x[c]
    sums = seg_sum(res, (row_at, row_ok, same_col))
    for c in range(cases):
        b[c] = sums[c]
        v = h[...] * sums[c]
        x0[c] = v
        put(row_of(c), v[0:1], v[rows - 1 : rows])
    for j in range(3):
        y = y3[j]
        put(row_of(cases + j), y[0:1], y[rows - 1 : rows])
    put(row_of(cases + 3), jnp.zeros((1, width), F32), jnp.zeros((1, width), F32))
    rsum[...] = lane_row([(c, total(res[c])) for c in range(cases)])


def coarse_step(x, above, below, ext, b, h, tables):
    cases = len(x)
    diag = 4.0 + ext[...]
    w = [diag * x[c] - neighbours(x[c], above[c], below[c]) for c in range(cases)]
    sums = seg_sum(w, tables)
    return [x[c] + h[...] * (b[c] - sums[c]) for c in range(cases)]


def edge_row(c):
    return (c // 3,) + row_of(5 + c % 3)


def coarse_kernel_a(me, x0, ext, b, row_at, row_ok, same_col, h, rsum, cross, chip, x1, to_cross, to_chip, part):
    before, after = sides(me, cross, chip)
    put = sender(me, to_cross, to_chip)
    cases, rows, width = x0.shape
    x = coarse_step(
        [x0[c] for c in range(cases)],
        [before[row_of(c)] for c in range(cases)],
        [after[row_of(c)] for c in range(cases)],
        ext, b, h, (row_at, row_ok, same_col),
    )
    weight = open_weight(ext[...])
    values = []
    for c in range(cases):
        x1[c] = x[c]
        put(row_of(c), x[c][0:1], x[c][rows - 1 : rows])
        own = rsum[:, c : c + 1] - total(weight * x[c])
        values.append((LANE_OWN + c, own))
        values.append((LANE_TOP + c, total(x[c][0:1])))
        values.append((LANE_BOTTOM + c, total(x[c][rows - 1 : rows])))
    values.append((LANE_EXT, total(ext[...])))
    part[...] = lane_row(values)


def answer_kernel(cases, me, ext, row_at, row_ok, same_col, h, y3, cross, chip, y4):
    before, after = sides(me, cross, chip)
    rows, width = ext.shape
    none = jnp.zeros((rows, width), F32)
    no_row = jnp.zeros((1, width), F32)
    above = [before[row_of(cases + j)] for j in range(3)] + [no_row, no_row]
    below = [no_row, no_row] + [after[row_of(cases + j)] for j in range(3)]
    y = coarse_step(
        [none] + [y3[j] for j in range(3)] + [none],
        above, below, ext, [none] * 5, h, (row_at, row_ok, same_col),
    )
    for j in range(5):
        y4[j] = y[j]


REACH_E = 3
ORDER = [0, -1, 1, -2, 2, -3, 3]
LANE_OWN, LANE_TOP, LANE_BOTTOM, LANE_EXT, LANE_D = 0, 8, 16, 24, 25
LANE_PERP, LANE_LOAD, LANE_C, LANE_L = 32, 40, 48, 104
FACTORS = [(j, k) for j in range(7) for k in range(j + 1, 7)]


def dot(x, y):
    return total(x * y)


def response_kernel(me, ext, cross, chip, y4, cross_y, chip_y, phi, q, part):
    before, after = sides(me, cross, chip)
    ab, be = sides(me, cross_y, chip_y)
    rows, width = ext.shape
    m = 2 * REACH_E + 1
    diag = 4.0 + ext[...]
    none = jnp.zeros((rows, width), F32)
    fields = [none] + [y4[j] for j in range(5)] + [none]
    two_rows = jnp.zeros((2, width), F32)
    halo = []
    for k in range(3):
        up, down = ab[k], be[k]
        halo.append(jnp.concatenate([up[0:5], two_rows, two_rows, down[0:5]], axis=0))

    d_halo = [4.0 + spread(before, after, k, m) for k in range(2)]
    x, res = two_sweeps(fields, halo, None, None, diag, d_halo, spread(before, after, 2, m))
    for j in range(m):
        phi[j] = x[j]
    every = res[0]
    for j in range(1, m):
        every = every + res[j]
    basis = [every] + [res[REACH_E + j] for j in ORDER[1:]]
    values = []
    for j in range(m):
        v = basis[j]
        q[j] = v
        d = dot(v, v)
        inv = jnp.where(d > 0.0, 1.0 / jnp.where(d > 0.0, d, 1.0), 0.0)
        values.append((LANE_D + j, d))
        for k in range(j + 1, m):
            factor = dot(v, basis[k]) * inv
            values.append((LANE_L + FACTORS.index((j, k)), factor))
            basis[k] = basis[k] - factor * v
    part[...] = lane_row(values)


def solve_slabs(g, groups, cells):
    own, top, bottom = (g[k : k + 8] for k in (LANE_OWN, LANE_TOP, LANE_BOTTOM))
    n = own.shape[1]
    lane = lax.broadcasted_iota(jnp.int32, own.shape, 1)
    b = own + jnp.where(lane == n - 1, 0.0, pltpu.roll(top, n - 1, 1))
    b = b + jnp.where(lane == 0, 0.0, pltpu.roll(bottom, 1, 1))
    b = b / (groups * float(n))
    mean = jnp.broadcast_to(g[LANE_EXT : LANE_EXT + 1], own.shape) / float(cells)
    d = 2.0 + mean / (float(n) * float(n))
    lower = jnp.where(lane == 0, 0.0, 1.0)
    upper = jnp.where(lane == n - 1, 0.0, 1.0)
    excess = (d - lower) - upper
    s = 1
    while s < n:
        inv = 1.0 / (lower + upper + excess)
        alpha = lower * pltpu.roll(inv, s, 1)
        gamma = upper * pltpu.roll(inv, n - s, 1)
        b = b + alpha * pltpu.roll(b, s, 1) + gamma * pltpu.roll(b, n - s, 1)
        excess = excess + alpha * pltpu.roll(excess, s, 1) + gamma * pltpu.roll(excess, n - s, 1)
        lower = alpha * pltpu.roll(lower, s, 1)
        upper = gamma * pltpu.roll(upper, n - s, 1)
        s *= 2
    return b / (lower + upper + excess)


def coarse_kernel_b(me, x1, ext, b, row_at, row_ok, same_col, h, y4, cross, chip, x3, to_cross, to_chip):
    before, after = sides(me, cross, chip)
    put = sender(me, to_cross, to_chip)
    cases, rows, width = x1.shape
    x = coarse_step(
        [x1[c] for c in range(cases)],
        [before[row_of(c)] for c in range(cases)],
        [after[row_of(c)] for c in range(cases)],
        ext, b, h, (row_at, row_ok, same_col),
    )
    for c in range(cases):
        x3[c] = x[c]
        put(edge_row(c), x[c][0:1], x[c][rows - 1 : rows])
    no_row = jnp.zeros((1, width), F32)
    for c in range(cases, 9):
        put(edge_row(c), no_row, no_row)
    for j in range(5):
        y = y4[j]
        for k in range(3):
            put((k,) + row_of(j), y[k : k + 1], y[rows - 1 - k : rows - k])


def coarse_kernel_c(me, x3, ext, b, row_at, row_ok, same_col, h, smooth, cross, chip, v, to_cross, to_chip):
    before, after = sides(me, cross, chip)
    put = sender(me, to_cross, to_chip)
    cases, rows, width = x3.shape
    x = coarse_step(
        [x3[c] for c in range(cases)],
        [before[edge_row(c)] for c in range(cases)],
        [after[edge_row(c)] for c in range(cases)],
        ext, b, h, (row_at, row_ok, same_col),
    )
    for c in range(cases):
        y = smooth[c] + x[c]
        v[c] = y
        for k in range(3):
            put((k,) + row_of(c), y[k : k + 1], y[rows - 1 - k : rows - k])


def post_kernel(me, v, f, ext, cross, chip, cross_v, chip_v, q, part_a, part_e, out, gather):
    before, after = sides(me, cross, chip)
    before_v, after_v = sides(me, cross_v, chip_v)
    cases, rows, width = v.shape
    m = q.shape[0]
    diag = 4.0 + ext[...]
    fl = [f[c] for c in range(cases)]
    v_halo = [both(before_v, after_v, k) for k in range(3)]
    f_halo = [both(before, after, 3 + k) for k in range(2)]
    d_halo = [4.0 + spread(before, after, k, cases) for k in range(2)]
    valid = spread(before, after, 2, cases)
    x, res = two_sweeps([v[c] for c in range(cases)], v_halo, fl, f_halo, diag, d_halo, valid)
    for c in range(cases):
        out[c] = x[c]
    inv = []
    for j in range(m):
        d = part_e[:, LANE_D + j : LANE_D + j + 1]
        inv.append(jnp.where(d > 0.0, 1.0 / jnp.where(d > 0.0, d, 1.0), 0.0))
    values = []
    for c in range(cases):
        r = res[c]
        share = None
        for _ in range(2):
            step = [dot(r, q[j]) * inv[j] for j in range(m)]
            for j in range(m):
                r = r - step[j] * q[j]
            share = step if share is None else [p + t for p, t in zip(share, step)]
        values.append((LANE_PERP + c, dot(r, r)))
        values.append((LANE_LOAD + c, dot(fl[c], fl[c])))
        for j in range(m):
            values.append((LANE_C + 8 * j + c, share[j]))
    row = part_a[...] + part_e[...] + lane_row(values)
    gather[...] = jnp.broadcast_to(row, gather.shape)


def final_kernel(groups, me, base, phi, gathered, out, ratio):
    cases, rows, width = base.shape
    n = gathered.shape[0]
    m = phi.shape[0]
    g = jnp.transpose(gathered[...])
    e = solve_slabs(g, groups, rows * width)
    lane = lax.broadcasted_iota(jnp.int32, e.shape, 1)
    near = [
        jnp.sum(jnp.where(lane == me[0] + j, e, 0.0), axis=1, keepdims=True)
        for j in range(-REACH_E, REACH_E + 1)
    ]
    for c in range(cases):
        x = base[c]
        for j in range(m):
            x = x + near[j][c : c + 1] * phi[j]
        out[c] = x

    def shifted(j):
        inside = (lane + j >= 0) & (lane + j < n)
        return jnp.where(inside, pltpu.roll(e, (-j) % n, 1), 0.0)

    def spread_row(k):
        return jnp.broadcast_to(g[k : k + 1], e.shape)

    t = [e] + [shifted(j) - e for j in ORDER[1:]]
    norm = g[LANE_PERP : LANE_PERP + 8]
    for j in range(m):
        z = g[LANE_C + 8 * j : LANE_C + 8 * j + 8] + t[j]
        for k in range(j + 1, m):
            z = z + spread_row(LANE_L + FACTORS.index((j, k))) * t[k]
        norm = norm + spread_row(LANE_D + j) * (z * z)
    norm = jnp.sum(norm, axis=1, keepdims=True)
    load = jnp.sum(g[LANE_LOAD : LANE_LOAD + 8], axis=1, keepdims=True)
    case = lax.broadcasted_iota(jnp.int32, norm.shape, 0)
    r = jnp.sqrt(jnp.where(case < cases, norm, 0.0) / jnp.where(case < cases, load, 1.0))
    ratio[...] = jnp.broadcast_to(lane_row([(c, r[c : c + 1]) for c in range(cases)]), ratio.shape)


def local(thermal_solution, heat_forcing, extinction_factor, cluster_label):
    cases, rows, width = thermal_solution.shape
    n = lax.axis_size("blk")
    n_rhs = lax.axis_size("rhs")
    groups = rows * width // 16
    field = (cases, rows, width)
    pairs = [(i, i + 1) for i in range(1, n - 1, 2)]
    cross_chip = pairs + [(j, i) for i, j in pairs]
    on_chip = [(i, i ^ 1) for i in range(n)]

    def exchange(cross, chip):
        cross = lax.ppermute(cross, "blk", cross_chip)
        return cross, lax.ppermute(chip, "blk", on_chip)

    edge = (cases, width)
    edges = (8, width)
    deep = (3, 8, width)
    cells = (rows, width)
    u, f, ext, lab = thermal_solution, heat_forcing, extinction_factor, cluster_label
    sent = vmem_call(
        pack_kernel,
        [(6, cases, width)] * 2,
        [
            pltpu.VMEM(field, F32),
            pltpu.VMEM(field, F32),
            pltpu.VMEM(cells, F32),
            pltpu.SemaphoreType.DMA((3,)),
        ],
        n_in=3,
        in_space=pl.ANY,
    )(u, f, ext)
    halo = exchange(*sent)
    shifts = len(offsets())
    *tables, y3 = vmem_call(
        functools.partial(table_kernel, n),
        [
            ((shifts, rows, width), jnp.int32),
            (shifts, rows, width),
            (rows - 1, rows, width),
            cells,
            (3, rows, width),
        ],
        n_in=2,
    )(ext, lab)
    call = vmem_call
    smooth, b, x0, *sent, rsum = call(
        pre_kernel, [field, field, field, edges, edges, (1, 128)], n_in=10
    )(u, f, ext, *halo, *tables, y3)
    rows_x = exchange(*sent)
    x1, *sent, part_a = call(coarse_kernel_a, [field, edge, edge, (1, 128)], n_in=10)(
        x0, ext, b, *tables, rsum, *rows_x
    )
    (y4,) = call(functools.partial(answer_kernel, cases), [(5, rows, width)], n_in=8)(
        ext, *tables, y3, *rows_x
    )
    rows_x = exchange(*sent)
    x3, *sent = call(coarse_kernel_b, [field, deep, deep], n_in=10)(
        x1, ext, b, *tables, y4, *rows_x
    )
    rows_x = exchange(*sent)
    m = 2 * REACH_E + 1
    phi, q, part_e = call(
        response_kernel, [(m, rows, width), (m, rows, width), (1, 128)], n_in=6
    )(ext, *halo, y4, *rows_x)
    v, *sent = call(
        coarse_kernel_c, [field, (3, cases, width), (3, cases, width)], n_in=10
    )(x3, ext, b, *tables, smooth, *rows_x)
    rows_x = exchange(*sent)
    base, mine = call(post_kernel, [field, (n, 128)], n_in=10)(
        v, f, ext, *halo, *rows_x, q, part_a, part_e
    )
    gathered = lax.all_to_all(mine, "blk", 0, 0, tiled=True)
    corrected, ratio = call(
        functools.partial(final_kernel, groups), [field, (n_rhs, 128)], n_in=3
    )(base, phi, gathered)
    every = lax.all_to_all(ratio, "rhs", 0, 0, tiled=True)
    return corrected, every[:, :cases].reshape(n_rhs * cases)


def solution(mesh):
    in_specs = (P("rhs", "blk", None), P("rhs", "blk", None), P("blk", None), P("blk", None))
    out_specs = (P("rhs", "blk", None), P())
    return jax.shard_map(local, mesh=mesh, in_specs=in_specs, out_specs=out_specs, check_vma=False)
```

```python
import functools

import jax
import jax.numpy as jnp
from jax import lax
from jax.experimental import pallas as pl
from jax.experimental.pallas import tpu as pltpu
from jax.sharding import PartitionSpec as P

damping_fine = 0.8
damping_coarse = 0.5
REACH = 7
F32 = jnp.float32


VMEM = pl.BlockSpec(memory_space=pltpu.VMEM)


def with_place(body):
    def kernel(*refs):
        body((lax.axis_index("blk"), lax.axis_index("rhs")), *refs)

    return kernel


def vmem_call(body, outs, scratch=(), n_in=0, in_space=pltpu.VMEM):
    limit = 48 << 20 if in_space == pltpu.VMEM else None
    return pl.pallas_call(
        with_place(body),
        out_shape=[
            jax.ShapeDtypeStruct(*(s if isinstance(s[0], tuple) else (s, F32))) for s in outs
        ],
        in_specs=[pl.BlockSpec(memory_space=in_space)] * n_in,
        out_specs=[VMEM] * len(outs),
        scratch_shapes=list(scratch),
        compiler_params=pltpu.CompilerParams(vmem_limit_bytes=limit),
    )


class View:
    def __init__(self, own_chip, cross, chip):
        self.own_chip = own_chip
        self.chip, self.cross = chip, cross

    def __getitem__(self, k):
        return jnp.where(self.own_chip, self.chip[k], self.cross[k])


def sides(me, cross, chip):
    odd = (me[0] & 1) == 1
    return View(odd, cross, chip), View(jnp.logical_not(odd), cross, chip)


def row_of(c):
    return (pl.ds(c, 1), slice(None))


def sender(me, cross, chip):
    odd = (me[0] & 1) == 1

    def put(k, first, last):
        chip[k] = jnp.where(odd, first, last)
        cross[k] = jnp.where(odd, last, first)

    return put


def iotas(shape):
    return (
        lax.broadcasted_iota(jnp.int32, shape, 0),
        lax.broadcasted_iota(jnp.int32, shape, 1),
    )


def sideways(x):
    rows, width = x.shape
    col = lax.broadcasted_iota(jnp.int32, x.shape, 1)
    left = jnp.where(col == 0, 0.0, pltpu.roll(x, 1, 1))
    right = jnp.where(col == width - 1, 0.0, pltpu.roll(x, width - 1, 1))
    return left + right


def neighbours(x, above, below):
    rows = x.shape[0]
    row = lax.broadcasted_iota(jnp.int32, x.shape, 0)
    up = jnp.where(row == 0, above, pltpu.roll(x, 1, 0))
    down = jnp.where(row == rows - 1, below, pltpu.roll(x, rows - 1, 0))
    return up + down + sideways(x)


def offsets():
    return [d for d in range(-REACH, REACH + 1) if d]


def seg_sum(fields, tables):
    row_at, row_ok, same_col = tables
    rows, width = fields[0].shape
    col = list(fields)
    for k in range(1, rows):
        m = same_col[k - 1]
        col = [s + m * pltpu.roll(w, k, 0) for s, w in zip(col, fields)]
    out = list(col)
    for d, dx in enumerate(offsets()):
        at, ok = row_at[d], row_ok[d]
        out = [
            t
            + ok
            * jnp.take_along_axis(
                pltpu.roll(s, (-dx) % width, 1), at, axis=0, mode="promise_in_bounds"
            )
            for t, s in zip(out, col)
        ]
    return out


def table_kernel(n, me, ext, lab, row_at, row_ok, same_col, h, y3):
    key = lab[...]
    rows, width = key.shape
    for k in range(1, rows):
        same_col[k - 1] = jnp.where(pltpu.roll(key, k, 0) == key, 1.0, 0.0)
    for d, dx in enumerate(offsets()):
        there = pltpu.roll(key, (-dx) % width, 1)
        at = jnp.full(key.shape, -1, jnp.int32)
        for r in range(rows):
            at = jnp.where(jnp.broadcast_to(there[r : r + 1], key.shape) == key, r, at)
        row_ok[d] = jnp.where(at >= 0, 1.0, 0.0)
        row_at[d] = jnp.maximum(at, 0)
    row, col = iotas(key.shape)
    one = jnp.ones(key.shape, F32)
    zero = jnp.zeros(key.shape, F32)
    m = jnp.where((pltpu.roll(key, 1, 0) == key) & (row > 0), one, zero)
    m = m + jnp.where((pltpu.roll(key, rows - 1, 0) == key) & (row < rows - 1), one, zero)
    m = m + jnp.where((pltpu.roll(key, 1, 1) == key) & (col > 0), one, zero)
    m = m + jnp.where((pltpu.roll(key, width - 1, 1) == key) & (col < width - 1), one, zero)
    above = jnp.where(me[0] > 0, 1.0, 0.0)
    below = jnp.where(me[0] < n - 1, 1.0, 0.0)
    top = jnp.where(row == 0, one, zero)
    bottom = jnp.where(row == rows - 1, one, zero)
    open_sides = open_weight(ext[...])
    diag1, s_top, s_own, s_bottom = seg_sum(
        [4.0 + ext[...] - m, top, open_sides, bottom], (row_at, row_ok, same_col)
    )
    half = damping_coarse / diag1
    h[...] = half
    y3[0] = above * (half * s_top)
    y3[1] = 1.0 - half * s_own
    y3[2] = below * (half * s_bottom)


def open_weight(ext):
    rows, width = ext.shape
    row, col = iotas(ext.shape)
    one = jnp.ones(ext.shape, F32)
    zero = jnp.zeros(ext.shape, F32)
    weight = ext
    for at_edge in (row == 0, row == rows - 1, col == 0, col == width - 1):
        weight = weight + jnp.where(at_edge, one, zero)
    return weight


GROUP_EXT = 5


def pack_kernel(me, u_hbm, f_hbm, ext_hbm, cross, chip, u, f, ext, sem):
    pairs = ((u_hbm, u), (f_hbm, f), (ext_hbm, ext))
    copies = [pltpu.make_async_copy(src, dst, sem.at[k]) for k, (src, dst) in enumerate(pairs)]
    for copy in copies:
        copy.start()
    for copy in copies:
        copy.wait()
    cases, rows, width = u.shape
    put = sender(me, cross, chip)
    ones = jnp.ones((1, width), F32)
    end = rows - 1
    for k in range(3):
        put(k, u[:, k, :], u[:, end - k, :])
    for k in range(2):
        put(3 + k, f[:, k, :], f[:, end - k, :])
        at = (GROUP_EXT,) + row_of(k)
        put(at, ext[pl.ds(k, 1), :], ext[pl.ds(end - k, 1), :])
    for k in range(2, cases):
        put((GROUP_EXT,) + row_of(k), ones, ones)


def both(before, after, k):
    return jnp.concatenate([before[k], after[k]], axis=0)


def spread(before, after, k, times):
    at = (GROUP_EXT,) + row_of(k)
    up, down = before[at], after[at]
    shape = (times, up.shape[1])
    return jnp.concatenate([jnp.broadcast_to(up, shape), jnp.broadcast_to(down, shape)], axis=0)


def two_sweeps(u, u_halo, f, f_halo, diag, diag_halo, valid):
    cases = len(u)
    rows = u[0].shape[0]
    gain = damping_fine / diag
    gain_halo = [damping_fine / d for d in diag_halo]
    keep = 1.0 - damping_fine

    def edge(x):
        return jnp.concatenate([v[0:1] for v in x] + [v[rows - 1 : rows] for v in x], axis=0)

    def around(x, halo, c):
        return neighbours(x[c], halo[0][c : c + 1], halo[0][cases + c : cases + c + 1])

    def sweep(x, halo, depth):
        new = []
        for c in range(cases):
            push = around(x, halo, c)
            new.append(keep * x[c] + gain * (push if f is None else f[c] + push))
        inner = [edge(x)] + halo
        new_halo = []
        for k in range(depth):
            push = inner[k] + inner[k + 2] + sideways(halo[k])
            push = push if f is None else f_halo[k] + push
            new_halo.append((keep * halo[k] + gain_halo[k] * push) * valid)
        return new, new_halo

    x, h = sweep(u, u_halo, 2)
    x, h = sweep(x, h, 1)
    res = []
    for c in range(cases):
        r = around(x, h, c) - diag * x[c]
        res.append(r if f is None else f[c] + r)
    return x, res


def total(x):
    rows, width = x.shape
    part = x[:, 0:128]
    for k in range(1, width // 128):
        part = part + x[:, k * 128 : (k + 1) * 128]
    return jnp.sum(jnp.sum(part, axis=1, keepdims=True), axis=0, keepdims=True)


def lane_row(values):
    lane = lax.broadcasted_iota(jnp.int32, (1, 128), 1)
    row = jnp.zeros((1, 128), F32)
    for k, v in values:
        row = jnp.where(lane == k, v, row)
    return row


def pre_kernel(me, u, f, ext, cross, chip, row_at, row_ok, same_col, h, y3, smooth, b, x0, to_cross, to_chip, rsum):
    before, after = sides(me, cross, chip)
    put = sender(me, to_cross, to_chip)
    cases, rows, width = u.shape
    diag = 4.0 + ext[...]
    us = [u[c] for c in range(cases)]
    fl = [f[c] for c in range(cases)]
    u_halo = [both(before, after, k) for k in range(3)]
    f_halo = [both(before, after, 3 + k) for k in range(2)]
    d_halo = [4.0 + spread(before, after, k, cases) for k in range(2)]
    valid = spread(before, after, 2, cases)
    x, res = two_sweeps(us, u_halo, fl, f_halo, diag, d_halo, valid)
    for c in range(cases):
        smooth[c] = x[c]
    sums = seg_sum(res, (row_at, row_ok, same_col))
    for c in range(cases):
        b[c] = sums[c]
        v = h[...] * sums[c]
        x0[c] = v
        put(row_of(c), v[0:1], v[rows - 1 : rows])
    for j in range(3):
        y = y3[j]
        put(row_of(cases + j), y[0:1], y[rows - 1 : rows])
    put(row_of(cases + 3), jnp.zeros((1, width), F32), jnp.zeros((1, width), F32))
    rsum[...] = lane_row([(c, total(res[c])) for c in range(cases)])


def coarse_step(x, above, below, ext, b, h, tables):
    cases = len(x)
    diag = 4.0 + ext[...]
    w = [diag * x[c] - neighbours(x[c], above[c], below[c]) for c in range(cases)]
    sums = seg_sum(w, tables)
    return [x[c] + h[...] * (b[c] - sums[c]) for c in range(cases)]


def flat_row(r):
    return (r // 4,) + row_of(r % 4)


def response_row(k, j):
    return flat_row(4 + 5 * k + j)


def coarse_kernel_a(me, x0, ext, b, row_at, row_ok, same_col, h, rsum, cross, chip, x1, to_cross, to_chip, part):
    before, after = sides(me, cross, chip)
    put = sender(me, to_cross, to_chip)
    cases, rows, width = x0.shape
    x = coarse_step(
        [x0[c] for c in range(cases)],
        [before[row_of(c)] for c in range(cases)],
        [after[row_of(c)] for c in range(cases)],
        ext, b, h, (row_at, row_ok, same_col),
    )
    weight = open_weight(ext[...])
    values = []
    for c in range(cases):
        x1[c] = x[c]
        put(row_of(c), x[c][0:1], x[c][rows - 1 : rows])
        own = rsum[:, c : c + 1] - total(weight * x[c])
        values.append((LANE_OWN + c, own))
        values.append((LANE_TOP + c, total(x[c][0:1])))
        values.append((LANE_BOTTOM + c, total(x[c][rows - 1 : rows])))
    values.append((LANE_EXT, total(ext[...])))
    part[...] = lane_row(values)


def answer_kernel(cases, me, ext, row_at, row_ok, same_col, h, y3, cross, chip, y4):
    before, after = sides(me, cross, chip)
    rows, width = ext.shape
    none = jnp.zeros((rows, width), F32)
    no_row = jnp.zeros((1, width), F32)
    above = [before[row_of(cases + j)] for j in range(3)] + [no_row, no_row]
    below = [no_row, no_row] + [after[row_of(cases + j)] for j in range(3)]
    y = coarse_step(
        [none] + [y3[j] for j in range(3)] + [none],
        above, below, ext, [none] * 5, h, (row_at, row_ok, same_col),
    )
    for j in range(5):
        y4[j] = y[j]


REACH_E = 3
ORDER = [0, -1, 1, -2, 2, -3, 3]
LANE_OWN, LANE_TOP, LANE_BOTTOM, LANE_EXT, LANE_D = 0, 8, 16, 24, 25
LANE_PERP, LANE_LOAD, LANE_C, LANE_L = 32, 40, 48, 104
FACTORS = [(j, k) for j in range(7) for k in range(j + 1, 7)]


def dot(x, y):
    return total(x * y)


def response_kernel(me, ext, cross, chip, y4, cross_y, chip_y, phi, q, part):
    before, after = sides(me, cross, chip)
    ab, be = sides(me, cross_y, chip_y)
    rows, width = ext.shape
    m = 2 * REACH_E + 1
    diag = 4.0 + ext[...]
    none = jnp.zeros((rows, width), F32)
    fields = [none] + [y4[j] for j in range(5)] + [none]
    two_rows = jnp.zeros((2, width), F32)
    halo = []
    for k in range(3):
        up = [ab[response_row(k, j)] for j in range(5)]
        down = [be[response_row(k, j)] for j in range(5)]
        halo.append(jnp.concatenate(up + [two_rows, two_rows] + down, axis=0))

    d_halo = [4.0 + spread(before, after, k, m) for k in range(2)]
    x, res = two_sweeps(fields, halo, None, None, diag, d_halo, spread(before, after, 2, m))
    for j in range(m):
        phi[j] = x[j]
    every = res[0]
    for j in range(1, m):
        every = every + res[j]
    basis = [every] + [res[REACH_E + j] for j in ORDER[1:]]
    values = []
    for j in range(m):
        v = basis[j]
        q[j] = v
        d = dot(v, v)
        inv = jnp.where(d > 0.0, 1.0 / jnp.where(d > 0.0, d, 1.0), 0.0)
        values.append((LANE_D + j, d))
        for k in range(j + 1, m):
            factor = dot(v, basis[k]) * inv
            values.append((LANE_L + FACTORS.index((j, k)), factor))
            basis[k] = basis[k] - factor * v
    part[...] = lane_row(values)


def solve_slabs(g, groups, cells):
    own, top, bottom = (g[k : k + 8] for k in (LANE_OWN, LANE_TOP, LANE_BOTTOM))
    n = own.shape[1]
    lane = lax.broadcasted_iota(jnp.int32, own.shape, 1)
    b = own + jnp.where(lane == n - 1, 0.0, pltpu.roll(top, n - 1, 1))
    b = b + jnp.where(lane == 0, 0.0, pltpu.roll(bottom, 1, 1))
    b = b / (groups * float(n))
    mean = jnp.broadcast_to(g[LANE_EXT : LANE_EXT + 1], own.shape) / float(cells)
    d = 2.0 + mean / (float(n) * float(n))
    lower = jnp.where(lane == 0, 0.0, 1.0)
    upper = jnp.where(lane == n - 1, 0.0, 1.0)
    excess = (d - lower) - upper
    s = 1
    while s < n:
        inv = 1.0 / (lower + upper + excess)
        alpha = lower * pltpu.roll(inv, s, 1)
        gamma = upper * pltpu.roll(inv, n - s, 1)
        b = b + alpha * pltpu.roll(b, s, 1) + gamma * pltpu.roll(b, n - s, 1)
        excess = excess + alpha * pltpu.roll(excess, s, 1) + gamma * pltpu.roll(excess, n - s, 1)
        lower = alpha * pltpu.roll(lower, s, 1)
        upper = gamma * pltpu.roll(upper, n - s, 1)
        s *= 2
    return b / (lower + upper + excess)


def coarse_kernel_b(me, x1, ext, b, row_at, row_ok, same_col, h, y4, cross, chip, x3, to_cross, to_chip):
    before, after = sides(me, cross, chip)
    put = sender(me, to_cross, to_chip)
    cases, rows, width = x1.shape
    x = coarse_step(
        [x1[c] for c in range(cases)],
        [before[row_of(c)] for c in range(cases)],
        [after[row_of(c)] for c in range(cases)],
        ext, b, h, (row_at, row_ok, same_col),
    )
    for c in range(cases):
        x3[c] = x[c]
        put(flat_row(c), x[c][0:1], x[c][rows - 1 : rows])
    no_row = jnp.zeros((1, width), F32)
    put(flat_row(19), no_row, no_row)
    for j in range(5):
        y = y4[j]
        for k in range(3):
            put(response_row(k, j), y[k : k + 1], y[rows - 1 - k : rows - k])


def coarse_kernel_c(me, x3, ext, b, row_at, row_ok, same_col, h, smooth, cross, chip, v, to_cross, to_chip):
    before, after = sides(me, cross, chip)
    put = sender(me, to_cross, to_chip)
    cases, rows, width = x3.shape
    x = coarse_step(
        [x3[c] for c in range(cases)],
        [before[flat_row(c)] for c in range(cases)],
        [after[flat_row(c)] for c in range(cases)],
        ext, b, h, (row_at, row_ok, same_col),
    )
    for c in range(cases):
        y = smooth[c] + x[c]
        v[c] = y
        for k in range(3):
            put((k,) + row_of(c), y[k : k + 1], y[rows - 1 - k : rows - k])


def post_kernel(me, v, f, ext, cross, chip, cross_v, chip_v, q, part_a, part_e, out, gather):
    before, after = sides(me, cross, chip)
    before_v, after_v = sides(me, cross_v, chip_v)
    cases, rows, width = v.shape
    m = q.shape[0]
    diag = 4.0 + ext[...]
    fl = [f[c] for c in range(cases)]
    v_halo = [both(before_v, after_v, k) for k in range(3)]
    f_halo = [both(before, after, 3 + k) for k in range(2)]
    d_halo = [4.0 + spread(before, after, k, cases) for k in range(2)]
    valid = spread(before, after, 2, cases)
    x, res = two_sweeps([v[c] for c in range(cases)], v_halo, fl, f_halo, diag, d_halo, valid)
    for c in range(cases):
        out[c] = x[c]
    inv = []
    for j in range(m):
        d = part_e[:, LANE_D + j : LANE_D + j + 1]
        inv.append(jnp.where(d > 0.0, 1.0 / jnp.where(d > 0.0, d, 1.0), 0.0))
    values = []
    for c in range(cases):
        r = res[c]
        share = [dot(r, q[j]) * inv[j] for j in range(m)]
        for j in range(m):
            r = r - share[j] * q[j]
        values.append((LANE_PERP + c, dot(r, r)))
        values.append((LANE_LOAD + c, dot(fl[c], fl[c])))
        for j in range(m):
            values.append((LANE_C + 8 * j + c, share[j]))
    row = part_a[...] + part_e[...] + lane_row(values)
    gather[...] = jnp.broadcast_to(row, gather.shape)


def ratio_kernel(groups, cases, cells, me, gathered, ratio, near):
    n = gathered.shape[0]
    m = 2 * REACH_E + 1
    g = jnp.transpose(gathered[...])
    e = solve_slabs(g, groups, cells)
    lane = lax.broadcasted_iota(jnp.int32, e.shape, 1)
    for j in range(m):
        at = lane == me[0] + j - REACH_E
        own = jnp.sum(jnp.where(at, e, 0.0), axis=1, keepdims=True)
        near[j] = jnp.broadcast_to(own, near.shape[1:])

    def shifted(j):
        inside = (lane + j >= 0) & (lane + j < n)
        return jnp.where(inside, pltpu.roll(e, (-j) % n, 1), 0.0)

    def spread_row(k):
        return jnp.broadcast_to(g[k : k + 1], e.shape)

    t = [e] + [shifted(j) - e for j in ORDER[1:]]
    norm = g[LANE_PERP : LANE_PERP + 8]
    for j in range(m):
        z = g[LANE_C + 8 * j : LANE_C + 8 * j + 8] + t[j]
        for k in range(j + 1, m):
            z = z + spread_row(LANE_L + FACTORS.index((j, k))) * t[k]
        norm = norm + spread_row(LANE_D + j) * (z * z)
    norm = jnp.sum(norm, axis=1, keepdims=True)
    load = jnp.sum(g[LANE_LOAD : LANE_LOAD + 8], axis=1, keepdims=True)
    case = lax.broadcasted_iota(jnp.int32, norm.shape, 0)
    r = jnp.sqrt(jnp.where(case < cases, norm, 0.0) / jnp.where(case < cases, load, 1.0))
    ratio[...] = jnp.broadcast_to(lane_row([(c, r[c : c + 1]) for c in range(cases)]), ratio.shape)


def final_kernel(me, base, phi, near, out):
    cases, rows, width = base.shape
    for c in range(cases):
        x = base[c]
        for j in range(phi.shape[0]):
            x = x + near[j, pl.ds(c, 1), 0:1] * phi[j]
        out[c] = x


def local(thermal_solution, heat_forcing, extinction_factor, cluster_label):
    cases, rows, width = thermal_solution.shape
    n = lax.axis_size("blk")
    n_rhs = lax.axis_size("rhs")
    groups = rows * width // 16
    field = (cases, rows, width)
    pairs = [(i, i + 1) for i in range(1, n - 1, 2)]
    cross_chip = pairs + [(j, i) for i, j in pairs]
    on_chip = [(i, i ^ 1) for i in range(n)]

    def exchange(cross, chip):
        cross = lax.ppermute(cross, "blk", cross_chip)
        return cross, lax.ppermute(chip, "blk", on_chip)

    edge = (cases, width)
    edges = (8, width)
    deep = (5, 4, width)
    cells = (rows, width)
    u, f, ext, lab = thermal_solution, heat_forcing, extinction_factor, cluster_label
    sent = vmem_call(
        pack_kernel,
        [(6, cases, width)] * 2,
        [
            pltpu.VMEM(field, F32),
            pltpu.VMEM(field, F32),
            pltpu.VMEM(cells, F32),
            pltpu.SemaphoreType.DMA((3,)),
        ],
        n_in=3,
        in_space=pl.ANY,
    )(u, f, ext)
    halo = exchange(*sent)
    shifts = len(offsets())
    *tables, y3 = vmem_call(
        functools.partial(table_kernel, n),
        [
            ((shifts, rows, width), jnp.int32),
            (shifts, rows, width),
            (rows - 1, rows, width),
            cells,
            (3, rows, width),
        ],
        n_in=2,
    )(ext, lab)
    call = vmem_call
    smooth, b, x0, *sent, rsum = call(
        pre_kernel, [field, field, field, edges, edges, (1, 128)], n_in=10
    )(u, f, ext, *halo, *tables, y3)
    rows_x = exchange(*sent)
    x1, *sent, part_a = call(coarse_kernel_a, [field, edge, edge, (1, 128)], n_in=10)(
        x0, ext, b, *tables, rsum, *rows_x
    )
    (y4,) = call(functools.partial(answer_kernel, cases), [(5, rows, width)], n_in=8)(
        ext, *tables, y3, *rows_x
    )
    rows_x = exchange(*sent)
    x3, *sent = call(coarse_kernel_b, [field, deep, deep], n_in=10)(
        x1, ext, b, *tables, y4, *rows_x
    )
    rows_x = exchange(*sent)
    m = 2 * REACH_E + 1
    phi, q, part_e = call(
        response_kernel, [(m, rows, width), (m, rows, width), (1, 128)], n_in=6
    )(ext, *halo, y4, *rows_x)
    v, *sent = call(
        coarse_kernel_c, [field, (3, cases, width), (3, cases, width)], n_in=10
    )(x3, ext, b, *tables, smooth, *rows_x)
    rows_x = exchange(*sent)
    base, mine = call(post_kernel, [field, (n, 128)], n_in=10)(
        v, f, ext, *halo, *rows_x, q, part_a, part_e
    )
    gathered = lax.all_to_all(mine, "blk", 0, 0, tiled=True)
    ratio, near = call(
        functools.partial(ratio_kernel, groups, cases, rows * width),
        [(n_rhs, 128), (m, 8, 128)],
        n_in=1,
    )(gathered)
    every = lax.all_to_all(ratio, "rhs", 0, 0, tiled=True)
    (corrected,) = call(final_kernel, [field], n_in=3)(base, phi, near)
    return corrected, every[:, :cases].reshape(n_rhs * cases)


def solution(mesh):
    in_specs = (P("rhs", "blk", None), P("rhs", "blk", None), P("blk", None), P("blk", None))
    out_specs = (P("rhs", "blk", None), P())
    return jax.shard_map(local, mesh=mesh, in_specs=in_specs, out_specs=out_specs, check_vma=False)
```

```python
import functools

import jax
import jax.numpy as jnp
from jax import lax
from jax.experimental import pallas as pl
from jax.experimental.pallas import tpu as pltpu
from jax.sharding import PartitionSpec as P

damping_fine = 0.8
damping_coarse = 0.5
REACH = 7
F32 = jnp.float32


VMEM = pl.BlockSpec(memory_space=pltpu.VMEM)


def with_place(body):
    def kernel(*refs):
        body((lax.axis_index("blk"), lax.axis_index("rhs")), *refs)

    return kernel


def vmem_call(body, outs, scratch=(), n_in=0, in_space=pltpu.VMEM):
    limit = 48 << 20 if in_space == pltpu.VMEM else None
    return pl.pallas_call(
        with_place(body),
        out_shape=[
            jax.ShapeDtypeStruct(*(s if isinstance(s[0], tuple) else (s, F32))) for s in outs
        ],
        in_specs=[pl.BlockSpec(memory_space=in_space)] * n_in,
        out_specs=[VMEM] * len(outs),
        scratch_shapes=list(scratch),
        compiler_params=pltpu.CompilerParams(vmem_limit_bytes=limit),
    )


class View:
    def __init__(self, own_chip, cross, chip):
        self.own_chip = own_chip
        self.chip, self.cross = chip, cross

    def __getitem__(self, k):
        return jnp.where(self.own_chip, self.chip[k], self.cross[k])


def sides(me, cross, chip):
    odd = (me[0] & 1) == 1
    return View(odd, cross, chip), View(jnp.logical_not(odd), cross, chip)


def row_of(c):
    return (pl.ds(c, 1), slice(None))


def sender(me, cross, chip):
    odd = (me[0] & 1) == 1

    def put(k, first, last):
        chip[k] = jnp.where(odd, first, last)
        cross[k] = jnp.where(odd, last, first)

    return put


def iotas(shape):
    return (
        lax.broadcasted_iota(jnp.int32, shape, 0),
        lax.broadcasted_iota(jnp.int32, shape, 1),
    )


def sideways(x):
    rows, width = x.shape
    col = lax.broadcasted_iota(jnp.int32, x.shape, 1)
    left = jnp.where(col == 0, 0.0, pltpu.roll(x, 1, 1))
    right = jnp.where(col == width - 1, 0.0, pltpu.roll(x, width - 1, 1))
    return left + right


def neighbours(x, above, below):
    rows = x.shape[0]
    row = lax.broadcasted_iota(jnp.int32, x.shape, 0)
    up = jnp.where(row == 0, above, pltpu.roll(x, 1, 0))
    down = jnp.where(row == rows - 1, below, pltpu.roll(x, rows - 1, 0))
    return up + down + sideways(x)


def offsets():
    return [d for d in range(-REACH, REACH + 1) if d]


def seg_sum(fields, tables):
    row_at, row_ok, same_col = tables
    rows, width = fields[0].shape
    col = list(fields)
    for k in range(1, rows):
        m = same_col[k - 1]
        col = [s + m * pltpu.roll(w, k, 0) for s, w in zip(col, fields)]
    out = list(col)
    for d, dx in enumerate(offsets()):
        at, ok = row_at[d], row_ok[d]
        out = [
            t
            + ok
            * jnp.take_along_axis(
                pltpu.roll(s, (-dx) % width, 1), at, axis=0, mode="promise_in_bounds"
            )
            for t, s in zip(out, col)
        ]
    return out


def table_kernel(n, me, ext, lab, row_at, row_ok, same_col, h, y3):
    key = lab[...]
    rows, width = key.shape
    for k in range(1, rows):
        same_col[k - 1] = jnp.where(pltpu.roll(key, k, 0) == key, 1.0, 0.0)
    for d, dx in enumerate(offsets()):
        there = pltpu.roll(key, (-dx) % width, 1)
        at = jnp.full(key.shape, -1, jnp.int32)
        for r in range(rows):
            at = jnp.where(jnp.broadcast_to(there[r : r + 1], key.shape) == key, r, at)
        row_ok[d] = jnp.where(at >= 0, 1.0, 0.0)
        row_at[d] = jnp.maximum(at, 0)
    row, col = iotas(key.shape)
    one = jnp.ones(key.shape, F32)
    zero = jnp.zeros(key.shape, F32)
    m = jnp.where((pltpu.roll(key, 1, 0) == key) & (row > 0), one, zero)
    m = m + jnp.where((pltpu.roll(key, rows - 1, 0) == key) & (row < rows - 1), one, zero)
    m = m + jnp.where((pltpu.roll(key, 1, 1) == key) & (col > 0), one, zero)
    m = m + jnp.where((pltpu.roll(key, width - 1, 1) == key) & (col < width - 1), one, zero)
    above = jnp.where(me[0] > 0, 1.0, 0.0)
    below = jnp.where(me[0] < n - 1, 1.0, 0.0)
    top = jnp.where(row == 0, one, zero)
    bottom = jnp.where(row == rows - 1, one, zero)
    open_sides = open_weight(ext[...])
    diag1, s_top, s_own, s_bottom = seg_sum(
        [4.0 + ext[...] - m, top, open_sides, bottom], (row_at, row_ok, same_col)
    )
    half = damping_coarse / diag1
    h[...] = half
    y3[0] = above * (half * s_top)
    y3[1] = 1.0 - half * s_own
    y3[2] = below * (half * s_bottom)


def open_weight(ext):
    rows, width = ext.shape
    row, col = iotas(ext.shape)
    one = jnp.ones(ext.shape, F32)
    zero = jnp.zeros(ext.shape, F32)
    weight = ext
    for at_edge in (row == 0, row == rows - 1, col == 0, col == width - 1):
        weight = weight + jnp.where(at_edge, one, zero)
    return weight


GROUP_EXT = 5


def pack_kernel(me, u_hbm, f_hbm, ext_hbm, cross, chip, u, f, ext, sem):
    pairs = ((u_hbm, u), (f_hbm, f), (ext_hbm, ext))
    copies = [pltpu.make_async_copy(src, dst, sem.at[k]) for k, (src, dst) in enumerate(pairs)]
    for copy in copies:
        copy.start(priority=1)
    for copy in copies:
        copy.wait()
    cases, rows, width = u.shape
    put = sender(me, cross, chip)
    ones = jnp.ones((1, width), F32)
    end = rows - 1
    for k in range(3):
        put(k, u[:, k, :], u[:, end - k, :])
    for k in range(2):
        put(3 + k, f[:, k, :], f[:, end - k, :])
        at = (GROUP_EXT,) + row_of(k)
        put(at, ext[pl.ds(k, 1), :], ext[pl.ds(end - k, 1), :])
    for k in range(2, cases):
        put((GROUP_EXT,) + row_of(k), ones, ones)


def both(before, after, k):
    return jnp.concatenate([before[k], after[k]], axis=0)


def spread(before, after, k, times):
    at = (GROUP_EXT,) + row_of(k)
    up, down = before[at], after[at]
    shape = (times, up.shape[1])
    return jnp.concatenate([jnp.broadcast_to(up, shape), jnp.broadcast_to(down, shape)], axis=0)


def two_sweeps(u, u_halo, f, f_halo, diag, diag_halo, valid):
    cases = len(u)
    rows = u[0].shape[0]
    gain = damping_fine / diag
    gain_halo = [damping_fine / d for d in diag_halo]
    keep = 1.0 - damping_fine

    def edge(x):
        return jnp.concatenate([v[0:1] for v in x] + [v[rows - 1 : rows] for v in x], axis=0)

    def around(x, halo, c):
        return neighbours(x[c], halo[0][c : c + 1], halo[0][cases + c : cases + c + 1])

    def sweep(x, halo, depth):
        new = []
        for c in range(cases):
            push = around(x, halo, c)
            new.append(keep * x[c] + gain * (push if f is None else f[c] + push))
        inner = [edge(x)] + halo
        new_halo = []
        for k in range(depth):
            push = inner[k] + inner[k + 2] + sideways(halo[k])
            push = push if f is None else f_halo[k] + push
            new_halo.append((keep * halo[k] + gain_halo[k] * push) * valid)
        return new, new_halo

    x, h = sweep(u, u_halo, 2)
    x, h = sweep(x, h, 1)
    res = []
    for c in range(cases):
        r = around(x, h, c) - diag * x[c]
        res.append(r if f is None else f[c] + r)
    return x, res


def total(x):
    rows, width = x.shape
    part = x[:, 0:128]
    for k in range(1, width // 128):
        part = part + x[:, k * 128 : (k + 1) * 128]
    return jnp.sum(jnp.sum(part, axis=1, keepdims=True), axis=0, keepdims=True)


def lane_row(values):
    lane = lax.broadcasted_iota(jnp.int32, (1, 128), 1)
    row = jnp.zeros((1, 128), F32)
    for k, v in values:
        row = jnp.where(lane == k, v, row)
    return row


def pre_kernel(me, u, f, ext, cross, chip, row_at, row_ok, same_col, h, y3, smooth, b, x0, to_cross, to_chip, rsum):
    before, after = sides(me, cross, chip)
    put = sender(me, to_cross, to_chip)
    cases, rows, width = u.shape
    diag = 4.0 + ext[...]
    us = [u[c] for c in range(cases)]
    fl = [f[c] for c in range(cases)]
    u_halo = [both(before, after, k) for k in range(3)]
    f_halo = [both(before, after, 3 + k) for k in range(2)]
    d_halo = [4.0 + spread(before, after, k, cases) for k in range(2)]
    valid = spread(before, after, 2, cases)
    x, res = two_sweeps(us, u_halo, fl, f_halo, diag, d_halo, valid)
    for c in range(cases):
        smooth[c] = x[c]
    sums = seg_sum(res, (row_at, row_ok, same_col))
    for c in range(cases):
        b[c] = sums[c]
        v = h[...] * sums[c]
        x0[c] = v
        put(row_of(c), v[0:1], v[rows - 1 : rows])
    for j in range(3):
        y = y3[j]
        put(row_of(cases + j), y[0:1], y[rows - 1 : rows])
    put(row_of(cases + 3), jnp.zeros((1, width), F32), jnp.zeros((1, width), F32))
    rsum[...] = lane_row([(c, total(res[c])) for c in range(cases)])


def coarse_step(x, above, below, ext, b, h, tables):
    cases = len(x)
    diag = 4.0 + ext[...]
    w = [diag * x[c] - neighbours(x[c], above[c], below[c]) for c in range(cases)]
    sums = seg_sum(w, tables)
    return [x[c] + h[...] * (b[c] - sums[c]) for c in range(cases)]


def flat_row(r):
    return (r // 4,) + row_of(r % 4)


def response_row(k, j):
    return flat_row(4 + 5 * k + j)


def coarse_kernel_a(me, x0, ext, b, row_at, row_ok, same_col, h, cross, chip, x1, to_cross, to_chip):
    before, after = sides(me, cross, chip)
    put = sender(me, to_cross, to_chip)
    cases, rows, width = x0.shape
    x = coarse_step(
        [x0[c] for c in range(cases)],
        [before[row_of(c)] for c in range(cases)],
        [after[row_of(c)] for c in range(cases)],
        ext, b, h, (row_at, row_ok, same_col),
    )
    for c in range(cases):
        x1[c] = x[c]
        put(row_of(c), x[c][0:1], x[c][rows - 1 : rows])


def sum_kernel(me, x1, ext, f, rsum, part):
    cases, rows, width = x1.shape
    weight = open_weight(ext[...])
    values = [(LANE_EXT, total(ext[...]))]
    for c in range(cases):
        x = x1[c]
        values.append((LANE_OWN + c, rsum[:, c : c + 1] - total(weight * x)))
        values.append((LANE_TOP + c, total(x[0:1])))
        values.append((LANE_BOTTOM + c, total(x[rows - 1 : rows])))
        values.append((LANE_LOAD + c, dot(f[c], f[c])))
    part[...] = lane_row(values)


def answer_kernel(cases, me, ext, row_at, row_ok, same_col, h, y3, cross, chip, y4):
    before, after = sides(me, cross, chip)
    rows, width = ext.shape
    none = jnp.zeros((rows, width), F32)
    no_row = jnp.zeros((1, width), F32)
    above = [before[row_of(cases + j)] for j in range(3)] + [no_row, no_row]
    below = [no_row, no_row] + [after[row_of(cases + j)] for j in range(3)]
    y = coarse_step(
        [none] + [y3[j] for j in range(3)] + [none],
        above, below, ext, [none] * 5, h, (row_at, row_ok, same_col),
    )
    for j in range(5):
        y4[j] = y[j]


REACH_E = 3
ORDER = [0, -1, 1, -2, 2, -3, 3]
LANE_OWN, LANE_TOP, LANE_BOTTOM, LANE_EXT, LANE_D = 0, 8, 16, 24, 25
LANE_PERP, LANE_LOAD, LANE_C, LANE_L = 32, 40, 48, 104
FACTORS = [(j, k) for j in range(7) for k in range(j + 1, 7)]


def dot(x, y):
    return total(x * y)


def response_kernel(me, ext, cross, chip, y4, cross_y, chip_y, phi, q, part):
    before, after = sides(me, cross, chip)
    ab, be = sides(me, cross_y, chip_y)
    rows, width = ext.shape
    m = 2 * REACH_E + 1
    diag = 4.0 + ext[...]
    none = jnp.zeros((rows, width), F32)
    fields = [none] + [y4[j] for j in range(5)] + [none]
    two_rows = jnp.zeros((2, width), F32)
    halo = []
    for k in range(3):
        up = [ab[response_row(k, j)] for j in range(5)]
        down = [be[response_row(k, j)] for j in range(5)]
        halo.append(jnp.concatenate(up + [two_rows, two_rows] + down, axis=0))

    d_halo = [4.0 + spread(before, after, k, m) for k in range(2)]
    x, res = two_sweeps(fields, halo, None, None, diag, d_halo, spread(before, after, 2, m))
    for j in range(m):
        phi[j] = x[j]
    every = res[0]
    for j in range(1, m):
        every = every + res[j]
    basis = [every] + [res[REACH_E + j] for j in ORDER[1:]]
    values = []
    for j in range(m):
        v = basis[j]
        q[j] = v
        d = dot(v, v)
        inv = jnp.where(d > 0.0, 1.0 / jnp.where(d > 0.0, d, 1.0), 0.0)
        values.append((LANE_D + j, d))
        for k in range(j + 1, m):
            factor = dot(v, basis[k]) * inv
            values.append((LANE_L + FACTORS.index((j, k)), factor))
            basis[k] = basis[k] - factor * v
    part[...] = lane_row(values)


def solve_slabs(g, groups, cells):
    own, top, bottom = (g[k : k + 8] for k in (LANE_OWN, LANE_TOP, LANE_BOTTOM))
    n = own.shape[1]
    lane = lax.broadcasted_iota(jnp.int32, own.shape, 1)
    b = own + jnp.where(lane == n - 1, 0.0, pltpu.roll(top, n - 1, 1))
    b = b + jnp.where(lane == 0, 0.0, pltpu.roll(bottom, 1, 1))
    b = b / (groups * float(n))
    mean = jnp.broadcast_to(g[LANE_EXT : LANE_EXT + 1], own.shape) / float(cells)
    d = 2.0 + mean / (float(n) * float(n))
    lower = jnp.where(lane == 0, 0.0, 1.0)
    upper = jnp.where(lane == n - 1, 0.0, 1.0)
    excess = (d - lower) - upper
    s = 1
    while s < n:
        inv = 1.0 / (lower + upper + excess)
        alpha = lower * pltpu.roll(inv, s, 1)
        gamma = upper * pltpu.roll(inv, n - s, 1)
        b = b + alpha * pltpu.roll(b, s, 1) + gamma * pltpu.roll(b, n - s, 1)
        excess = excess + alpha * pltpu.roll(excess, s, 1) + gamma * pltpu.roll(excess, n - s, 1)
        lower = alpha * pltpu.roll(lower, s, 1)
        upper = gamma * pltpu.roll(upper, n - s, 1)
        s *= 2
    return b / (lower + upper + excess)


def coarse_kernel_b(me, x1, ext, b, row_at, row_ok, same_col, h, y4, cross, chip, x3, to_cross, to_chip):
    before, after = sides(me, cross, chip)
    put = sender(me, to_cross, to_chip)
    cases, rows, width = x1.shape
    x = coarse_step(
        [x1[c] for c in range(cases)],
        [before[row_of(c)] for c in range(cases)],
        [after[row_of(c)] for c in range(cases)],
        ext, b, h, (row_at, row_ok, same_col),
    )
    for c in range(cases):
        x3[c] = x[c]
        put(flat_row(c), x[c][0:1], x[c][rows - 1 : rows])
    no_row = jnp.zeros((1, width), F32)
    put(flat_row(19), no_row, no_row)
    for j in range(5):
        y = y4[j]
        for k in range(3):
            put(response_row(k, j), y[k : k + 1], y[rows - 1 - k : rows - k])


def coarse_kernel_c(me, x3, ext, b, row_at, row_ok, same_col, h, smooth, cross, chip, part, v, to_cross, to_chip):
    before, after = sides(me, cross, chip)
    put = sender(me, to_cross, to_chip)
    cases, rows, width = x3.shape
    x = coarse_step(
        [x3[c] for c in range(cases)],
        [before[flat_row(c)] for c in range(cases)],
        [after[flat_row(c)] for c in range(cases)],
        ext, b, h, (row_at, row_ok, same_col),
    )
    for c in range(cases):
        y = smooth[c] + x[c]
        v[c] = y
        for k in range(3):
            put((k,) + row_of(c), y[k : k + 1], y[rows - 1 - k : rows - k])


def post_kernel(me, v, f, ext, cross, chip, cross_v, chip_v, q, part_a, part_e, out, gather):
    before, after = sides(me, cross, chip)
    before_v, after_v = sides(me, cross_v, chip_v)
    cases, rows, width = v.shape
    m = q.shape[0]
    diag = 4.0 + ext[...]
    fl = [f[c] for c in range(cases)]
    v_halo = [both(before_v, after_v, k) for k in range(3)]
    f_halo = [both(before, after, 3 + k) for k in range(2)]
    d_halo = [4.0 + spread(before, after, k, cases) for k in range(2)]
    valid = spread(before, after, 2, cases)
    x, res = two_sweeps([v[c] for c in range(cases)], v_halo, fl, f_halo, diag, d_halo, valid)
    for c in range(cases):
        out[c] = x[c]
    inv = []
    for j in range(m):
        d = part_e[:, LANE_D + j : LANE_D + j + 1]
        inv.append(jnp.where(d > 0.0, 1.0 / jnp.where(d > 0.0, d, 1.0), 0.0))
    values = []
    for c in range(cases):
        r = res[c]
        share = [dot(r, q[j]) * inv[j] for j in range(m)]
        for j in range(m):
            r = r - share[j] * q[j]
        values.append((LANE_PERP + c, dot(r, r)))
        for j in range(m):
            values.append((LANE_C + 8 * j + c, share[j]))
    row = part_a[...] + part_e[...] + lane_row(values)
    gather[...] = jnp.broadcast_to(row, gather.shape)


def ratio_kernel(groups, cases, cells, me, gathered, ratio, near):
    n = gathered.shape[0]
    m = 2 * REACH_E + 1
    g = jnp.transpose(gathered[...])
    e = solve_slabs(g, groups, cells)
    lane = lax.broadcasted_iota(jnp.int32, e.shape, 1)
    for j in range(m):
        at = lane == me[0] + j - REACH_E
        own = jnp.sum(jnp.where(at, e, 0.0), axis=1, keepdims=True)
        near[j] = jnp.broadcast_to(own, near.shape[1:])

    def shifted(j):
        inside = (lane + j >= 0) & (lane + j < n)
        return jnp.where(inside, pltpu.roll(e, (-j) % n, 1), 0.0)

    def spread_row(k):
        return jnp.broadcast_to(g[k : k + 1], e.shape)

    t = [e] + [shifted(j) - e for j in ORDER[1:]]
    norm = g[LANE_PERP : LANE_PERP + 8]
    for j in range(m):
        z = g[LANE_C + 8 * j : LANE_C + 8 * j + 8] + t[j]
        for k in range(j + 1, m):
            z = z + spread_row(LANE_L + FACTORS.index((j, k))) * t[k]
        norm = norm + spread_row(LANE_D + j) * (z * z)
    norm = jnp.sum(norm, axis=1, keepdims=True)
    load = jnp.sum(g[LANE_LOAD : LANE_LOAD + 8], axis=1, keepdims=True)
    case = lax.broadcasted_iota(jnp.int32, norm.shape, 0)
    r = jnp.sqrt(jnp.where(case < cases, norm, 0.0) / jnp.where(case < cases, load, 1.0))
    ratio[...] = jnp.broadcast_to(lane_row([(c, r[c : c + 1]) for c in range(cases)]), ratio.shape)


def final_kernel(me, base, phi, near, out):
    cases, rows, width = base.shape
    for c in range(cases):
        x = base[c]
        for j in range(phi.shape[0]):
            x = x + near[j, pl.ds(c, 1), 0:1] * phi[j]
        out[c] = x


def local(thermal_solution, heat_forcing, extinction_factor, cluster_label):
    cases, rows, width = thermal_solution.shape
    n = lax.axis_size("blk")
    n_rhs = lax.axis_size("rhs")
    groups = rows * width // 16
    field = (cases, rows, width)
    pairs = [(i, i + 1) for i in range(1, n - 1, 2)]
    cross_chip = pairs + [(j, i) for i, j in pairs]
    on_chip = [(i, i ^ 1) for i in range(n)]

    def exchange(cross, chip):
        cross = lax.ppermute(cross, "blk", cross_chip)
        return cross, lax.ppermute(chip, "blk", on_chip)

    edge = (cases, width)
    edges = (8, width)
    deep = (5, 4, width)
    cells = (rows, width)
    u, f, ext, lab = thermal_solution, heat_forcing, extinction_factor, cluster_label
    sent = vmem_call(
        pack_kernel,
        [(6, cases, width)] * 2,
        [
            pltpu.VMEM(field, F32),
            pltpu.VMEM(field, F32),
            pltpu.VMEM(cells, F32),
            pltpu.SemaphoreType.DMA((3,)),
        ],
        n_in=3,
        in_space=pl.ANY,
    )(u, f, ext)
    halo = exchange(*sent)
    shifts = len(offsets())
    *tables, y3 = vmem_call(
        functools.partial(table_kernel, n),
        [
            ((shifts, rows, width), jnp.int32),
            (shifts, rows, width),
            (rows - 1, rows, width),
            cells,
            (3, rows, width),
        ],
        n_in=2,
    )(ext, lab)
    call = vmem_call
    smooth, b, x0, *sent, rsum = call(
        pre_kernel, [field, field, field, edges, edges, (1, 128)], n_in=10
    )(u, f, ext, *halo, *tables, y3)
    rows_x = exchange(*sent)
    x1, *sent = call(coarse_kernel_a, [field, edge, edge], n_in=9)(
        x0, ext, b, *tables, *rows_x
    )
    (part_a,) = call(sum_kernel, [(1, 128)], n_in=4)(x1, ext, f, rsum)
    (y4,) = call(functools.partial(answer_kernel, cases), [(5, rows, width)], n_in=8)(
        ext, *tables, y3, *rows_x
    )
    rows_x = exchange(*sent)
    x3, *sent = call(coarse_kernel_b, [field, deep, deep], n_in=10)(
        x1, ext, b, *tables, y4, *rows_x
    )
    rows_x = exchange(*sent)
    m = 2 * REACH_E + 1
    phi, q, part_e = call(
        response_kernel, [(m, rows, width), (m, rows, width), (1, 128)], n_in=6
    )(ext, *halo, y4, *rows_x)
    v, *sent = call(
        coarse_kernel_c, [field, (3, cases, width), (3, cases, width)], n_in=11
    )(x3, ext, b, *tables, smooth, *rows_x, part_a)
    rows_x = exchange(*sent)
    base, mine = call(post_kernel, [field, (n, 128)], n_in=10)(
        v, f, ext, *halo, *rows_x, q, part_a, part_e
    )
    gathered = lax.all_to_all(mine, "blk", 0, 0, tiled=True)
    ratio, near = call(
        functools.partial(ratio_kernel, groups, cases, rows * width),
        [(n_rhs, 128), (m, 8, 128)],
        n_in=1,
    )(gathered)
    every = lax.all_to_all(ratio, "rhs", 0, 0, tiled=True)
    (corrected,) = call(final_kernel, [field], n_in=3)(base, phi, near)
    return corrected, every[:, :cases].reshape(n_rhs * cases)


def solution(mesh):
    in_specs = (P("rhs", "blk", None), P("rhs", "blk", None), P("blk", None), P("blk", None))
    out_specs = (P("rhs", "blk", None), P())
    return jax.shard_map(local, mesh=mesh, in_specs=in_specs, out_specs=out_specs, check_vma=False)
```

```python
import functools

import jax
import jax.numpy as jnp
from jax import lax
from jax.experimental import pallas as pl
from jax.experimental.pallas import tpu as pltpu
from jax.sharding import PartitionSpec as P

damping_fine = 0.8
damping_coarse = 0.5
REACH = 7
F32 = jnp.float32


VMEM = pl.BlockSpec(memory_space=pltpu.VMEM)


def with_place(body):
    def kernel(*refs):
        body((lax.axis_index("blk"), lax.axis_index("rhs")), *refs)

    return kernel


def vmem_call(body, outs, scratch=(), n_in=0, in_space=pltpu.VMEM):
    limit = 48 << 20 if in_space == pltpu.VMEM else 56_288_000
    return pl.pallas_call(
        with_place(body),
        out_shape=[
            jax.ShapeDtypeStruct(*(s if isinstance(s[0], tuple) else (s, F32))) for s in outs
        ],
        in_specs=[pl.BlockSpec(memory_space=in_space)] * n_in,
        out_specs=[VMEM] * len(outs),
        scratch_shapes=list(scratch),
        compiler_params=pltpu.CompilerParams(vmem_limit_bytes=limit),
    )


class View:
    def __init__(self, own_chip, cross, chip):
        self.own_chip = own_chip
        self.chip, self.cross = chip, cross

    def __getitem__(self, k):
        return jnp.where(self.own_chip, self.chip[k], self.cross[k])


def sides(me, cross, chip):
    odd = (me[0] & 1) == 1
    return View(odd, cross, chip), View(jnp.logical_not(odd), cross, chip)


def row_of(c):
    return (pl.ds(c, 1), slice(None))


def sender(me, cross, chip):
    odd = (me[0] & 1) == 1

    def put(k, first, last):
        chip[k] = jnp.where(odd, first, last)
        cross[k] = jnp.where(odd, last, first)

    return put


def iotas(shape):
    return (
        lax.broadcasted_iota(jnp.int32, shape, 0),
        lax.broadcasted_iota(jnp.int32, shape, 1),
    )


def sideways(x):
    rows, width = x.shape
    col = lax.broadcasted_iota(jnp.int32, x.shape, 1)
    left = jnp.where(col == 0, 0.0, pltpu.roll(x, 1, 1))
    right = jnp.where(col == width - 1, 0.0, pltpu.roll(x, width - 1, 1))
    return left + right


def neighbours(x, above, below):
    rows = x.shape[0]
    row = lax.broadcasted_iota(jnp.int32, x.shape, 0)
    up = jnp.where(row == 0, above, pltpu.roll(x, 1, 0))
    down = jnp.where(row == rows - 1, below, pltpu.roll(x, rows - 1, 0))
    return up + down + sideways(x)


def offsets():
    return [d for d in range(-REACH, REACH + 1) if d]


def seg_sum(fields, tables):
    row_at, row_ok, same_col = tables
    rows, width = fields[0].shape
    col = list(fields)
    for k in range(1, rows):
        m = same_col[k - 1]
        col = [s + m * pltpu.roll(w, k, 0) for s, w in zip(col, fields)]
    out = list(col)
    for d, dx in enumerate(offsets()):
        at, ok = row_at[d], row_ok[d]
        out = [
            t
            + ok
            * jnp.take_along_axis(
                pltpu.roll(s, (-dx) % width, 1), at, axis=0, mode="promise_in_bounds"
            )
            for t, s in zip(out, col)
        ]
    return out


def table_kernel(n, me, ext, lab, row_at, row_ok, same_col, h, y3):
    key = lab[...]
    rows, width = key.shape
    for k in range(1, rows):
        same_col[k - 1] = jnp.where(pltpu.roll(key, k, 0) == key, 1.0, 0.0)
    for d, dx in enumerate(offsets()):
        there = pltpu.roll(key, (-dx) % width, 1)
        at = jnp.full(key.shape, -1, jnp.int32)
        for r in range(rows):
            at = jnp.where(jnp.broadcast_to(there[r : r + 1], key.shape) == key, r, at)
        row_ok[d] = jnp.where(at >= 0, 1.0, 0.0)
        row_at[d] = jnp.maximum(at, 0)
    row, col = iotas(key.shape)
    one = jnp.ones(key.shape, F32)
    zero = jnp.zeros(key.shape, F32)
    m = jnp.where((pltpu.roll(key, 1, 0) == key) & (row > 0), one, zero)
    m = m + jnp.where((pltpu.roll(key, rows - 1, 0) == key) & (row < rows - 1), one, zero)
    m = m + jnp.where((pltpu.roll(key, 1, 1) == key) & (col > 0), one, zero)
    m = m + jnp.where((pltpu.roll(key, width - 1, 1) == key) & (col < width - 1), one, zero)
    above = jnp.where(me[0] > 0, 1.0, 0.0)
    below = jnp.where(me[0] < n - 1, 1.0, 0.0)
    top = jnp.where(row == 0, one, zero)
    bottom = jnp.where(row == rows - 1, one, zero)
    open_sides = open_weight(ext[...])
    diag1, s_top, s_own, s_bottom = seg_sum(
        [4.0 + ext[...] - m, top, open_sides, bottom], (row_at, row_ok, same_col)
    )
    half = damping_coarse / diag1
    h[...] = half
    y3[0] = above * (half * s_top)
    y3[1] = 1.0 - half * s_own
    y3[2] = below * (half * s_bottom)


def open_weight(ext):
    rows, width = ext.shape
    row, col = iotas(ext.shape)
    one = jnp.ones(ext.shape, F32)
    zero = jnp.zeros(ext.shape, F32)
    weight = ext
    for at_edge in (row == 0, row == rows - 1, col == 0, col == width - 1):
        weight = weight + jnp.where(at_edge, one, zero)
    return weight


GROUP_EXT = 5


def pack_kernel(me, u_hbm, f_hbm, ext_hbm, cross, chip, u, f, ext, sem):
    pairs = ((u_hbm, u), (f_hbm, f), (ext_hbm, ext))
    copies = [pltpu.make_async_copy(src, dst, sem.at[k]) for k, (src, dst) in enumerate(pairs)]
    for copy in copies:
        copy.start()
    for copy in copies:
        copy.wait()
    cases, rows, width = u.shape
    put = sender(me, cross, chip)
    ones = jnp.ones((1, width), F32)
    end = rows - 1
    for k in range(3):
        put(k, u[:, k, :], u[:, end - k, :])
    for k in range(2):
        put(3 + k, f[:, k, :], f[:, end - k, :])
        at = (GROUP_EXT,) + row_of(k)
        put(at, ext[pl.ds(k, 1), :], ext[pl.ds(end - k, 1), :])
    for k in range(2, cases):
        put((GROUP_EXT,) + row_of(k), ones, ones)


def both(before, after, k):
    return jnp.concatenate([before[k], after[k]], axis=0)


def spread(before, after, k, times):
    at = (GROUP_EXT,) + row_of(k)
    up, down = before[at], after[at]
    shape = (times, up.shape[1])
    return jnp.concatenate([jnp.broadcast_to(up, shape), jnp.broadcast_to(down, shape)], axis=0)


def two_sweeps(u, u_halo, f, f_halo, diag, diag_halo, valid):
    cases = len(u)
    rows = u[0].shape[0]
    gain = damping_fine / diag
    gain_halo = [damping_fine / d for d in diag_halo]
    keep = 1.0 - damping_fine

    def edge(x):
        return jnp.concatenate([v[0:1] for v in x] + [v[rows - 1 : rows] for v in x], axis=0)

    def around(x, halo, c):
        return neighbours(x[c], halo[0][c : c + 1], halo[0][cases + c : cases + c + 1])

    def sweep(x, halo, depth):
        new = []
        for c in range(cases):
            push = around(x, halo, c)
            new.append(keep * x[c] + gain * (push if f is None else f[c] + push))
        inner = [edge(x)] + halo
        new_halo = []
        for k in range(depth):
            push = inner[k] + inner[k + 2] + sideways(halo[k])
            push = push if f is None else f_halo[k] + push
            new_halo.append((keep * halo[k] + gain_halo[k] * push) * valid)
        return new, new_halo

    x, h = sweep(u, u_halo, 2)
    x, h = sweep(x, h, 1)
    res = []
    for c in range(cases):
        r = around(x, h, c) - diag * x[c]
        res.append(r if f is None else f[c] + r)
    return x, res


def total(x):
    rows, width = x.shape
    part = x[:, 0:128]
    for k in range(1, width // 128):
        part = part + x[:, k * 128 : (k + 1) * 128]
    return jnp.sum(jnp.sum(part, axis=1, keepdims=True), axis=0, keepdims=True)


def lane_row(values):
    lane = lax.broadcasted_iota(jnp.int32, (1, 128), 1)
    row = jnp.zeros((1, 128), F32)
    for k, v in values:
        row = jnp.where(lane == k, v, row)
    return row


def pre_kernel(me, u, f, ext, cross, chip, row_at, row_ok, same_col, h, y3, smooth, b, x0, to_cross, to_chip, rsum):
    before, after = sides(me, cross, chip)
    put = sender(me, to_cross, to_chip)
    cases, rows, width = u.shape
    diag = 4.0 + ext[...]
    us = [u[c] for c in range(cases)]
    fl = [f[c] for c in range(cases)]
    u_halo = [both(before, after, k) for k in range(3)]
    f_halo = [both(before, after, 3 + k) for k in range(2)]
    d_halo = [4.0 + spread(before, after, k, cases) for k in range(2)]
    valid = spread(before, after, 2, cases)
    x, res = two_sweeps(us, u_halo, fl, f_halo, diag, d_halo, valid)
    for c in range(cases):
        smooth[c] = x[c]
    sums = seg_sum(res, (row_at, row_ok, same_col))
    for c in range(cases):
        b[c] = sums[c]
        v = h[...] * sums[c]
        x0[c] = v
        put(row_of(c), v[0:1], v[rows - 1 : rows])
    for j in range(3):
        y = y3[j]
        put(row_of(cases + j), y[0:1], y[rows - 1 : rows])
    put(row_of(cases + 3), jnp.zeros((1, width), F32), jnp.zeros((1, width), F32))
    rsum[...] = lane_row([(c, total(res[c])) for c in range(cases)])


def coarse_step(x, above, below, ext, b, h, tables):
    cases = len(x)
    diag = 4.0 + ext[...]
    w = [diag * x[c] - neighbours(x[c], above[c], below[c]) for c in range(cases)]
    sums = seg_sum(w, tables)
    return [x[c] + h[...] * (b[c] - sums[c]) for c in range(cases)]


def flat_row(r):
    return (r // 4,) + row_of(r % 4)


def response_row(k, j):
    return flat_row(4 + 5 * k + j)


def coarse_kernel_a(me, x0, ext, b, row_at, row_ok, same_col, h, cross, chip, x1, to_cross, to_chip):
    before, after = sides(me, cross, chip)
    put = sender(me, to_cross, to_chip)
    cases, rows, width = x0.shape
    x = coarse_step(
        [x0[c] for c in range(cases)],
        [before[row_of(c)] for c in range(cases)],
        [after[row_of(c)] for c in range(cases)],
        ext, b, h, (row_at, row_ok, same_col),
    )
    for c in range(cases):
        x1[c] = x[c]
        put(row_of(c), x[c][0:1], x[c][rows - 1 : rows])


def sum_kernel(me, x1, ext, f, rsum, part):
    cases, rows, width = x1.shape
    weight = open_weight(ext[...])
    values = [(LANE_EXT, total(ext[...]))]
    for c in range(cases):
        x = x1[c]
        values.append((LANE_OWN + c, rsum[:, c : c + 1] - total(weight * x)))
        values.append((LANE_TOP + c, total(x[0:1])))
        values.append((LANE_BOTTOM + c, total(x[rows - 1 : rows])))
        values.append((LANE_LOAD + c, dot(f[c], f[c])))
    part[...] = lane_row(values)


def answer_kernel(cases, me, ext, row_at, row_ok, same_col, h, y3, cross, chip, y4):
    before, after = sides(me, cross, chip)
    rows, width = ext.shape
    none = jnp.zeros((rows, width), F32)
    no_row = jnp.zeros((1, width), F32)
    above = [before[row_of(cases + j)] for j in range(3)] + [no_row, no_row]
    below = [no_row, no_row] + [after[row_of(cases + j)] for j in range(3)]
    y = coarse_step(
        [none] + [y3[j] for j in range(3)] + [none],
        above, below, ext, [none] * 5, h, (row_at, row_ok, same_col),
    )
    for j in range(5):
        y4[j] = y[j]


REACH_E = 3
ORDER = [0, -1, 1, -2, 2, -3, 3]
LANE_OWN, LANE_TOP, LANE_BOTTOM, LANE_EXT, LANE_D = 0, 8, 16, 24, 25
LANE_PERP, LANE_LOAD, LANE_C, LANE_L = 32, 40, 48, 104
FACTORS = [(j, k) for j in range(7) for k in range(j + 1, 7)]


def dot(x, y):
    return total(x * y)


def response_kernel(me, ext, cross, chip, y4, cross_y, chip_y, phi, q, part):
    before, after = sides(me, cross, chip)
    ab, be = sides(me, cross_y, chip_y)
    rows, width = ext.shape
    m = 2 * REACH_E + 1
    diag = 4.0 + ext[...]
    none = jnp.zeros((rows, width), F32)
    fields = [none] + [y4[j] for j in range(5)] + [none]
    two_rows = jnp.zeros((2, width), F32)
    halo = []
    for k in range(3):
        up = [ab[response_row(k, j)] for j in range(5)]
        down = [be[response_row(k, j)] for j in range(5)]
        halo.append(jnp.concatenate(up + [two_rows, two_rows] + down, axis=0))

    d_halo = [4.0 + spread(before, after, k, m) for k in range(2)]
    x, res = two_sweeps(fields, halo, None, None, diag, d_halo, spread(before, after, 2, m))
    for j in range(m):
        phi[j] = x[j]
    every = res[0]
    for j in range(1, m):
        every = every + res[j]
    basis = [every] + [res[REACH_E + j] for j in ORDER[1:]]
    values = []
    for j in range(m):
        v = basis[j]
        q[j] = v
        d = dot(v, v)
        inv = jnp.where(d > 0.0, 1.0 / jnp.where(d > 0.0, d, 1.0), 0.0)
        values.append((LANE_D + j, d))
        for k in range(j + 1, m):
            factor = dot(v, basis[k]) * inv
            values.append((LANE_L + FACTORS.index((j, k)), factor))
            basis[k] = basis[k] - factor * v
    part[...] = lane_row(values)


def solve_slabs(g, groups, cells):
    own, top, bottom = (g[k : k + 8] for k in (LANE_OWN, LANE_TOP, LANE_BOTTOM))
    n = own.shape[1]
    lane = lax.broadcasted_iota(jnp.int32, own.shape, 1)
    b = own + jnp.where(lane == n - 1, 0.0, pltpu.roll(top, n - 1, 1))
    b = b + jnp.where(lane == 0, 0.0, pltpu.roll(bottom, 1, 1))
    b = b / (groups * float(n))
    mean = jnp.broadcast_to(g[LANE_EXT : LANE_EXT + 1], own.shape) / float(cells)
    d = 2.0 + mean / (float(n) * float(n))
    lower = jnp.where(lane == 0, 0.0, 1.0)
    upper = jnp.where(lane == n - 1, 0.0, 1.0)
    excess = (d - lower) - upper
    s = 1
    while s < n:
        inv = 1.0 / (lower + upper + excess)
        alpha = lower * pltpu.roll(inv, s, 1)
        gamma = upper * pltpu.roll(inv, n - s, 1)
        b = b + alpha * pltpu.roll(b, s, 1) + gamma * pltpu.roll(b, n - s, 1)
        excess = excess + alpha * pltpu.roll(excess, s, 1) + gamma * pltpu.roll(excess, n - s, 1)
        lower = alpha * pltpu.roll(lower, s, 1)
        upper = gamma * pltpu.roll(upper, n - s, 1)
        s *= 2
    return b / (lower + upper + excess)


def coarse_kernel_b(me, x1, ext, b, row_at, row_ok, same_col, h, y4, cross, chip, x3, to_cross, to_chip):
    before, after = sides(me, cross, chip)
    put = sender(me, to_cross, to_chip)
    cases, rows, width = x1.shape
    x = coarse_step(
        [x1[c] for c in range(cases)],
        [before[row_of(c)] for c in range(cases)],
        [after[row_of(c)] for c in range(cases)],
        ext, b, h, (row_at, row_ok, same_col),
    )
    for c in range(cases):
        x3[c] = x[c]
        put(flat_row(c), x[c][0:1], x[c][rows - 1 : rows])
    no_row = jnp.zeros((1, width), F32)
    put(flat_row(19), no_row, no_row)
    for j in range(5):
        y = y4[j]
        for k in range(3):
            put(response_row(k, j), y[k : k + 1], y[rows - 1 - k : rows - k])


def coarse_kernel_c(me, x3, ext, b, row_at, row_ok, same_col, h, smooth, cross, chip, part, v, to_cross, to_chip):
    before, after = sides(me, cross, chip)
    put = sender(me, to_cross, to_chip)
    cases, rows, width = x3.shape
    x = coarse_step(
        [x3[c] for c in range(cases)],
        [before[flat_row(c)] for c in range(cases)],
        [after[flat_row(c)] for c in range(cases)],
        ext, b, h, (row_at, row_ok, same_col),
    )
    for c in range(cases):
        y = smooth[c] + x[c]
        v[c] = y
        for k in range(3):
            put((k,) + row_of(c), y[k : k + 1], y[rows - 1 - k : rows - k])


def post_kernel(me, v, f, ext, cross, chip, cross_v, chip_v, q, part_a, part_e, out, gather):
    before, after = sides(me, cross, chip)
    before_v, after_v = sides(me, cross_v, chip_v)
    cases, rows, width = v.shape
    m = q.shape[0]
    diag = 4.0 + ext[...]
    fl = [f[c] for c in range(cases)]
    v_halo = [both(before_v, after_v, k) for k in range(3)]
    f_halo = [both(before, after, 3 + k) for k in range(2)]
    d_halo = [4.0 + spread(before, after, k, cases) for k in range(2)]
    valid = spread(before, after, 2, cases)
    x, res = two_sweeps([v[c] for c in range(cases)], v_halo, fl, f_halo, diag, d_halo, valid)
    for c in range(cases):
        out[c] = x[c]
    inv = []
    for j in range(m):
        d = part_e[:, LANE_D + j : LANE_D + j + 1]
        inv.append(jnp.where(d > 0.0, 1.0 / jnp.where(d > 0.0, d, 1.0), 0.0))
    values = []
    for c in range(cases):
        r = res[c]
        share = [dot(r, q[j]) * inv[j] for j in range(m)]
        for j in range(m):
            r = r - share[j] * q[j]
        values.append((LANE_PERP + c, dot(r, r)))
        for j in range(m):
            values.append((LANE_C + 8 * j + c, share[j]))
    row = part_a[...] + part_e[...] + lane_row(values)
    gather[...] = jnp.broadcast_to(row, gather.shape)


def ratio_kernel(groups, cases, cells, me, gathered, ratio, near):
    n = gathered.shape[0]
    m = 2 * REACH_E + 1
    g = jnp.transpose(gathered[...])
    e = solve_slabs(g, groups, cells)
    lane = lax.broadcasted_iota(jnp.int32, e.shape, 1)
    for j in range(m):
        at = lane == me[0] + j - REACH_E
        own = jnp.sum(jnp.where(at, e, 0.0), axis=1, keepdims=True)
        near[j] = jnp.broadcast_to(own, near.shape[1:])

    def shifted(j):
        inside = (lane + j >= 0) & (lane + j < n)
        return jnp.where(inside, pltpu.roll(e, (-j) % n, 1), 0.0)

    def spread_row(k):
        return jnp.broadcast_to(g[k : k + 1], e.shape)

    t = [e] + [shifted(j) - e for j in ORDER[1:]]
    norm = g[LANE_PERP : LANE_PERP + 8]
    for j in range(m):
        z = g[LANE_C + 8 * j : LANE_C + 8 * j + 8] + t[j]
        for k in range(j + 1, m):
            z = z + spread_row(LANE_L + FACTORS.index((j, k))) * t[k]
        norm = norm + spread_row(LANE_D + j) * (z * z)
    norm = jnp.sum(norm, axis=1, keepdims=True)
    load = jnp.sum(g[LANE_LOAD : LANE_LOAD + 8], axis=1, keepdims=True)
    case = lax.broadcasted_iota(jnp.int32, norm.shape, 0)
    r = jnp.sqrt(jnp.where(case < cases, norm, 0.0) / jnp.where(case < cases, load, 1.0))
    ratio[...] = jnp.broadcast_to(lane_row([(c, r[c : c + 1]) for c in range(cases)]), ratio.shape)


def final_kernel(me, base, phi, near, out):
    cases, rows, width = base.shape
    for c in range(cases):
        x = base[c]
        for j in range(phi.shape[0]):
            x = x + near[j, pl.ds(c, 1), 0:1] * phi[j]
        out[c] = x


def local(thermal_solution, heat_forcing, extinction_factor, cluster_label):
    cases, rows, width = thermal_solution.shape
    n = lax.axis_size("blk")
    n_rhs = lax.axis_size("rhs")
    groups = rows * width // 16
    field = (cases, rows, width)
    pairs = [(i, i + 1) for i in range(1, n - 1, 2)]
    cross_chip = pairs + [(j, i) for i, j in pairs]
    on_chip = [(i, i ^ 1) for i in range(n)]

    def exchange(cross, chip):
        cross = lax.ppermute(cross, "blk", cross_chip)
        return cross, lax.ppermute(chip, "blk", on_chip)

    edge = (cases, width)
    edges = (8, width)
    deep = (5, 4, width)
    cells = (rows, width)
    u, f, ext, lab = thermal_solution, heat_forcing, extinction_factor, cluster_label
    sent = vmem_call(
        pack_kernel,
        [(6, cases, width)] * 2,
        [
            pltpu.VMEM(field, F32),
            pltpu.VMEM(field, F32),
            pltpu.VMEM(cells, F32),
            pltpu.SemaphoreType.DMA((3,)),
        ],
        n_in=3,
        in_space=pl.ANY,
    )(u, f, ext)
    halo = exchange(*sent)
    shifts = len(offsets())
    *tables, y3 = vmem_call(
        functools.partial(table_kernel, n),
        [
            ((shifts, rows, width), jnp.int32),
            (shifts, rows, width),
            (rows - 1, rows, width),
            cells,
            (3, rows, width),
        ],
        n_in=2,
    )(ext, lab)
    call = vmem_call
    smooth, b, x0, *sent, rsum = call(
        pre_kernel, [field, field, field, edges, edges, (1, 128)], n_in=10
    )(u, f, ext, *halo, *tables, y3)
    rows_x = exchange(*sent)
    x1, *sent = call(coarse_kernel_a, [field, edge, edge], n_in=9)(
        x0, ext, b, *tables, *rows_x
    )
    (part_a,) = call(sum_kernel, [(1, 128)], n_in=4)(x1, ext, f, rsum)
    (y4,) = call(functools.partial(answer_kernel, cases), [(5, rows, width)], n_in=8)(
        ext, *tables, y3, *rows_x
    )
    rows_x = exchange(*sent)
    x3, *sent = call(coarse_kernel_b, [field, deep, deep], n_in=10)(
        x1, ext, b, *tables, y4, *rows_x
    )
    rows_x = exchange(*sent)
    m = 2 * REACH_E + 1
    phi, q, part_e = call(
        response_kernel, [(m, rows, width), (m, rows, width), (1, 128)], n_in=6
    )(ext, *halo, y4, *rows_x)
    v, *sent = call(
        coarse_kernel_c, [field, (3, cases, width), (3, cases, width)], n_in=11
    )(x3, ext, b, *tables, smooth, *rows_x, part_a)
    rows_x = exchange(*sent)
    base, mine = call(post_kernel, [field, (n, 128)], n_in=10)(
        v, f, ext, *halo, *rows_x, q, part_a, part_e
    )
    gathered = lax.all_to_all(mine, "blk", 0, 0, tiled=True)
    ratio, near = call(
        functools.partial(ratio_kernel, groups, cases, rows * width),
        [(n_rhs, 128), (m, 8, 128)],
        n_in=1,
    )(gathered)
    every = lax.all_to_all(ratio, "rhs", 0, 0, tiled=True)
    (corrected,) = call(final_kernel, [field], n_in=3)(base, phi, near)
    return corrected, every[:, :cases].reshape(n_rhs * cases)


def solution(mesh):
    in_specs = (P("rhs", "blk", None), P("rhs", "blk", None), P("blk", None), P("blk", None))
    out_specs = (P("rhs", "blk", None), P())
    return jax.shard_map(local, mesh=mesh, in_specs=in_specs, out_specs=out_specs, check_vma=False)
```

```python
import functools

import jax
import jax.numpy as jnp
from jax import lax
from jax.experimental import pallas as pl
from jax.experimental.pallas import tpu as pltpu
from jax.sharding import PartitionSpec as P

damping_fine = 0.8
damping_coarse = 0.5
REACH = 7
F32 = jnp.float32


VMEM = pl.BlockSpec(memory_space=pltpu.VMEM)


def with_place(body):
    def kernel(*refs):
        body((lax.axis_index("blk"), lax.axis_index("rhs")), *refs)

    return kernel


def vmem_call(body, outs, scratch=(), n_in=0, in_space=pltpu.VMEM):
    limit = 48 << 20 if in_space == pltpu.VMEM else 56_288_000
    return pl.pallas_call(
        with_place(body),
        out_shape=[
            jax.ShapeDtypeStruct(*(s if isinstance(s[0], tuple) else (s, F32))) for s in outs
        ],
        in_specs=[pl.BlockSpec(memory_space=in_space)] * n_in,
        out_specs=[VMEM] * len(outs),
        scratch_shapes=list(scratch),
        compiler_params=pltpu.CompilerParams(vmem_limit_bytes=limit),
    )


class View:
    def __init__(self, own_chip, cross, chip):
        self.own_chip = own_chip
        self.chip, self.cross = chip, cross

    def __getitem__(self, k):
        return jnp.where(self.own_chip, self.chip[k], self.cross[k])


def sides(me, cross, chip):
    odd = (me[0] & 1) == 1
    return View(odd, cross, chip), View(jnp.logical_not(odd), cross, chip)


def row_of(c):
    return (pl.ds(c, 1), slice(None))


def sender(me, cross, chip):
    odd = (me[0] & 1) == 1

    def put(k, first, last):
        chip[k] = jnp.where(odd, first, last)
        cross[k] = jnp.where(odd, last, first)

    return put


def iotas(shape):
    return (
        lax.broadcasted_iota(jnp.int32, shape, 0),
        lax.broadcasted_iota(jnp.int32, shape, 1),
    )


def sideways(x):
    rows, width = x.shape
    col = lax.broadcasted_iota(jnp.int32, x.shape, 1)
    left = jnp.where(col == 0, 0.0, pltpu.roll(x, 1, 1))
    right = jnp.where(col == width - 1, 0.0, pltpu.roll(x, width - 1, 1))
    return left + right


def neighbours(x, above, below):
    rows = x.shape[0]
    row = lax.broadcasted_iota(jnp.int32, x.shape, 0)
    up = jnp.where(row == 0, above, pltpu.roll(x, 1, 0))
    down = jnp.where(row == rows - 1, below, pltpu.roll(x, rows - 1, 0))
    return up + down + sideways(x)


def offsets():
    return [d for d in range(-REACH, REACH + 1) if d]


def seg_sum(fields, tables):
    row_at, row_ok, same_col = tables
    rows, width = fields[0].shape
    col = list(fields)
    for k in range(1, rows):
        m = same_col[k - 1]
        col = [s + m * pltpu.roll(w, k, 0) for s, w in zip(col, fields)]
    out = list(col)
    for d, dx in enumerate(offsets()):
        at, ok = row_at[d], row_ok[d]
        out = [
            t
            + ok
            * jnp.take_along_axis(
                pltpu.roll(s, (-dx) % width, 1), at, axis=0, mode="promise_in_bounds"
            )
            for t, s in zip(out, col)
        ]
    return out


def table_kernel(n, me, ext, lab, row_at, row_ok, same_col, h, y3):
    key = lab[...]
    rows, width = key.shape
    for k in range(1, rows):
        same_col[k - 1] = jnp.where(pltpu.roll(key, k, 0) == key, 1.0, 0.0)
    for d, dx in enumerate(offsets()):
        there = pltpu.roll(key, (-dx) % width, 1)
        at = jnp.full(key.shape, -1, jnp.int32)
        for r in range(rows):
            at = jnp.where(jnp.broadcast_to(there[r : r + 1], key.shape) == key, r, at)
        row_ok[d] = jnp.where(at >= 0, 1.0, 0.0)
        row_at[d] = jnp.maximum(at, 0)
    row, col = iotas(key.shape)
    one = jnp.ones(key.shape, F32)
    zero = jnp.zeros(key.shape, F32)
    m = jnp.where((pltpu.roll(key, 1, 0) == key) & (row > 0), one, zero)
    m = m + jnp.where((pltpu.roll(key, rows - 1, 0) == key) & (row < rows - 1), one, zero)
    m = m + jnp.where((pltpu.roll(key, 1, 1) == key) & (col > 0), one, zero)
    m = m + jnp.where((pltpu.roll(key, width - 1, 1) == key) & (col < width - 1), one, zero)
    above = jnp.where(me[0] > 0, 1.0, 0.0)
    below = jnp.where(me[0] < n - 1, 1.0, 0.0)
    top = jnp.where(row == 0, one, zero)
    bottom = jnp.where(row == rows - 1, one, zero)
    open_sides = open_weight(ext[...])
    diag1, s_top, s_own, s_bottom = seg_sum(
        [4.0 + ext[...] - m, top, open_sides, bottom], (row_at, row_ok, same_col)
    )
    half = damping_coarse / diag1
    h[...] = half
    y3[0] = above * (half * s_top)
    y3[1] = 1.0 - half * s_own
    y3[2] = below * (half * s_bottom)


def open_weight(ext):
    rows, width = ext.shape
    row, col = iotas(ext.shape)
    one = jnp.ones(ext.shape, F32)
    zero = jnp.zeros(ext.shape, F32)
    weight = ext
    for at_edge in (row == 0, row == rows - 1, col == 0, col == width - 1):
        weight = weight + jnp.where(at_edge, one, zero)
    return weight


GROUP_EXT = 5


def pack_kernel(me, u_hbm, f_hbm, ext_hbm, cross, chip, u, f, ext, sem):
    pairs = ((u_hbm, u), (f_hbm, f), (ext_hbm, ext))
    copies = [pltpu.make_async_copy(src, dst, sem.at[k]) for k, (src, dst) in enumerate(pairs)]
    for copy in copies:
        copy.start()
    for copy in copies:
        copy.wait()
    cases, rows, width = u.shape
    put = sender(me, cross, chip)
    ones = jnp.ones((1, width), F32)
    end = rows - 1
    for k in range(3):
        put(k, u[:, k, :], u[:, end - k, :])
    for k in range(2):
        put(3 + k, f[:, k, :], f[:, end - k, :])
        at = (GROUP_EXT,) + row_of(k)
        put(at, ext[pl.ds(k, 1), :], ext[pl.ds(end - k, 1), :])
    for k in range(2, cases):
        put((GROUP_EXT,) + row_of(k), ones, ones)


def both(before, after, k):
    return jnp.concatenate([before[k], after[k]], axis=0)


def spread(before, after, k, times):
    at = (GROUP_EXT,) + row_of(k)
    up, down = before[at], after[at]
    shape = (times, up.shape[1])
    return jnp.concatenate([jnp.broadcast_to(up, shape), jnp.broadcast_to(down, shape)], axis=0)


def two_sweeps(u, u_halo, f, f_halo, diag, diag_halo, valid):
    cases = len(u)
    rows = u[0].shape[0]
    gain = damping_fine / diag
    gain_halo = [damping_fine / d for d in diag_halo]
    keep = 1.0 - damping_fine

    def edge(x):
        return jnp.concatenate([v[0:1] for v in x] + [v[rows - 1 : rows] for v in x], axis=0)

    def around(x, halo, c):
        return neighbours(x[c], halo[0][c : c + 1], halo[0][cases + c : cases + c + 1])

    def sweep(x, halo, depth):
        new = []
        for c in range(cases):
            push = around(x, halo, c)
            new.append(keep * x[c] + gain * (push if f is None else f[c] + push))
        inner = [edge(x)] + halo
        new_halo = []
        for k in range(depth):
            push = inner[k] + inner[k + 2] + sideways(halo[k])
            push = push if f is None else f_halo[k] + push
            new_halo.append((keep * halo[k] + gain_halo[k] * push) * valid)
        return new, new_halo

    x, h = sweep(u, u_halo, 2)
    x, h = sweep(x, h, 1)
    res = []
    for c in range(cases):
        r = around(x, h, c) - diag * x[c]
        res.append(r if f is None else f[c] + r)
    return x, res


def total(x):
    rows, width = x.shape
    part = x[:, 0:128]
    for k in range(1, width // 128):
        part = part + x[:, k * 128 : (k + 1) * 128]
    return jnp.sum(jnp.sum(part, axis=1, keepdims=True), axis=0, keepdims=True)


def lane_row(values):
    lane = lax.broadcasted_iota(jnp.int32, (1, 128), 1)
    row = jnp.zeros((1, 128), F32)
    for k, v in values:
        row = jnp.where(lane == k, v, row)
    return row


def pre_kernel(me, u, f, ext, cross, chip, row_at, row_ok, same_col, h, y3, smooth, b, x0, to_cross, to_chip, rsum):
    before, after = sides(me, cross, chip)
    put = sender(me, to_cross, to_chip)
    cases, rows, width = u.shape
    diag = 4.0 + ext[...]
    us = [u[c] for c in range(cases)]
    fl = [f[c] for c in range(cases)]
    u_halo = [both(before, after, k) for k in range(3)]
    f_halo = [both(before, after, 3 + k) for k in range(2)]
    d_halo = [4.0 + spread(before, after, k, cases) for k in range(2)]
    valid = spread(before, after, 2, cases)
    x, res = two_sweeps(us, u_halo, fl, f_halo, diag, d_halo, valid)
    for c in range(cases):
        smooth[c] = x[c]
    sums = seg_sum(res, (row_at, row_ok, same_col))
    for c in range(cases):
        b[c] = sums[c]
        v = h[...] * sums[c]
        x0[c] = v
        put(row_of(c), v[0:1], v[rows - 1 : rows])
    for j in range(3):
        y = y3[j]
        put(row_of(cases + j), y[0:1], y[rows - 1 : rows])
    put(row_of(cases + 3), jnp.zeros((1, width), F32), jnp.zeros((1, width), F32))
    rsum[...] = lane_row([(c, total(res[c])) for c in range(cases)])


def coarse_step(x, above, below, ext, b, h, tables):
    cases = len(x)
    diag = 4.0 + ext[...]
    w = [diag * x[c] - neighbours(x[c], above[c], below[c]) for c in range(cases)]
    sums = seg_sum(w, tables)
    return [x[c] + h[...] * (b[c] - sums[c]) for c in range(cases)]


def flat_row(r):
    return (r // 4,) + row_of(r % 4)


def response_row(k, j):
    return flat_row(4 + 5 * k + j)


def coarse_kernel_a(me, x0, ext, b, row_at, row_ok, same_col, h, cross, chip, x1, to_cross, to_chip):
    before, after = sides(me, cross, chip)
    put = sender(me, to_cross, to_chip)
    cases, rows, width = x0.shape
    x = coarse_step(
        [x0[c] for c in range(cases)],
        [before[row_of(c)] for c in range(cases)],
        [after[row_of(c)] for c in range(cases)],
        ext, b, h, (row_at, row_ok, same_col),
    )
    for c in range(cases):
        x1[c] = x[c]
        put(row_of(c), x[c][0:1], x[c][rows - 1 : rows])


def sum_kernel(me, x1, ext, f, rsum, part):
    cases, rows, width = x1.shape
    weight = open_weight(ext[...])
    values = [(LANE_EXT, total(ext[...]))]
    for c in range(cases):
        x = x1[c]
        values.append((LANE_OWN + c, rsum[:, c : c + 1] - total(weight * x)))
        values.append((LANE_TOP + c, total(x[0:1])))
        values.append((LANE_BOTTOM + c, total(x[rows - 1 : rows])))
        values.append((LANE_LOAD + c, dot(f[c], f[c])))
    part[...] = lane_row(values)


def answer_kernel(cases, me, ext, row_at, row_ok, same_col, h, y3, cross, chip, y4):
    before, after = sides(me, cross, chip)
    rows, width = ext.shape
    none = jnp.zeros((rows, width), F32)
    no_row = jnp.zeros((1, width), F32)
    above = [before[row_of(cases + j)] for j in range(3)] + [no_row, no_row]
    below = [no_row, no_row] + [after[row_of(cases + j)] for j in range(3)]
    y = coarse_step(
        [none] + [y3[j] for j in range(3)] + [none],
        above, below, ext, [none] * 5, h, (row_at, row_ok, same_col),
    )
    for j in range(5):
        y4[j] = y[j]


REACH_E = 3
ORDER = [0, -1, 1, -2, 2, -3, 3]
LANE_OWN, LANE_TOP, LANE_BOTTOM, LANE_EXT, LANE_D = 0, 8, 16, 24, 25
LANE_PERP, LANE_LOAD, LANE_C, LANE_L = 32, 40, 48, 104
FACTORS = [(j, k) for j in range(7) for k in range(j + 1, 7)]


def dot(x, y):
    return total(x * y)


def response_kernel(me, ext, cross, chip, y4, cross_y, chip_y, phi, q, part):
    before, after = sides(me, cross, chip)
    ab, be = sides(me, cross_y, chip_y)
    rows, width = ext.shape
    m = 2 * REACH_E + 1
    diag = 4.0 + ext[...]
    none = jnp.zeros((rows, width), F32)
    fields = [none] + [y4[j] for j in range(5)] + [none]
    two_rows = jnp.zeros((2, width), F32)
    halo = []
    for k in range(3):
        up = [ab[response_row(k, j)] for j in range(5)]
        down = [be[response_row(k, j)] for j in range(5)]
        halo.append(jnp.concatenate(up + [two_rows, two_rows] + down, axis=0))

    d_halo = [4.0 + spread(before, after, k, m) for k in range(2)]
    x, res = two_sweeps(fields, halo, None, None, diag, d_halo, spread(before, after, 2, m))
    for j in range(m):
        phi[j] = x[j]
    every = res[0]
    for j in range(1, m):
        every = every + res[j]
    basis = [every] + [res[REACH_E + j] for j in ORDER[1:]]
    values = []
    for j in range(m):
        v = basis[j]
        q[j] = v
        d = dot(v, v)
        inv = jnp.where(d > 0.0, 1.0 / jnp.where(d > 0.0, d, 1.0), 0.0)
        values.append((LANE_D + j, d))
        for k in range(j + 1, m):
            factor = dot(v, basis[k]) * inv
            values.append((LANE_L + FACTORS.index((j, k)), factor))
            basis[k] = basis[k] - factor * v
    part[...] = lane_row(values)


def solve_slabs(g, groups, cells):
    own, top, bottom = (g[k : k + 8] for k in (LANE_OWN, LANE_TOP, LANE_BOTTOM))
    n = own.shape[1]
    lane = lax.broadcasted_iota(jnp.int32, own.shape, 1)
    b = own + jnp.where(lane == n - 1, 0.0, pltpu.roll(top, n - 1, 1))
    b = b + jnp.where(lane == 0, 0.0, pltpu.roll(bottom, 1, 1))
    b = b / (groups * float(n))
    mean = jnp.broadcast_to(g[LANE_EXT : LANE_EXT + 1], own.shape) / float(cells)
    d = 2.0 + mean / (float(n) * float(n))
    lower = jnp.where(lane == 0, 0.0, 1.0)
    upper = jnp.where(lane == n - 1, 0.0, 1.0)
    half = b.shape[0] // 2
    sub = lax.broadcasted_iota(jnp.int32, b.shape, 0)
    both_rows = jnp.where(sub < half, b, (d - lower) - upper)

    def excess():
        return jnp.broadcast_to(both_rows[half : half + 1], b.shape)

    s = 1
    while s < n:
        inv = 1.0 / (lower + upper + excess())
        alpha = lower * pltpu.roll(inv, s, 1)
        gamma = upper * pltpu.roll(inv, n - s, 1)
        down, up = pltpu.roll(both_rows, s, 1), pltpu.roll(both_rows, n - s, 1)
        both_rows = both_rows + alpha * down + gamma * up
        lower = alpha * pltpu.roll(lower, s, 1)
        upper = gamma * pltpu.roll(upper, n - s, 1)
        s *= 2
    return jnp.where(sub < half, both_rows / excess(), 0.0)


def coarse_kernel_b(me, x1, ext, b, row_at, row_ok, same_col, h, y4, cross, chip, x3, to_cross, to_chip):
    before, after = sides(me, cross, chip)
    put = sender(me, to_cross, to_chip)
    cases, rows, width = x1.shape
    x = coarse_step(
        [x1[c] for c in range(cases)],
        [before[row_of(c)] for c in range(cases)],
        [after[row_of(c)] for c in range(cases)],
        ext, b, h, (row_at, row_ok, same_col),
    )
    for c in range(cases):
        x3[c] = x[c]
        put(flat_row(c), x[c][0:1], x[c][rows - 1 : rows])
    no_row = jnp.zeros((1, width), F32)
    put(flat_row(19), no_row, no_row)
    for j in range(5):
        y = y4[j]
        for k in range(3):
            put(response_row(k, j), y[k : k + 1], y[rows - 1 - k : rows - k])


def coarse_kernel_c(me, x3, ext, b, row_at, row_ok, same_col, h, smooth, cross, chip, part, v, to_cross, to_chip):
    before, after = sides(me, cross, chip)
    put = sender(me, to_cross, to_chip)
    cases, rows, width = x3.shape
    x = coarse_step(
        [x3[c] for c in range(cases)],
        [before[flat_row(c)] for c in range(cases)],
        [after[flat_row(c)] for c in range(cases)],
        ext, b, h, (row_at, row_ok, same_col),
    )
    for c in range(cases):
        y = smooth[c] + x[c]
        v[c] = y
        for k in range(3):
            put((k,) + row_of(c), y[k : k + 1], y[rows - 1 - k : rows - k])


def post_kernel(me, v, f, ext, cross, chip, cross_v, chip_v, q, part_a, part_e, out, gather):
    before, after = sides(me, cross, chip)
    before_v, after_v = sides(me, cross_v, chip_v)
    cases, rows, width = v.shape
    m = q.shape[0]
    diag = 4.0 + ext[...]
    fl = [f[c] for c in range(cases)]
    v_halo = [both(before_v, after_v, k) for k in range(3)]
    f_halo = [both(before, after, 3 + k) for k in range(2)]
    d_halo = [4.0 + spread(before, after, k, cases) for k in range(2)]
    valid = spread(before, after, 2, cases)
    x, res = two_sweeps([v[c] for c in range(cases)], v_halo, fl, f_halo, diag, d_halo, valid)
    for c in range(cases):
        out[c] = x[c]
    inv = []
    for j in range(m):
        d = part_e[:, LANE_D + j : LANE_D + j + 1]
        inv.append(jnp.where(d > 0.0, 1.0 / jnp.where(d > 0.0, d, 1.0), 0.0))
    values = []
    for c in range(cases):
        r = res[c]
        share = [dot(r, q[j]) * inv[j] for j in range(m)]
        for j in range(m):
            r = r - share[j] * q[j]
        values.append((LANE_PERP + c, dot(r, r)))
        for j in range(m):
            values.append((LANE_C + 8 * j + c, share[j]))
    row = part_a[...] + part_e[...] + lane_row(values)
    gather[...] = jnp.broadcast_to(row, gather.shape)


def ratio_kernel(groups, cases, cells, me, gathered, ratio, corrections):
    n = gathered.shape[0]
    m = 2 * REACH_E + 1
    g = jnp.transpose(gathered[...])
    e = solve_slabs(g, groups, cells)
    corrections[...] = e
    lane = lax.broadcasted_iota(jnp.int32, e.shape, 1)

    def shifted(j):
        inside = (lane + j >= 0) & (lane + j < n)
        return jnp.where(inside, pltpu.roll(e, (-j) % n, 1), 0.0)

    def spread_row(k):
        return jnp.broadcast_to(g[k : k + 1], e.shape)

    t = [e] + [shifted(j) - e for j in ORDER[1:]]
    norm = g[LANE_PERP : LANE_PERP + 8]
    for j in range(m):
        z = g[LANE_C + 8 * j : LANE_C + 8 * j + 8] + t[j]
        for k in range(j + 1, m):
            z = z + spread_row(LANE_L + FACTORS.index((j, k))) * t[k]
        norm = norm + spread_row(LANE_D + j) * (z * z)
    norm = jnp.sum(norm, axis=1, keepdims=True)
    load = jnp.sum(g[LANE_LOAD : LANE_LOAD + 8], axis=1, keepdims=True)
    case = lax.broadcasted_iota(jnp.int32, norm.shape, 0)
    r = jnp.sqrt(jnp.where(case < cases, norm, 0.0) / jnp.where(case < cases, load, 1.0))
    ratio[...] = jnp.broadcast_to(lane_row([(c, r[c : c + 1]) for c in range(cases)]), ratio.shape)


def final_kernel(me, base, phi, corrections, out):
    cases, rows, width = base.shape
    e = corrections[...]
    lane = lax.broadcasted_iota(jnp.int32, e.shape, 1)
    near = [
        jnp.sum(jnp.where(lane == me[0] + j, e, 0.0), axis=1, keepdims=True)
        for j in range(-REACH_E, REACH_E + 1)
    ]
    for c in range(cases):
        x = base[c]
        for j in range(phi.shape[0]):
            x = x + near[j][c : c + 1] * phi[j]
        out[c] = x


def local(thermal_solution, heat_forcing, extinction_factor, cluster_label):
    cases, rows, width = thermal_solution.shape
    n = lax.axis_size("blk")
    n_rhs = lax.axis_size("rhs")
    groups = rows * width // 16
    field = (cases, rows, width)
    pairs = [(i, i + 1) for i in range(1, n - 1, 2)]
    cross_chip = pairs + [(j, i) for i, j in pairs]
    on_chip = [(i, i ^ 1) for i in range(n)]

    def exchange(cross, chip):
        cross = lax.ppermute(cross, "blk", cross_chip)
        return cross, lax.ppermute(chip, "blk", on_chip)

    edge = (cases, width)
    edges = (8, width)
    deep = (5, 4, width)
    cells = (rows, width)
    u, f, ext, lab = thermal_solution, heat_forcing, extinction_factor, cluster_label
    sent = vmem_call(
        pack_kernel,
        [(6, cases, width)] * 2,
        [
            pltpu.VMEM(field, F32),
            pltpu.VMEM(field, F32),
            pltpu.VMEM(cells, F32),
            pltpu.SemaphoreType.DMA((3,)),
        ],
        n_in=3,
        in_space=pl.ANY,
    )(u, f, ext)
    halo = exchange(*sent)
    shifts = len(offsets())
    *tables, y3 = vmem_call(
        functools.partial(table_kernel, n),
        [
            ((shifts, rows, width), jnp.int32),
            (shifts, rows, width),
            (rows - 1, rows, width),
            cells,
            (3, rows, width),
        ],
        n_in=2,
    )(ext, lab)
    call = vmem_call
    smooth, b, x0, *sent, rsum = call(
        pre_kernel, [field, field, field, edges, edges, (1, 128)], n_in=10
    )(u, f, ext, *halo, *tables, y3)
    rows_x = exchange(*sent)
    x1, *sent = call(coarse_kernel_a, [field, edge, edge], n_in=9)(
        x0, ext, b, *tables, *rows_x
    )
    (part_a,) = call(sum_kernel, [(1, 128)], n_in=4)(x1, ext, f, rsum)
    (y4,) = call(functools.partial(answer_kernel, cases), [(5, rows, width)], n_in=8)(
        ext, *tables, y3, *rows_x
    )
    rows_x = exchange(*sent)
    x3, *sent = call(coarse_kernel_b, [field, deep, deep], n_in=10)(
        x1, ext, b, *tables, y4, *rows_x
    )
    rows_x = exchange(*sent)
    m = 2 * REACH_E + 1
    phi, q, part_e = call(
        response_kernel, [(m, rows, width), (m, rows, width), (1, 128)], n_in=6
    )(ext, *halo, y4, *rows_x)
    v, *sent = call(
        coarse_kernel_c, [field, (3, cases, width), (3, cases, width)], n_in=11
    )(x3, ext, b, *tables, smooth, *rows_x, part_a)
    rows_x = exchange(*sent)
    base, mine = call(post_kernel, [field, (n, 128)], n_in=10)(
        v, f, ext, *halo, *rows_x, q, part_a, part_e
    )
    gathered = lax.all_to_all(mine, "blk", 0, 0, tiled=True)
    ratio, corrections = call(
        functools.partial(ratio_kernel, groups, cases, rows * width),
        [(n_rhs, 128), (8, n)],
        n_in=1,
    )(gathered)
    every = lax.all_to_all(ratio, "rhs", 0, 0, tiled=True)
    (corrected,) = call(final_kernel, [field], n_in=3)(base, phi, corrections)
    return corrected, every[:, :cases].reshape(n_rhs * cases)


def solution(mesh):
    in_specs = (P("rhs", "blk", None), P("rhs", "blk", None), P("blk", None), P("blk", None))
    out_specs = (P("rhs", "blk", None), P())
    return jax.shard_map(local, mesh=mesh, in_specs=in_specs, out_specs=out_specs, check_vma=False)
```

```python
import functools

import jax
import jax.numpy as jnp
from jax import lax
from jax.experimental import pallas as pl
from jax.experimental.pallas import tpu as pltpu
from jax.sharding import PartitionSpec as P

damping_fine = 0.8
damping_coarse = 0.5
REACH = 7
F32 = jnp.float32


VMEM = pl.BlockSpec(memory_space=pltpu.VMEM)


def with_place(body):
    def kernel(*refs):
        body((lax.axis_index("blk"), lax.axis_index("rhs")), *refs)

    return kernel


def vmem_call(body, outs, scratch=(), n_in=0, in_space=pltpu.VMEM):
    limit = 48 << 20 if in_space == pltpu.VMEM else 56_288_000
    return pl.pallas_call(
        with_place(body),
        out_shape=[
            jax.ShapeDtypeStruct(*(s if isinstance(s[0], tuple) else (s, F32))) for s in outs
        ],
        in_specs=[pl.BlockSpec(memory_space=in_space)] * n_in,
        out_specs=[VMEM] * len(outs),
        scratch_shapes=list(scratch),
        compiler_params=pltpu.CompilerParams(vmem_limit_bytes=limit),
    )


class View:
    def __init__(self, own_chip, cross, chip):
        self.own_chip = own_chip
        self.chip, self.cross = chip, cross

    def __getitem__(self, k):
        return jnp.where(self.own_chip, self.chip[k], self.cross[k])


def sides(me, cross, chip):
    odd = (me[0] & 1) == 1
    return View(odd, cross, chip), View(jnp.logical_not(odd), cross, chip)


def row_of(c):
    return (pl.ds(c, 1), slice(None))


def sender(me, cross, chip):
    odd = (me[0] & 1) == 1

    def put(k, first, last):
        chip[k] = jnp.where(odd, first, last)
        cross[k] = jnp.where(odd, last, first)

    return put


def iotas(shape):
    return (
        lax.broadcasted_iota(jnp.int32, shape, 0),
        lax.broadcasted_iota(jnp.int32, shape, 1),
    )


def sideways(x):
    rows, width = x.shape
    col = lax.broadcasted_iota(jnp.int32, x.shape, 1)
    left = jnp.where(col == 0, 0.0, pltpu.roll(x, 1, 1))
    right = jnp.where(col == width - 1, 0.0, pltpu.roll(x, width - 1, 1))
    return left + right


def neighbours(x, above, below):
    rows = x.shape[0]
    row = lax.broadcasted_iota(jnp.int32, x.shape, 0)
    up = jnp.where(row == 0, above, pltpu.roll(x, 1, 0))
    down = jnp.where(row == rows - 1, below, pltpu.roll(x, rows - 1, 0))
    return up + down + sideways(x)


def offsets():
    return [d for d in range(-REACH, REACH + 1) if d]


def seg_sum(fields, tables):
    row_at, row_ok, same_col = tables
    rows, width = fields[0].shape
    col = list(fields)
    for k in range(1, rows):
        m = same_col[k - 1]
        col = [s + m * pltpu.roll(w, k, 0) for s, w in zip(col, fields)]
    out = list(col)
    for d, dx in enumerate(offsets()):
        at, ok = row_at[d], row_ok[d]
        out = [
            t
            + ok
            * jnp.take_along_axis(
                pltpu.roll(s, (-dx) % width, 1), at, axis=0, mode="promise_in_bounds"
            )
            for t, s in zip(out, col)
        ]
    return out


def table_kernel(n, me, ext, lab, row_at, row_ok, same_col, h, y3):
    key = lab[...]
    rows, width = key.shape
    for k in range(1, rows):
        same_col[k - 1] = jnp.where(pltpu.roll(key, k, 0) == key, 1.0, 0.0)
    for d, dx in enumerate(offsets()):
        there = pltpu.roll(key, (-dx) % width, 1)
        at = jnp.full(key.shape, -1, jnp.int32)
        for r in range(rows):
            at = jnp.where(jnp.broadcast_to(there[r : r + 1], key.shape) == key, r, at)
        row_ok[d] = jnp.where(at >= 0, 1.0, 0.0)
        row_at[d] = jnp.maximum(at, 0)
    row, col = iotas(key.shape)
    one = jnp.ones(key.shape, F32)
    zero = jnp.zeros(key.shape, F32)
    m = jnp.where((pltpu.roll(key, 1, 0) == key) & (row > 0), one, zero)
    m = m + jnp.where((pltpu.roll(key, rows - 1, 0) == key) & (row < rows - 1), one, zero)
    m = m + jnp.where((pltpu.roll(key, 1, 1) == key) & (col > 0), one, zero)
    m = m + jnp.where((pltpu.roll(key, width - 1, 1) == key) & (col < width - 1), one, zero)
    above = jnp.where(me[0] > 0, 1.0, 0.0)
    below = jnp.where(me[0] < n - 1, 1.0, 0.0)
    top = jnp.where(row == 0, one, zero)
    bottom = jnp.where(row == rows - 1, one, zero)
    open_sides = open_weight(ext[...])
    diag1, s_top, s_own, s_bottom = seg_sum(
        [4.0 + ext[...] - m, top, open_sides, bottom], (row_at, row_ok, same_col)
    )
    half = damping_coarse / diag1
    h[...] = half
    y3[0] = above * (half * s_top)
    y3[1] = 1.0 - half * s_own
    y3[2] = below * (half * s_bottom)


def open_weight(ext):
    rows, width = ext.shape
    row, col = iotas(ext.shape)
    one = jnp.ones(ext.shape, F32)
    zero = jnp.zeros(ext.shape, F32)
    weight = ext
    for at_edge in (row == 0, row == rows - 1, col == 0, col == width - 1):
        weight = weight + jnp.where(at_edge, one, zero)
    return weight


GROUP_EXT = 5


def pack_kernel(me, u_hbm, f_hbm, ext_hbm, cross, chip, u, f, ext, sem):
    pairs = ((u_hbm, u), (f_hbm, f), (ext_hbm, ext))
    copies = [pltpu.make_async_copy(src, dst, sem.at[k]) for k, (src, dst) in enumerate(pairs)]
    for copy in copies:
        copy.start()
    for copy in copies:
        copy.wait()
    cases, rows, width = u.shape
    put = sender(me, cross, chip)
    ones = jnp.ones((1, width), F32)
    end = rows - 1
    for k in range(3):
        put(k, u[:, k, :], u[:, end - k, :])
    for k in range(2):
        put(3 + k, f[:, k, :], f[:, end - k, :])
        at = (GROUP_EXT,) + row_of(k)
        put(at, ext[pl.ds(k, 1), :], ext[pl.ds(end - k, 1), :])
    for k in range(2, cases):
        put((GROUP_EXT,) + row_of(k), ones, ones)


def both(before, after, k):
    return jnp.concatenate([before[k], after[k]], axis=0)


def spread(before, after, k, times):
    at = (GROUP_EXT,) + row_of(k)
    up, down = before[at], after[at]
    shape = (times, up.shape[1])
    return jnp.concatenate([jnp.broadcast_to(up, shape), jnp.broadcast_to(down, shape)], axis=0)


def two_sweeps(u, u_halo, f, f_halo, diag, diag_halo, valid):
    cases = len(u)
    rows = u[0].shape[0]
    gain = damping_fine / diag
    gain_halo = [damping_fine / d for d in diag_halo]
    keep = 1.0 - damping_fine

    def edge(x):
        return jnp.concatenate([v[0:1] for v in x] + [v[rows - 1 : rows] for v in x], axis=0)

    def around(x, halo, c):
        return neighbours(x[c], halo[0][c : c + 1], halo[0][cases + c : cases + c + 1])

    def sweep(x, halo, depth):
        new = []
        for c in range(cases):
            push = around(x, halo, c)
            new.append(keep * x[c] + gain * (push if f is None else f[c] + push))
        inner = [edge(x)] + halo
        new_halo = []
        for k in range(depth):
            push = inner[k] + inner[k + 2] + sideways(halo[k])
            push = push if f is None else f_halo[k] + push
            new_halo.append((keep * halo[k] + gain_halo[k] * push) * valid)
        return new, new_halo

    x, h = sweep(u, u_halo, 2)
    x, h = sweep(x, h, 1)
    res = []
    for c in range(cases):
        r = around(x, h, c) - diag * x[c]
        res.append(r if f is None else f[c] + r)
    return x, res


def total(x):
    rows, width = x.shape
    part = x[:, 0:128]
    for k in range(1, width // 128):
        part = part + x[:, k * 128 : (k + 1) * 128]
    return jnp.sum(jnp.sum(part, axis=1, keepdims=True), axis=0, keepdims=True)


def lane_row(values):
    lane = lax.broadcasted_iota(jnp.int32, (1, 128), 1)
    row = jnp.zeros((1, 128), F32)
    for k, v in values:
        row = jnp.where(lane == k, v, row)
    return row


def pre_kernel(me, u, f, ext, cross, chip, row_at, row_ok, same_col, h, y3, smooth, b, x0, to_cross, to_chip, rsum):
    before, after = sides(me, cross, chip)
    put = sender(me, to_cross, to_chip)
    cases, rows, width = u.shape
    diag = 4.0 + ext[...]
    us = [u[c] for c in range(cases)]
    fl = [f[c] for c in range(cases)]
    u_halo = [both(before, after, k) for k in range(3)]
    f_halo = [both(before, after, 3 + k) for k in range(2)]
    d_halo = [4.0 + spread(before, after, k, cases) for k in range(2)]
    valid = spread(before, after, 2, cases)
    x, res = two_sweeps(us, u_halo, fl, f_halo, diag, d_halo, valid)
    for c in range(cases):
        smooth[c] = x[c]
    sums = seg_sum(res, (row_at, row_ok, same_col))
    for c in range(cases):
        b[c] = sums[c]
        v = h[...] * sums[c]
        x0[c] = v
        put(row_of(c), v[0:1], v[rows - 1 : rows])
    for j in range(3):
        y = y3[j]
        put(row_of(cases + j), y[0:1], y[rows - 1 : rows])
    put(row_of(cases + 3), jnp.zeros((1, width), F32), jnp.zeros((1, width), F32))
    rsum[...] = lane_row([(c, total(res[c])) for c in range(cases)])


def coarse_step(x, above, below, ext, b, h, tables):
    cases = len(x)
    diag = 4.0 + ext[...]
    w = [diag * x[c] - neighbours(x[c], above[c], below[c]) for c in range(cases)]
    sums = seg_sum(w, tables)
    return [x[c] + h[...] * (b[c] - sums[c]) for c in range(cases)]


def flat_row(r):
    return (r // 4,) + row_of(r % 4)


def response_row(k, j):
    return flat_row(4 + 5 * k + j)


def coarse_kernel_a(me, x0, ext, b, row_at, row_ok, same_col, h, cross, chip, x1, to_cross, to_chip):
    before, after = sides(me, cross, chip)
    put = sender(me, to_cross, to_chip)
    cases, rows, width = x0.shape
    x = coarse_step(
        [x0[c] for c in range(cases)],
        [before[row_of(c)] for c in range(cases)],
        [after[row_of(c)] for c in range(cases)],
        ext, b, h, (row_at, row_ok, same_col),
    )
    for c in range(cases):
        x1[c] = x[c]
        put(row_of(c), x[c][0:1], x[c][rows - 1 : rows])


def sum_kernel(me, x1, ext, f, rsum, part):
    cases, rows, width = x1.shape
    weight = open_weight(ext[...])
    values = [(LANE_EXT, total(ext[...]))]
    for c in range(cases):
        x = x1[c]
        values.append((LANE_OWN + c, rsum[:, c : c + 1] - total(weight * x)))
        values.append((LANE_TOP + c, total(x[0:1])))
        values.append((LANE_BOTTOM + c, total(x[rows - 1 : rows])))
        values.append((LANE_LOAD + c, dot(f[c], f[c])))
    part[...] = lane_row(values)


def answer_kernel(cases, me, ext, row_at, row_ok, same_col, h, y3, cross, chip, y4):
    before, after = sides(me, cross, chip)
    rows, width = ext.shape
    none = jnp.zeros((rows, width), F32)
    no_row = jnp.zeros((1, width), F32)
    above = [before[row_of(cases + j)] for j in range(3)] + [no_row, no_row]
    below = [no_row, no_row] + [after[row_of(cases + j)] for j in range(3)]
    y = coarse_step(
        [none] + [y3[j] for j in range(3)] + [none],
        above, below, ext, [none] * 5, h, (row_at, row_ok, same_col),
    )
    for j in range(5):
        y4[j] = y[j]


REACH_E = 3
ORDER = [0, -1, 1, -2, 2, -3, 3]
LANE_OWN, LANE_TOP, LANE_BOTTOM, LANE_EXT, LANE_D = 0, 8, 16, 24, 25
LANE_PERP, LANE_LOAD, LANE_C, LANE_L = 32, 40, 48, 104
FACTORS = [(j, k) for j in range(7) for k in range(j + 1, 7)]


def dot(x, y):
    return total(x * y)


def response_kernel(me, ext, cross, chip, y4, cross_y, chip_y, phi, q, scaled, part):
    before, after = sides(me, cross, chip)
    ab, be = sides(me, cross_y, chip_y)
    rows, width = ext.shape
    m = 2 * REACH_E + 1
    diag = 4.0 + ext[...]
    none = jnp.zeros((rows, width), F32)
    fields = [none] + [y4[j] for j in range(5)] + [none]
    two_rows = jnp.zeros((2, width), F32)
    halo = []
    for k in range(3):
        up = [ab[response_row(k, j)] for j in range(5)]
        down = [be[response_row(k, j)] for j in range(5)]
        halo.append(jnp.concatenate(up + [two_rows, two_rows] + down, axis=0))

    d_halo = [4.0 + spread(before, after, k, m) for k in range(2)]
    x, res = two_sweeps(fields, halo, None, None, diag, d_halo, spread(before, after, 2, m))
    for j in range(m):
        phi[j] = x[j]
    every = res[0]
    for j in range(1, m):
        every = every + res[j]
    basis = [every] + [res[REACH_E + j] for j in ORDER[1:]]
    values = []
    for j in range(m):
        v = basis[j]
        q[j] = v
        d = dot(v, v)
        inv = jnp.where(d > 0.0, 1.0 / jnp.where(d > 0.0, d, 1.0), 0.0)
        scaled[j] = inv * v
        values.append((LANE_D + j, d))
        for k in range(j + 1, m):
            factor = dot(v, basis[k]) * inv
            values.append((LANE_L + FACTORS.index((j, k)), factor))
            basis[k] = basis[k] - factor * v
    part[...] = lane_row(values)


def solve_slabs(g, groups, cells):
    own, top, bottom = (g[k : k + 8] for k in (LANE_OWN, LANE_TOP, LANE_BOTTOM))
    n = own.shape[1]
    lane = lax.broadcasted_iota(jnp.int32, own.shape, 1)
    b = own + jnp.where(lane == n - 1, 0.0, pltpu.roll(top, n - 1, 1))
    b = b + jnp.where(lane == 0, 0.0, pltpu.roll(bottom, 1, 1))
    b = b / (groups * float(n))
    mean = jnp.broadcast_to(g[LANE_EXT : LANE_EXT + 1], own.shape) / float(cells)
    d = 2.0 + mean / (float(n) * float(n))
    lower = jnp.where(lane == 0, 0.0, 1.0)
    upper = jnp.where(lane == n - 1, 0.0, 1.0)
    excess = (d - lower) - upper
    s = 1
    while s < n:
        inv = 1.0 / (lower + upper + excess)
        alpha = lower * pltpu.roll(inv, s, 1)
        gamma = upper * pltpu.roll(inv, n - s, 1)
        b = b + alpha * pltpu.roll(b, s, 1) + gamma * pltpu.roll(b, n - s, 1)
        excess = excess + alpha * pltpu.roll(excess, s, 1) + gamma * pltpu.roll(excess, n - s, 1)
        lower = alpha * pltpu.roll(lower, s, 1)
        upper = gamma * pltpu.roll(upper, n - s, 1)
        s *= 2
    return b / (lower + upper + excess)


def coarse_kernel_b(me, x1, ext, b, row_at, row_ok, same_col, h, y4, cross, chip, x3, to_cross, to_chip):
    before, after = sides(me, cross, chip)
    put = sender(me, to_cross, to_chip)
    cases, rows, width = x1.shape
    x = coarse_step(
        [x1[c] for c in range(cases)],
        [before[row_of(c)] for c in range(cases)],
        [after[row_of(c)] for c in range(cases)],
        ext, b, h, (row_at, row_ok, same_col),
    )
    for c in range(cases):
        x3[c] = x[c]
        put(flat_row(c), x[c][0:1], x[c][rows - 1 : rows])
    no_row = jnp.zeros((1, width), F32)
    put(flat_row(19), no_row, no_row)
    for j in range(5):
        y = y4[j]
        for k in range(3):
            put(response_row(k, j), y[k : k + 1], y[rows - 1 - k : rows - k])


def coarse_kernel_c(me, x3, ext, b, row_at, row_ok, same_col, h, smooth, cross, chip, part, v, to_cross, to_chip):
    before, after = sides(me, cross, chip)
    put = sender(me, to_cross, to_chip)
    cases, rows, width = x3.shape
    x = coarse_step(
        [x3[c] for c in range(cases)],
        [before[flat_row(c)] for c in range(cases)],
        [after[flat_row(c)] for c in range(cases)],
        ext, b, h, (row_at, row_ok, same_col),
    )
    for c in range(cases):
        y = smooth[c] + x[c]
        v[c] = y
        for k in range(3):
            put((k,) + row_of(c), y[k : k + 1], y[rows - 1 - k : rows - k])


def post_kernel(me, v, f, ext, cross, chip, cross_v, chip_v, q, scaled, part_a, part_e, out, gather):
    before, after = sides(me, cross, chip)
    before_v, after_v = sides(me, cross_v, chip_v)
    cases, rows, width = v.shape
    m = q.shape[0]
    diag = 4.0 + ext[...]
    fl = [f[c] for c in range(cases)]
    v_halo = [both(before_v, after_v, k) for k in range(3)]
    f_halo = [both(before, after, 3 + k) for k in range(2)]
    d_halo = [4.0 + spread(before, after, k, cases) for k in range(2)]
    valid = spread(before, after, 2, cases)
    x, res = two_sweeps([v[c] for c in range(cases)], v_halo, fl, f_halo, diag, d_halo, valid)
    for c in range(cases):
        out[c] = x[c]
    values = []
    for c in range(cases):
        r = res[c]
        share = [dot(r, scaled[j]) for j in range(m)]
        for j in range(m):
            r = r - share[j] * q[j]
        values.append((LANE_PERP + c, dot(r, r)))
        for j in range(m):
            values.append((LANE_C + 8 * j + c, share[j]))
    row = part_a[...] + part_e[...] + lane_row(values)
    gather[...] = jnp.broadcast_to(row, gather.shape)


def ratio_kernel(groups, cases, cells, me, gathered, ratio, near):
    n = gathered.shape[0]
    m = 2 * REACH_E + 1
    g = jnp.transpose(gathered[...])
    e = solve_slabs(g, groups, cells)
    lane = lax.broadcasted_iota(jnp.int32, e.shape, 1)
    for j in range(m):
        at = lane == me[0] + j - REACH_E
        own = jnp.sum(jnp.where(at, e, 0.0), axis=1, keepdims=True)
        near[j] = jnp.broadcast_to(own, near.shape[1:])

    def shifted(j):
        inside = (lane + j >= 0) & (lane + j < n)
        return jnp.where(inside, pltpu.roll(e, (-j) % n, 1), 0.0)

    def spread_row(k):
        return jnp.broadcast_to(g[k : k + 1], e.shape)

    t = [e] + [shifted(j) - e for j in ORDER[1:]]
    norm = g[LANE_PERP : LANE_PERP + 8]
    for j in range(m):
        z = g[LANE_C + 8 * j : LANE_C + 8 * j + 8] + t[j]
        for k in range(j + 1, m):
            z = z + spread_row(LANE_L + FACTORS.index((j, k))) * t[k]
        norm = norm + spread_row(LANE_D + j) * (z * z)
    norm = jnp.sum(norm, axis=1, keepdims=True)
    load = jnp.sum(g[LANE_LOAD : LANE_LOAD + 8], axis=1, keepdims=True)
    case = lax.broadcasted_iota(jnp.int32, norm.shape, 0)
    r = jnp.sqrt(jnp.where(case < cases, norm, 0.0) / jnp.where(case < cases, load, 1.0))
    ratio[...] = jnp.broadcast_to(lane_row([(c, r[c : c + 1]) for c in range(cases)]), ratio.shape)


def final_kernel(me, base, phi, near, out):
    cases, rows, width = base.shape
    for c in range(cases):
        x = base[c]
        for j in range(phi.shape[0]):
            x = x + near[j, pl.ds(c, 1), 0:1] * phi[j]
        out[c] = x


def local(thermal_solution, heat_forcing, extinction_factor, cluster_label):
    cases, rows, width = thermal_solution.shape
    n = lax.axis_size("blk")
    n_rhs = lax.axis_size("rhs")
    groups = rows * width // 16
    field = (cases, rows, width)
    pairs = [(i, i + 1) for i in range(1, n - 1, 2)]
    cross_chip = pairs + [(j, i) for i, j in pairs]
    on_chip = [(i, i ^ 1) for i in range(n)]

    def exchange(cross, chip):
        cross = lax.ppermute(cross, "blk", cross_chip)
        return cross, lax.ppermute(chip, "blk", on_chip)

    edge = (cases, width)
    edges = (8, width)
    deep = (5, 4, width)
    cells = (rows, width)
    u, f, ext, lab = thermal_solution, heat_forcing, extinction_factor, cluster_label
    sent = vmem_call(
        pack_kernel,
        [(6, cases, width)] * 2,
        [
            pltpu.VMEM(field, F32),
            pltpu.VMEM(field, F32),
            pltpu.VMEM(cells, F32),
            pltpu.SemaphoreType.DMA((3,)),
        ],
        n_in=3,
        in_space=pl.ANY,
    )(u, f, ext)
    halo = exchange(*sent)
    shifts = len(offsets())
    *tables, y3 = vmem_call(
        functools.partial(table_kernel, n),
        [
            ((shifts, rows, width), jnp.int32),
            (shifts, rows, width),
            (rows - 1, rows, width),
            cells,
            (3, rows, width),
        ],
        n_in=2,
    )(ext, lab)
    call = vmem_call
    smooth, b, x0, *sent, rsum = call(
        pre_kernel, [field, field, field, edges, edges, (1, 128)], n_in=10
    )(u, f, ext, *halo, *tables, y3)
    rows_x = exchange(*sent)
    x1, *sent = call(coarse_kernel_a, [field, edge, edge], n_in=9)(
        x0, ext, b, *tables, *rows_x
    )
    (part_a,) = call(sum_kernel, [(1, 128)], n_in=4)(x1, ext, f, rsum)
    (y4,) = call(functools.partial(answer_kernel, cases), [(5, rows, width)], n_in=8)(
        ext, *tables, y3, *rows_x
    )
    rows_x = exchange(*sent)
    x3, *sent = call(coarse_kernel_b, [field, deep, deep], n_in=10)(
        x1, ext, b, *tables, y4, *rows_x
    )
    rows_x = exchange(*sent)
    m = 2 * REACH_E + 1
    phi, q, scaled, part_e = call(
        response_kernel, [(m, rows, width)] * 3 + [(1, 128)], n_in=6
    )(ext, *halo, y4, *rows_x)
    v, *sent = call(
        coarse_kernel_c, [field, (3, cases, width), (3, cases, width)], n_in=11
    )(x3, ext, b, *tables, smooth, *rows_x, part_a)
    rows_x = exchange(*sent)
    base, mine = call(post_kernel, [field, (n, 128)], n_in=11)(
        v, f, ext, *halo, *rows_x, q, scaled, part_a, part_e
    )
    gathered = lax.all_to_all(mine, "blk", 0, 0, tiled=True)
    ratio, near = call(
        functools.partial(ratio_kernel, groups, cases, rows * width),
        [(n_rhs, 128), (m, 8, 128)],
        n_in=1,
    )(gathered)
    every = lax.all_to_all(ratio, "rhs", 0, 0, tiled=True)
    (corrected,) = call(final_kernel, [field], n_in=3)(base, phi, near)
    return corrected, every[:, :cases].reshape(n_rhs * cases)


def solution(mesh):
    in_specs = (P("rhs", "blk", None), P("rhs", "blk", None), P("blk", None), P("blk", None))
    out_specs = (P("rhs", "blk", None), P())
    return jax.shard_map(local, mesh=mesh, in_specs=in_specs, out_specs=out_specs, check_vma=False)
```

```python
import functools

import jax
import jax.numpy as jnp
from jax import lax
from jax.experimental import pallas as pl
from jax.experimental.pallas import tpu as pltpu
from jax.sharding import PartitionSpec as P

damping_fine = 0.8
damping_coarse = 0.5
REACH = 7
F32 = jnp.float32


VMEM = pl.BlockSpec(memory_space=pltpu.VMEM)


def with_place(body):
    def kernel(*refs):
        body((lax.axis_index("blk"), lax.axis_index("rhs")), *refs)

    return kernel


def vmem_call(body, outs, scratch=(), n_in=0, in_space=pltpu.VMEM):
    limit = 48 << 20 if in_space == pltpu.VMEM else 56_288_000
    return pl.pallas_call(
        with_place(body),
        out_shape=[
            jax.ShapeDtypeStruct(*(s if isinstance(s[0], tuple) else (s, F32))) for s in outs
        ],
        in_specs=[pl.BlockSpec(memory_space=in_space)] * n_in,
        out_specs=[VMEM] * len(outs),
        scratch_shapes=list(scratch),
        compiler_params=pltpu.CompilerParams(vmem_limit_bytes=limit),
    )


class View:
    def __init__(self, own_chip, cross, chip):
        self.own_chip = own_chip
        self.chip, self.cross = chip, cross

    def __getitem__(self, k):
        return jnp.where(self.own_chip, self.chip[k], self.cross[k])


def sides(me, cross, chip):
    odd = (me[0] & 1) == 1
    return View(odd, cross, chip), View(jnp.logical_not(odd), cross, chip)


def row_of(c):
    return (pl.ds(c, 1), slice(None))


def sender(me, cross, chip):
    odd = (me[0] & 1) == 1

    def put(k, first, last):
        chip[k] = jnp.where(odd, first, last)
        cross[k] = jnp.where(odd, last, first)

    return put


def iotas(shape):
    return (
        lax.broadcasted_iota(jnp.int32, shape, 0),
        lax.broadcasted_iota(jnp.int32, shape, 1),
    )


def sideways(x):
    rows, width = x.shape
    col = lax.broadcasted_iota(jnp.int32, x.shape, 1)
    left = jnp.where(col == 0, 0.0, pltpu.roll(x, 1, 1))
    right = jnp.where(col == width - 1, 0.0, pltpu.roll(x, width - 1, 1))
    return left + right


def neighbours(x, above, below):
    rows = x.shape[0]
    row = lax.broadcasted_iota(jnp.int32, x.shape, 0)
    up = jnp.where(row == 0, above, pltpu.roll(x, 1, 0))
    down = jnp.where(row == rows - 1, below, pltpu.roll(x, rows - 1, 0))
    return up + down + sideways(x)


def offsets():
    return [d for d in range(-REACH, REACH + 1) if d]


def seg_sum(fields, tables):
    row_at, row_ok, same_col = tables
    rows, width = fields[0].shape
    col = list(fields)
    for k in range(1, rows):
        m = same_col[k - 1]
        col = [s + m * pltpu.roll(w, k, 0) for s, w in zip(col, fields)]
    out = list(col)
    for d, dx in enumerate(offsets()):
        at, ok = row_at[d], row_ok[d]
        out = [
            t
            + ok
            * jnp.take_along_axis(
                pltpu.roll(s, (-dx) % width, 1), at, axis=0, mode="promise_in_bounds"
            )
            for t, s in zip(out, col)
        ]
    return out


def table_kernel(n, me, ext, lab, row_at, row_ok, same_col, h, y3):
    key = lab[...]
    rows, width = key.shape
    for k in range(1, rows):
        same_col[k - 1] = jnp.where(pltpu.roll(key, k, 0) == key, 1.0, 0.0)
    for d, dx in enumerate(offsets()):
        there = pltpu.roll(key, (-dx) % width, 1)
        at = jnp.full(key.shape, -1, jnp.int32)
        for r in range(rows):
            at = jnp.where(jnp.broadcast_to(there[r : r + 1], key.shape) == key, r, at)
        row_ok[d] = jnp.where(at >= 0, 1.0, 0.0)
        row_at[d] = jnp.maximum(at, 0)
    row, col = iotas(key.shape)
    one = jnp.ones(key.shape, F32)
    zero = jnp.zeros(key.shape, F32)
    m = jnp.where((pltpu.roll(key, 1, 0) == key) & (row > 0), one, zero)
    m = m + jnp.where((pltpu.roll(key, rows - 1, 0) == key) & (row < rows - 1), one, zero)
    m = m + jnp.where((pltpu.roll(key, 1, 1) == key) & (col > 0), one, zero)
    m = m + jnp.where((pltpu.roll(key, width - 1, 1) == key) & (col < width - 1), one, zero)
    above = jnp.where(me[0] > 0, 1.0, 0.0)
    below = jnp.where(me[0] < n - 1, 1.0, 0.0)
    top = jnp.where(row == 0, one, zero)
    bottom = jnp.where(row == rows - 1, one, zero)
    open_sides = open_weight(ext[...])
    diag1, s_top, s_own, s_bottom = seg_sum(
        [4.0 + ext[...] - m, top, open_sides, bottom], (row_at, row_ok, same_col)
    )
    half = damping_coarse / diag1
    h[...] = half
    y3[0] = above * (half * s_top)
    y3[1] = 1.0 - half * s_own
    y3[2] = below * (half * s_bottom)


def open_weight(ext):
    rows, width = ext.shape
    row, col = iotas(ext.shape)
    one = jnp.ones(ext.shape, F32)
    zero = jnp.zeros(ext.shape, F32)
    weight = ext
    for at_edge in (row == 0, row == rows - 1, col == 0, col == width - 1):
        weight = weight + jnp.where(at_edge, one, zero)
    return weight


GROUP_EXT = 5


def pack_kernel(me, u_hbm, f_hbm, ext_hbm, cross, chip, u, f, ext, sem):
    pairs = ((u_hbm, u), (f_hbm, f), (ext_hbm, ext))
    copies = [pltpu.make_async_copy(src, dst, sem.at[k]) for k, (src, dst) in enumerate(pairs)]
    for copy in copies:
        copy.start()
    for copy in copies:
        copy.wait()
    cases, rows, width = u.shape
    put = sender(me, cross, chip)
    ones = jnp.ones((1, width), F32)
    end = rows - 1
    for k in range(3):
        put(k, u[:, k, :], u[:, end - k, :])
    for k in range(2):
        put(3 + k, f[:, k, :], f[:, end - k, :])
        at = (GROUP_EXT,) + row_of(k)
        put(at, ext[pl.ds(k, 1), :], ext[pl.ds(end - k, 1), :])
    for k in range(2, cases):
        put((GROUP_EXT,) + row_of(k), ones, ones)


def both(before, after, k):
    return jnp.concatenate([before[k], after[k]], axis=0)


def spread(before, after, k, times):
    at = (GROUP_EXT,) + row_of(k)
    up, down = before[at], after[at]
    shape = (times, up.shape[1])
    return jnp.concatenate([jnp.broadcast_to(up, shape), jnp.broadcast_to(down, shape)], axis=0)


def two_sweeps(u, u_halo, f, f_halo, diag, diag_halo, valid):
    cases = len(u)
    rows = u[0].shape[0]
    gain = damping_fine / diag
    gain_halo = [damping_fine / d for d in diag_halo]
    keep = 1.0 - damping_fine

    def edge(x):
        return jnp.concatenate([v[0:1] for v in x] + [v[rows - 1 : rows] for v in x], axis=0)

    def around(x, halo, c):
        return neighbours(x[c], halo[0][c : c + 1], halo[0][cases + c : cases + c + 1])

    def sweep(x, halo, depth):
        new = []
        for c in range(cases):
            push = around(x, halo, c)
            new.append(keep * x[c] + gain * (push if f is None else f[c] + push))
        inner = [edge(x)] + halo
        new_halo = []
        for k in range(depth):
            push = inner[k] + inner[k + 2] + sideways(halo[k])
            push = push if f is None else f_halo[k] + push
            new_halo.append((keep * halo[k] + gain_halo[k] * push) * valid)
        return new, new_halo

    x, h = sweep(u, u_halo, 2)
    x, h = sweep(x, h, 1)
    res = []
    for c in range(cases):
        r = around(x, h, c) - diag * x[c]
        res.append(r if f is None else f[c] + r)
    return x, res


def total(x):
    rows, width = x.shape
    part = x[:, 0:128]
    for k in range(1, width // 128):
        part = part + x[:, k * 128 : (k + 1) * 128]
    return jnp.sum(jnp.sum(part, axis=0, keepdims=True), axis=1, keepdims=True)


def lane_row(values):
    lane = lax.broadcasted_iota(jnp.int32, (1, 128), 1)
    row = jnp.zeros((1, 128), F32)
    for k, v in values:
        row = jnp.where(lane == k, v, row)
    return row


def pre_kernel(me, u, f, ext, cross, chip, row_at, row_ok, same_col, h, y3, smooth, b, x0, to_cross, to_chip, rsum):
    before, after = sides(me, cross, chip)
    put = sender(me, to_cross, to_chip)
    cases, rows, width = u.shape
    diag = 4.0 + ext[...]
    us = [u[c] for c in range(cases)]
    fl = [f[c] for c in range(cases)]
    u_halo = [both(before, after, k) for k in range(3)]
    f_halo = [both(before, after, 3 + k) for k in range(2)]
    d_halo = [4.0 + spread(before, after, k, cases) for k in range(2)]
    valid = spread(before, after, 2, cases)
    x, res = two_sweeps(us, u_halo, fl, f_halo, diag, d_halo, valid)
    for c in range(cases):
        smooth[c] = x[c]
    sums = seg_sum(res, (row_at, row_ok, same_col))
    for c in range(cases):
        b[c] = sums[c]
        v = h[...] * sums[c]
        x0[c] = v
        put(row_of(c), v[0:1], v[rows - 1 : rows])
    for j in range(3):
        y = y3[j]
        put(row_of(cases + j), y[0:1], y[rows - 1 : rows])
    put(row_of(cases + 3), jnp.zeros((1, width), F32), jnp.zeros((1, width), F32))
    rsum[...] = lane_row([(c, total(res[c])) for c in range(cases)])


def coarse_step(x, above, below, ext, b, h, tables):
    cases = len(x)
    diag = 4.0 + ext[...]
    w = [diag * x[c] - neighbours(x[c], above[c], below[c]) for c in range(cases)]
    sums = seg_sum(w, tables)
    return [x[c] + h[...] * (b[c] - sums[c]) for c in range(cases)]


def flat_row(r):
    return (r // 4,) + row_of(r % 4)


def response_row(k, j):
    return flat_row(4 + 5 * k + j)


def coarse_kernel_a(me, x0, ext, b, row_at, row_ok, same_col, h, cross, chip, x1, to_cross, to_chip):
    before, after = sides(me, cross, chip)
    put = sender(me, to_cross, to_chip)
    cases, rows, width = x0.shape
    x = coarse_step(
        [x0[c] for c in range(cases)],
        [before[row_of(c)] for c in range(cases)],
        [after[row_of(c)] for c in range(cases)],
        ext, b, h, (row_at, row_ok, same_col),
    )
    for c in range(cases):
        x1[c] = x[c]
        put(row_of(c), x[c][0:1], x[c][rows - 1 : rows])


def sum_kernel(me, x1, ext, f, rsum, part):
    cases, rows, width = x1.shape
    weight = open_weight(ext[...])
    values = [(LANE_EXT, total(ext[...]))]
    for c in range(cases):
        x = x1[c]
        values.append((LANE_OWN + c, rsum[:, c : c + 1] - total(weight * x)))
        values.append((LANE_TOP + c, total(x[0:1])))
        values.append((LANE_BOTTOM + c, total(x[rows - 1 : rows])))
        values.append((LANE_LOAD + c, dot(f[c], f[c])))
    part[...] = lane_row(values)


def answer_kernel(cases, me, ext, row_at, row_ok, same_col, h, y3, cross, chip, y4):
    before, after = sides(me, cross, chip)
    rows, width = ext.shape
    none = jnp.zeros((rows, width), F32)
    no_row = jnp.zeros((1, width), F32)
    above = [before[row_of(cases + j)] for j in range(3)] + [no_row, no_row]
    below = [no_row, no_row] + [after[row_of(cases + j)] for j in range(3)]
    y = coarse_step(
        [none] + [y3[j] for j in range(3)] + [none],
        above, below, ext, [none] * 5, h, (row_at, row_ok, same_col),
    )
    for j in range(5):
        y4[j] = y[j]


REACH_E = 3
ORDER = [0, -1, 1, -2, 2, -3, 3]
LANE_OWN, LANE_TOP, LANE_BOTTOM, LANE_EXT, LANE_D = 0, 8, 16, 24, 25
LANE_PERP, LANE_LOAD, LANE_C, LANE_L = 32, 40, 48, 104
FACTORS = [(j, k) for j in range(7) for k in range(j + 1, 7)]


def dot(x, y):
    return total(x * y)


def response_kernel(me, ext, cross, chip, y4, cross_y, chip_y, phi, q, scaled, part):
    before, after = sides(me, cross, chip)
    ab, be = sides(me, cross_y, chip_y)
    rows, width = ext.shape
    m = 2 * REACH_E + 1
    diag = 4.0 + ext[...]
    none = jnp.zeros((rows, width), F32)
    fields = [none] + [y4[j] for j in range(5)] + [none]
    two_rows = jnp.zeros((2, width), F32)
    halo = []
    for k in range(3):
        up = [ab[response_row(k, j)] for j in range(5)]
        down = [be[response_row(k, j)] for j in range(5)]
        halo.append(jnp.concatenate(up + [two_rows, two_rows] + down, axis=0))

    d_halo = [4.0 + spread(before, after, k, m) for k in range(2)]
    x, res = two_sweeps(fields, halo, None, None, diag, d_halo, spread(before, after, 2, m))
    for j in range(m):
        phi[j] = x[j]
    every = res[0]
    for j in range(1, m):
        every = every + res[j]
    basis = [every] + [res[REACH_E + j] for j in ORDER[1:]]
    values = []
    for j in range(m):
        v = basis[j]
        q[j] = v
        d = dot(v, v)
        inv = jnp.where(d > 0.0, 1.0 / jnp.where(d > 0.0, d, 1.0), 0.0)
        scaled[j] = inv * v
        values.append((LANE_D + j, d))
        for k in range(j + 1, m):
            factor = dot(v, basis[k]) * inv
            values.append((LANE_L + FACTORS.index((j, k)), factor))
            basis[k] = basis[k] - factor * v
    part[...] = lane_row(values)


def solve_slabs(g, groups, cells):
    own, top, bottom = (g[k : k + 8] for k in (LANE_OWN, LANE_TOP, LANE_BOTTOM))
    n = own.shape[1]
    lane = lax.broadcasted_iota(jnp.int32, own.shape, 1)
    b = own + jnp.where(lane == n - 1, 0.0, pltpu.roll(top, n - 1, 1))
    b = b + jnp.where(lane == 0, 0.0, pltpu.roll(bottom, 1, 1))
    b = b / (groups * float(n))
    mean = jnp.broadcast_to(g[LANE_EXT : LANE_EXT + 1], own.shape) / float(cells)
    d = 2.0 + mean / (float(n) * float(n))
    lower = jnp.where(lane == 0, 0.0, 1.0)
    upper = jnp.where(lane == n - 1, 0.0, 1.0)
    excess = (d - lower) - upper
    s = 1
    while s < n:
        inv = 1.0 / (lower + upper + excess)
        alpha = lower * pltpu.roll(inv, s, 1)
        gamma = upper * pltpu.roll(inv, n - s, 1)
        b = b + alpha * pltpu.roll(b, s, 1) + gamma * pltpu.roll(b, n - s, 1)
        excess = excess + alpha * pltpu.roll(excess, s, 1) + gamma * pltpu.roll(excess, n - s, 1)
        lower = alpha * pltpu.roll(lower, s, 1)
        upper = gamma * pltpu.roll(upper, n - s, 1)
        s *= 2
    return b / (lower + upper + excess)


def coarse_kernel_b(me, x1, ext, b, row_at, row_ok, same_col, h, y4, cross, chip, x3, to_cross, to_chip):
    before, after = sides(me, cross, chip)
    put = sender(me, to_cross, to_chip)
    cases, rows, width = x1.shape
    x = coarse_step(
        [x1[c] for c in range(cases)],
        [before[row_of(c)] for c in range(cases)],
        [after[row_of(c)] for c in range(cases)],
        ext, b, h, (row_at, row_ok, same_col),
    )
    for c in range(cases):
        x3[c] = x[c]
        put(flat_row(c), x[c][0:1], x[c][rows - 1 : rows])
    no_row = jnp.zeros((1, width), F32)
    put(flat_row(19), no_row, no_row)
    for j in range(5):
        y = y4[j]
        for k in range(3):
            put(response_row(k, j), y[k : k + 1], y[rows - 1 - k : rows - k])


def coarse_kernel_c(me, x3, ext, b, row_at, row_ok, same_col, h, smooth, cross, chip, part, v, to_cross, to_chip):
    before, after = sides(me, cross, chip)
    put = sender(me, to_cross, to_chip)
    cases, rows, width = x3.shape
    x = coarse_step(
        [x3[c] for c in range(cases)],
        [before[flat_row(c)] for c in range(cases)],
        [after[flat_row(c)] for c in range(cases)],
        ext, b, h, (row_at, row_ok, same_col),
    )
    for c in range(cases):
        y = smooth[c] + x[c]
        v[c] = y
        for k in range(3):
            put((k,) + row_of(c), y[k : k + 1], y[rows - 1 - k : rows - k])


def post_kernel(me, v, f, ext, cross, chip, cross_v, chip_v, q, scaled, part_a, part_e, out, gather):
    before, after = sides(me, cross, chip)
    before_v, after_v = sides(me, cross_v, chip_v)
    cases, rows, width = v.shape
    m = q.shape[0]
    diag = 4.0 + ext[...]
    fl = [f[c] for c in range(cases)]
    v_halo = [both(before_v, after_v, k) for k in range(3)]
    f_halo = [both(before, after, 3 + k) for k in range(2)]
    d_halo = [4.0 + spread(before, after, k, cases) for k in range(2)]
    valid = spread(before, after, 2, cases)
    x, res = two_sweeps([v[c] for c in range(cases)], v_halo, fl, f_halo, diag, d_halo, valid)
    for c in range(cases):
        out[c] = x[c]
    values = []
    for c in range(cases):
        r = res[c]
        share = [dot(r, scaled[j]) for j in range(m)]
        for j in range(m):
            r = r - share[j] * q[j]
        values.append((LANE_PERP + c, dot(r, r)))
        for j in range(m):
            values.append((LANE_C + 8 * j + c, share[j]))
    row = part_a[...] + part_e[...] + lane_row(values)
    gather[...] = jnp.broadcast_to(row, gather.shape)


def ratio_kernel(groups, cases, cells, me, gathered, ratio, near):
    n = gathered.shape[0]
    m = 2 * REACH_E + 1
    g = jnp.transpose(gathered[...])
    e = solve_slabs(g, groups, cells)
    lane = lax.broadcasted_iota(jnp.int32, e.shape, 1)
    for j in range(m):
        at = lane == me[0] + j - REACH_E
        own = jnp.sum(jnp.where(at, e, 0.0), axis=1, keepdims=True)
        near[j] = jnp.broadcast_to(own, near.shape[1:])

    def shifted(j):
        inside = (lane + j >= 0) & (lane + j < n)
        return jnp.where(inside, pltpu.roll(e, (-j) % n, 1), 0.0)

    def spread_row(k):
        return jnp.broadcast_to(g[k : k + 1], e.shape)

    t = [e] + [shifted(j) - e for j in ORDER[1:]]
    norm = g[LANE_PERP : LANE_PERP + 8]
    for j in range(m):
        z = g[LANE_C + 8 * j : LANE_C + 8 * j + 8] + t[j]
        for k in range(j + 1, m):
            z = z + spread_row(LANE_L + FACTORS.index((j, k))) * t[k]
        norm = norm + spread_row(LANE_D + j) * (z * z)
    norm = jnp.sum(norm, axis=1, keepdims=True)
    load = jnp.sum(g[LANE_LOAD : LANE_LOAD + 8], axis=1, keepdims=True)
    case = lax.broadcasted_iota(jnp.int32, norm.shape, 0)
    r = jnp.sqrt(jnp.where(case < cases, norm, 0.0) / jnp.where(case < cases, load, 1.0))
    ratio[...] = jnp.broadcast_to(lane_row([(c, r[c : c + 1]) for c in range(cases)]), ratio.shape)


def final_kernel(me, base, phi, near, out):
    cases, rows, width = base.shape
    for c in range(cases):
        x = base[c]
        for j in range(phi.shape[0]):
            x = x + near[j, pl.ds(c, 1), 0:1] * phi[j]
        out[c] = x


def local(thermal_solution, heat_forcing, extinction_factor, cluster_label):
    cases, rows, width = thermal_solution.shape
    n = lax.axis_size("blk")
    n_rhs = lax.axis_size("rhs")
    groups = rows * width // 16
    field = (cases, rows, width)
    pairs = [(i, i + 1) for i in range(1, n - 1, 2)]
    cross_chip = pairs + [(j, i) for i, j in pairs]
    on_chip = [(i, i ^ 1) for i in range(n)]

    def exchange(cross, chip):
        cross = lax.ppermute(cross, "blk", cross_chip)
        return cross, lax.ppermute(chip, "blk", on_chip)

    edge = (cases, width)
    edges = (8, width)
    deep = (5, 4, width)
    cells = (rows, width)
    u, f, ext, lab = thermal_solution, heat_forcing, extinction_factor, cluster_label
    sent = vmem_call(
        pack_kernel,
        [(6, cases, width)] * 2,
        [
            pltpu.VMEM(field, F32),
            pltpu.VMEM(field, F32),
            pltpu.VMEM(cells, F32),
            pltpu.SemaphoreType.DMA((3,)),
        ],
        n_in=3,
        in_space=pl.ANY,
    )(u, f, ext)
    halo = exchange(*sent)
    shifts = len(offsets())
    *tables, y3 = vmem_call(
        functools.partial(table_kernel, n),
        [
            ((shifts, rows, width), jnp.int32),
            (shifts, rows, width),
            (rows - 1, rows, width),
            cells,
            (3, rows, width),
        ],
        n_in=2,
    )(ext, lab)
    call = vmem_call
    smooth, b, x0, *sent, rsum = call(
        pre_kernel, [field, field, field, edges, edges, (1, 128)], n_in=10
    )(u, f, ext, *halo, *tables, y3)
    rows_x = exchange(*sent)
    x1, *sent = call(coarse_kernel_a, [field, edge, edge], n_in=9)(
        x0, ext, b, *tables, *rows_x
    )
    (part_a,) = call(sum_kernel, [(1, 128)], n_in=4)(x1, ext, f, rsum)
    (y4,) = call(functools.partial(answer_kernel, cases), [(5, rows, width)], n_in=8)(
        ext, *tables, y3, *rows_x
    )
    rows_x = exchange(*sent)
    x3, *sent = call(coarse_kernel_b, [field, deep, deep], n_in=10)(
        x1, ext, b, *tables, y4, *rows_x
    )
    rows_x = exchange(*sent)
    m = 2 * REACH_E + 1
    phi, q, scaled, part_e = call(
        response_kernel, [(m, rows, width)] * 3 + [(1, 128)], n_in=6
    )(ext, *halo, y4, *rows_x)
    v, *sent = call(
        coarse_kernel_c, [field, (3, cases, width), (3, cases, width)], n_in=11
    )(x3, ext, b, *tables, smooth, *rows_x, part_a)
    rows_x = exchange(*sent)
    base, mine = call(post_kernel, [field, (n, 128)], n_in=11)(
        v, f, ext, *halo, *rows_x, q, scaled, part_a, part_e
    )
    gathered = lax.all_to_all(mine, "blk", 0, 0, tiled=True)
    ratio, near = call(
        functools.partial(ratio_kernel, groups, cases, rows * width),
        [(n_rhs, 128), (m, 8, 128)],
        n_in=1,
    )(gathered)
    every = lax.all_to_all(ratio, "rhs", 0, 0, tiled=True)
    (corrected,) = call(final_kernel, [field], n_in=3)(base, phi, near)
    return corrected, every[:, :cases].reshape(n_rhs * cases)


def solution(mesh):
    in_specs = (P("rhs", "blk", None), P("rhs", "blk", None), P("blk", None), P("blk", None))
    out_specs = (P("rhs", "blk", None), P())
    return jax.shard_map(local, mesh=mesh, in_specs=in_specs, out_specs=out_specs, check_vma=False)
```
